32 devices in a mesh: wide: 8 (over y, x, core), narrow: 4 (over z).
Axes of the slice: x: 2, y: 2, z: 4, core: 2. Of those that a mesh axis runs over, the one named last changes fastest.
Arguments:
- tokens: bfloat16 [4096, 1024], P(('wide', 'narrow')), may hold values from -6 to 6
- log_decay: float32 [8, 4096], P(None, 'wide'), as said below
- lengths: int32 [1], replicated, may hold values from 1024 to 4096, as said below
- pad_counts: int32 [1], replicated, may hold values from 0 to 255
- w_query: bfloat16 [1024, 1024], replicated, may hold values from -0.1875 to 0.1875
- w_key: bfloat16 [1024, 1024], replicated, may hold values from -0.1875 to 0.1875
- w_value: bfloat16 [1024, 1024], replicated, may hold values from -0.1875 to 0.1875
- w_gate: bfloat16 [1024, 1024], replicated, may hold values from -0.1875 to 0.1875
- w_out: bfloat16 [1024, 1024], replicated, may hold values from -0.375 to 0.375
- w_first: bfloat16 [1024, 2816], P(None, 'narrow'), may hold values from -0.1875 to 0.1875
- w_second: bfloat16 [1024, 2816], P(None, 'narrow'), may hold values from -0.1875 to 0.1875
- w_third: bfloat16 [2816, 1024], P('narrow'), may hold values from -0.109375 to 0.109375
- cotangent: bfloat16 [4096, 1024], P(('wide', 'narrow')), may hold values from -6 to 6
Outputs:
- output: bfloat16 [4096, 1024], P(('wide', 'narrow'))
- grad_tokens: float32 [4096, 1024], P(('wide', 'narrow'))
- grad_w_query: float32 [1024, 1024], replicated
- grad_w_key: float32 [1024, 1024], replicated
- grad_w_value: float32 [1024, 1024], replicated
- grad_w_gate: float32 [1024, 1024], replicated
- grad_w_out: float32 [1024, 1024], replicated
- grad_w_first: float32 [1024, 2816], P(None, 'narrow')
- grad_w_second: float32 [1024, 2816], P(None, 'narrow')
- grad_w_third: float32 [2816, 1024], P('narrow')
The draws below stay inside these ranges and needn't reach their ends.
Inputs may be any that keep to these rules, and one draw needn't show every extreme that they name: `lengths`: multiples of 256 that sum to 4096; the longest is exactly 4096. `log_decay`: strictly negative.
All inputs are finite; a program needn't handle non-finite values.
Results may differ from the reference program's by a relative error of at most 0.017.
Values may be sent and summed in bfloat16 or wider, within the bound.
No kernel may reach another device: no remote copies, remote signals or barrier semaphores. Data moves between devices by JAX's collectives and lax.ppermute only.
A program may use at most 192 MiB of HBM per device.

```python
import math
import jax
import jax.numpy as jnp
from jax import lax

D = 1024
HEADS = 8
HEAD_DIM = 128
FF = 2816
BLOCK = 256
MIN_LEN = 1024
TOK_DEV = 512
STREAM_ITEMS = 4096
SEQS = 1
FILLED_SPAN = 4096


def draw_lengths(key, part):
    seq_count = SEQS
    min_blocks = MIN_LEN // BLOCK
    max_blocks = FILLED_SPAN // BLOCK
    spare_blocks = STREAM_ITEMS // BLOCK - max_blocks - min_blocks * (seq_count - 1)
    others = jnp.full((seq_count - 1,), min_blocks, jnp.int32)
    if spare_blocks > 0:
        block_room = max_blocks - min_blocks
        labels = jnp.repeat(jnp.arange(seq_count - 1, dtype=jnp.int32), block_room)
        chosen = jax.random.permutation(jax.random.fold_in(key, 1), labels)[:spare_blocks]
        targets = jnp.arange(seq_count - 1, dtype=jnp.int32)
        others = others + jnp.sum((chosen[:, None] == targets[None, :]).astype(jnp.int32), axis=0, dtype=jnp.int32)
    longest_at = jax.random.randint(jax.random.fold_in(key, 2), (), 0, seq_count)
    slot_ids = jnp.arange(seq_count, dtype=jnp.int32)
    padded_others = jnp.concatenate([others, jnp.zeros((1,), jnp.int32)])
    source = slot_ids - (slot_ids > longest_at).astype(jnp.int32)
    blocks = jnp.where(slot_ids == longest_at, max_blocks, padded_others[source])
    return (blocks * BLOCK).astype(jnp.int32)


def draw_log_decay(key, part):
    derived_prng_keys = jax.random.split(key, 7)
    fast_share = 0.5
    fast_head = jax.random.uniform(derived_prng_keys[0], (HEADS, 1)) < fast_share
    fast_rate = jax.random.uniform(derived_prng_keys[1], (HEADS, 1), minval=4.0, maxval=8.0) / BLOCK
    slow_rate = jax.random.uniform(derived_prng_keys[2], (HEADS, 1), minval=0.1, maxval=0.4) * math.log(10.0) / FILLED_SPAN
    default_mean_span = jnp.where(fast_head, fast_rate, slow_rate)
    item_window = jnp.exp(jax.random.uniform(derived_prng_keys[3], (HEADS, STREAM_ITEMS // TOK_DEV), minval=-0.7, maxval=0.7))
    item_window = jnp.repeat(item_window, TOK_DEV, axis=1)
    jitter_noise = jax.random.uniform(derived_prng_keys[4], (HEADS, STREAM_ITEMS), minval=0.5, maxval=1.5)
    spike_pick_mask = jax.random.uniform(derived_prng_keys[5], (STREAM_ITEMS,))
    spike_span = jax.random.uniform(derived_prng_keys[6], (STREAM_ITEMS,), minval=0.2, maxval=0.5)
    span_spike_draw = jnp.where(spike_pick_mask < 2.0 / FILLED_SPAN, -jnp.log(1.0 - spike_span), 0.0)
    return (-(default_mean_span * item_window * jitter_noise) - span_spike_draw[None, :]).astype(jnp.float32)


def steps_of(rng, extent, shards, smallest, largest):
    def one(dim, shards_of):
        heights = jax.random.uniform(jax.random.fold_in(jax.random.fold_in(rng, 6), dim), (shards_of,), jnp.float32, smallest / len(shards), largest / len(shards))
        return jnp.repeat(jnp.exp(heights), extent[dim] // shards_of).reshape((-1,) + (1,) * (len(extent) - dim - 1))

    gain = one(*shards[0])
    for cut in shards[1:]:
        gain = gain * one(*cut)
    return gain


def noise(own_key, extent, scale, reach, cuts=(), held_as=jnp.bfloat16):
    values = scale * jax.random.normal(own_key, extent, jnp.float32)
    if cuts:
        values = values * steps_of(own_key, extent, cuts, -0.22, 0.18)
    return jnp.clip(values, -reach, reach).astype(held_as)


def setup_inputs(seed: int = 0) -> dict:
    splits = jax.random.split(jax.random.key(seed), 14)
    return {
        "tokens": noise(splits[0], (STREAM_ITEMS, D), 1.0, 6.0, ((0, 32),)),
        "log_decay": draw_log_decay(jax.random.fold_in(splits[13], 71), 0),
        "lengths": draw_lengths(jax.random.fold_in(splits[13], 71), 0),
        "pad_counts": jax.random.randint(splits[3], (SEQS,), 0, BLOCK).astype(jnp.int32),
        "w_query": noise(splits[4], (D, D), D ** -0.5, 0.1875),
        "w_key": noise(splits[5], (D, D), D ** -0.5, 0.1875),
        "w_value": noise(splits[6], (D, D), D ** -0.5, 0.1875),
        "w_gate": noise(splits[7], (D, D), D ** -0.5, 0.1875),
        "w_out": noise(splits[8], (D, D), (D // 4) ** -0.5, 0.375),
        "w_first": noise(splits[9], (D, FF), D ** -0.5, 0.1875, ((1, 4),)),
        "w_second": noise(splits[10], (D, FF), D ** -0.5, 0.1875, ((1, 4),)),
        "w_third": noise(splits[11], (FF, D), FF ** -0.5, 0.109375, ((0, 4),)),
        "cotangent": noise(splits[12], (STREAM_ITEMS, D), 1.0, 6.0, ((0, 32),)),
    }


epsilon = 1e-06
precise = lax.Precision.HIGHEST

@jax.custom_vjp
def low(v):
    return lax.optimization_barrier(v.astype(jnp.bfloat16)).astype(jnp.float32)

@jax.custom_vjp
def low_back(v):
    return v

def low_keep(v):
    return (low(v), None)

def low_pass(kept, grad):
    return (grad,)

def back_keep(v):
    return (v, None)

def back_low(kept, grad):
    return (low(grad),)
low.defvjp(low_keep, low_pass)
low_back.defvjp(back_keep, back_low)

def rms_norm(values):
    return values * lax.rsqrt(lax.optimization_barrier(jnp.mean(values * values, axis=-1, keepdims=True)) + epsilon)

def matmul(left_hand, right_hand):
    return jnp.dot(left_hand, right_hand, precision=precise, preferred_element_type=jnp.float32)

def token_layout(lengths, pad_counts, anchor, total_rows):
    ends = jnp.cumsum(lengths, dtype=jnp.int32)
    starts = ends - lengths
    position = anchor + jnp.arange(total_rows, dtype=jnp.int32)
    inside = (position[:, None] >= starts[None, :]) & (position[:, None] < ends[None, :])
    limit = lax.optimization_barrier(jnp.sum(jnp.where(inside, (ends - pad_counts)[None, :], 0), axis=1, dtype=jnp.int32))
    live = (position < limit).astype(jnp.float32)
    opening = jnp.any(position[:, None] == starts[None, :], axis=1).astype(jnp.float32)
    return (live, opening)

def to_blocks(values, head_count):
    row_count, model_width = values.shape
    shaped = values.reshape(row_count // BLOCK, BLOCK, head_count, model_width // head_count)
    return shaped.transpose(0, 2, 1, 3)

def block_step(state, inputs):
    query_blk, key_blk, value_blk, decay_blk, keep_now = inputs
    cumulative = jnp.cumsum(decay_blk, axis=1)
    positions = jnp.arange(BLOCK, dtype=jnp.int32)
    causal = positions[:, None] >= positions[None, :]
    spread = cumulative[:, :, None] - cumulative[:, None, :]
    weights = jnp.where(causal, jnp.exp(jnp.where(causal, spread, 0.0)), 0.0)
    raw_scores = low_back(jnp.einsum('htd,hsd->hts', query_blk, key_blk, precision=precise))
    scores = low(raw_scores * weights)
    intra = jnp.einsum('hts,hsd->htd', scores, value_blk, precision=precise)
    entering = state * keep_now
    inter = jnp.einsum('htd,hde->hte', query_blk * jnp.exp(cumulative)[:, :, None], entering, precision=precise)
    tail = jnp.exp(cumulative[:, -1:] - cumulative)
    update = jnp.einsum('hsd,hse->hde', key_blk * tail[:, :, None], value_blk, precision=precise)
    new_state = jnp.exp(cumulative[:, -1])[:, None, None] * entering + update
    return (new_state, intra + inter)

def forward(tokens, w_query, w_key, w_value, w_gate, w_out, w_first, w_second, w_third, log_decay, live, keep_blocks):
    total_rows = tokens.shape[0]
    normed_one = low(rms_norm(tokens))
    query_act = low(jax.nn.silu(low_back(matmul(normed_one, w_query))))
    key_act = low(jax.nn.silu(low_back(matmul(normed_one, w_key))) * live[:, None])
    value_act = low(low_back(matmul(normed_one, w_value)))
    gate_act = jax.nn.sigmoid(low_back(matmul(normed_one, w_gate)))
    block_count = total_rows // BLOCK
    decay_blocks = log_decay.reshape(HEADS, block_count, BLOCK).transpose(1, 0, 2)
    start_state = jnp.zeros((HEADS, HEAD_DIM, HEAD_DIM), jnp.float32)
    final_state, mixed_out = lax.scan(jax.checkpoint(block_step), start_state, (to_blocks(query_act, HEADS), to_blocks(key_act, HEADS), to_blocks(value_act, HEADS), decay_blocks, keep_blocks))
    attended = low_back(mixed_out.transpose(0, 2, 1, 3).reshape(total_rows, D))
    gated = low(rms_norm(attended) * gate_act)
    hidden = tokens + low_back(matmul(gated, w_out))
    normed_two = low(rms_norm(hidden))
    product = low(low_back(matmul(normed_two, w_first)) * low_back(matmul(normed_two, w_second)))
    return hidden + matmul(product, w_third)

def reference(tokens, log_decay, lengths, pad_counts, w_query, w_key, w_value, w_gate, w_out, w_first, w_second, w_third, cotangent):
    total_rows = tokens.shape[0]
    live, opening = token_layout(lengths, pad_counts, 0, total_rows)
    keep_blocks = 1.0 - opening.reshape(total_rows // BLOCK, BLOCK)[:, 0]

    def wrapped(tokens_in, query_in, key_in, value_in, gate_in, out_in, first_in, second_in, third_in):
        return forward(tokens_in, query_in, key_in, value_in, gate_in, out_in, first_in, second_in, third_in, log_decay, live, keep_blocks)
    result, pullback = jax.vjp(wrapped, tokens.astype(jnp.float32), w_query.astype(jnp.float32), w_key.astype(jnp.float32), w_value.astype(jnp.float32), w_gate.astype(jnp.float32), w_out.astype(jnp.float32), w_first.astype(jnp.float32), w_second.astype(jnp.float32), w_third.astype(jnp.float32))
    grads = pullback(cotangent.astype(jnp.float32))
    return (result.astype(jnp.bfloat16), grads[0], grads[1], grads[2], grads[3], grads[4], grads[5], grads[6], grads[7], grads[8])
```

```python
import functools

import jax
import jax.numpy as jnp
from jax import lax
from jax.experimental import pallas as pl
from jax.experimental.pallas import tpu as pltpu
from jax.sharding import PartitionSpec as P

BLOCK = 256
epsilon = 1e-06
bf16 = jnp.bfloat16
f32 = jnp.float32
SMEM = pl.BlockSpec(memory_space=pltpu.SMEM)
PARAMS = pltpu.CompilerParams(dimension_semantics=("arbitrary",), vmem_limit_bytes=56 << 20)


def mm(a, b):
    return lax.dot_general(a, b, (((1,), (0,)), ((), ())), preferred_element_type=f32)


def mt(a, b):
    return lax.dot_general(a, b, (((1,), (1,)), ((), ())), preferred_element_type=f32)


def tm(a, b):
    return lax.dot_general(a, b, (((0,), (0,)), ((), ())), preferred_element_type=f32)


def inv_rms(values):
    return lax.rsqrt(jnp.mean(values * values, axis=-1, keepdims=True) + epsilon)


def sigmoid(values):
    return 1.0 / (1.0 + jnp.exp(-values))


def slope(values):
    squashed = sigmoid(values)
    return squashed * (1.0 + values * (1.0 - squashed))


def rms_back(values, inverse, gradient):
    normed = values * inverse
    return inverse * (gradient - normed * jnp.mean(gradient * normed, axis=-1, keepdims=True))


def token_layout(lengths, pad_counts, anchor, total_rows):
    ends = jnp.cumsum(lengths, dtype=jnp.int32)
    starts = ends - lengths
    position = anchor + jnp.arange(total_rows, dtype=jnp.int32)
    inside = (position[:, None] >= starts[None, :]) & (position[:, None] < ends[None, :])
    limit = jnp.sum(jnp.where(inside, (ends - pad_counts)[None, :], 0), axis=1, dtype=jnp.int32)
    live = (position < limit).astype(f32)
    opening = jnp.any(position[:, None] == starts[None, :], axis=1).astype(f32)
    return (live, opening)


def whole(shape):
    zeros = (0,) * len(shape)
    return pl.BlockSpec(shape, lambda *_: zeros)


def rows(shape, index):
    rest = (0,) * (len(shape) - 1)
    return pl.BlockSpec(shape, lambda b: (index(b), *rest))


def decay_weights(g_col, g_row):
    size = g_col.shape[0]
    causal = lax.broadcasted_iota(jnp.int32, (size, size), 0) >= lax.broadcasted_iota(
        jnp.int32, (size, size), 1
    )
    return jnp.where(causal, jnp.exp(jnp.where(causal, g_col - g_row, 0.0)), 0.0)


def forward_kernel(hn, hd, decay, tok, wq, wk, wv, live, gcol, grow, tail,
                   n1, ql, kl, q, k, v, intra, contrib, final, state):
    b = pl.program_id(0)
    values = tok[...].astype(f32)
    normed = (values * inv_rms(values)).astype(bf16)
    n1[...] = normed
    q_lin = mm(normed, wq[...])
    k_lin = mm(normed, wk[...])
    ql[...] = q_lin
    kl[...] = k_lin
    q[...] = (q_lin * sigmoid(q_lin)).astype(bf16)
    k[...] = (k_lin * sigmoid(k_lin) * live[...]).astype(bf16)
    v[...] = mm(normed, wv[...]).astype(bf16)
    for h in range(hn):
        at = slice(h * hd, (h + 1) * hd)
        qh, kh, vh = q[:, at], k[:, at], v[:, at]
        weights = decay_weights(gcol[:, h : h + 1], grow[0, h : h + 1, :])
        scores = (mt(qh, kh) * weights).astype(bf16)
        intra[:, at] = mm(scores, vh)
        key_tail = (kh.astype(f32) * tail[:, h : h + 1]).astype(bf16)
        now = tm(key_tail, vh)
        contrib[0, h] = now
        before = jnp.where(b == 0, 0.0, state[h])
        state[h] = decay[b, h] * before + now
        final[h] = state[h].astype(bf16)


def attend_kernel(hn, hd, wide, decay, keep, coef, gathered, contrib, q, intra, rise,
                  att, kent, state):
    b = pl.program_id(0)
    for h in range(hn):
        @pl.when(b == 0)
        def _():
            total = coef[0, h] * gathered[0, h].astype(f32)
            for j in range(1, wide):
                total = total + coef[j, h] * gathered[j, h].astype(f32)
            state[h] = total
        at = slice(h * hd, (h + 1) * hd)
        entering = state[h]
        kept = (keep[b] * entering).astype(bf16)
        kent[0, h] = kept
        att[:, at] = (intra[:, at] + rise[:, h : h + 1] * mm(q[:, at], kept)).astype(bf16)
        state[h] = decay[b, h] * entering + contrib[0, h]


def join(parts):
    return jnp.concatenate([parts[i] for i in range(parts.shape[0])], axis=1)


def hidden_kernel(att, gate, tok, wo, hidden, n2):
    values = join(att).astype(f32)
    gated = (values * inv_rms(values) * gate[...]).astype(bf16)
    hid = tok[...].astype(f32) + mm(gated, wo[...])
    hidden[...] = hid
    n2[...] = (hid * inv_rms(hid)).astype(bf16)


def ffn_kernel(n2, cot, w1, w2, w3, product, gf, gs, gn2):
    normed = n2[...]
    first = mm(normed, w1[...])
    second = mm(normed, w2[...])
    product[...] = (first * second).astype(bf16)
    grad = mt(cot[...], w3[...])
    gf[...] = (grad * second).astype(bf16)
    gs[...] = (grad * first).astype(bf16)
    gn2[...] = (mt(gf[...], w1[...]) + mt(gs[...], w2[...])).astype(bf16)


def residual_kernel(parts, gn2, hidden, cot, wo, att, gate, grad_hidden, packed, ga, ggl):
    hid = hidden[...]
    gh = cot[...].astype(f32) + rms_back(hid, inv_rms(hid), gn2[...].astype(f32))
    grad_hidden[...] = gh
    low = gh.astype(bf16)
    width = low.shape[1]
    gg = mt(low, wo[...])
    values = join(att).astype(f32)
    inverse = inv_rms(values)
    act = gate[...]
    ggl[...] = (gg * (values * inverse) * act * (1.0 - act)).astype(bf16)
    back = rms_back(values, inverse, gg * act).astype(bf16)
    size = width // parts
    for i in range(parts):
        ga[i] = back[:, i * size : (i + 1) * size]
    packed[:, :width] = low
    high = inverse.astype(bf16)
    rest = inverse - high.astype(f32)
    middle = rest.astype(bf16)
    tailing = (rest - middle.astype(f32)).astype(bf16)
    lane = lax.broadcasted_iota(jnp.int32, (low.shape[0], 128), 1)
    spread = jnp.where(
        lane == 0, high.astype(f32), jnp.where(lane == 1, middle.astype(f32), tailing.astype(f32))
    )
    packed[:, width:] = spread.astype(bf16)


def query_kernel(hn, hd, blocks, decay, keep, ga, q, k, v, ql, kent, gcol, grow, rise,
                 dq, gk, gv, direct, first, state):
    i = pl.program_id(0)
    b = blocks - 1 - i
    for h in range(hn):
        at = slice(h * hd, (h + 1) * hd)
        g, qh, kh, vh = ga[:, at], q[:, at], k[:, at], v[:, at]
        weights = decay_weights(gcol[:, h : h + 1], grow[0, h : h + 1, :])
        scores = (mt(qh, kh) * weights).astype(bf16)
        raw = (mt(g, vh) * weights).astype(bf16)
        up = rise[:, h : h + 1]
        gq = mm(raw, kh) + up * mt(g, kent[0, h])
        dq[:, at] = (gq * slope(ql[:, at])).astype(bf16)
        gk[:, at] = tm(raw, qh)
        gv[:, at] = tm(scores, g)
        now = keep[b] * tm((qh.astype(f32) * up).astype(bf16), g)
        direct[0, h] = now
        after = jnp.where(i == 0, 0.0, state[h])
        state[h] = now + decay[b, h] * after
        first[h] = state[h].astype(bf16)


def spread(wide, own, source, keep, send, item):
    tall = source.shape[0] // wide
    for j in range(wide):
        at = pl.ds(pl.multiple_of((own ^ j) * tall, tall), tall)
        out = keep if j % 2 == 0 else send
        out[j // 2, item] = source[at, :].astype(bf16)


def key_kernel(hn, hd, wide, blocks, own, decay, coef, gathered, direct, n1, dq, k, v, kl, gk, gv,
               tail, live, wq, wk, wv, kept, sent, gn1, state, dk, dv, aq, ak, av):
    i = pl.program_id(0)
    b = blocks - 1 - i
    for h in range(hn):
        @pl.when(i == 0)
        def _():
            total = coef[0, h] * gathered[0, h].astype(f32)
            for j in range(1, wide):
                total = total + coef[j, h] * gathered[j, h].astype(f32)
            state[h] = total
        at = slice(h * hd, (h + 1) * hd)
        after = state[h]
        low = after.astype(bf16)
        down = tail[:, h : h + 1]
        grad_key = gk[:, at] + down * mt(v[:, at], low)
        dk[:, at] = (grad_key * live[...] * slope(kl[:, at])).astype(bf16)
        dv[:, at] = (gv[:, at] + down * mm(k[:, at], low)).astype(bf16)
        state[h] = direct[0, h] + decay[b, h] * after
    normed = n1[...]
    for item, (acc, part) in enumerate(((aq, dq), (ak, dk), (av, dv))):
        now = tm(normed, part[...])

        @pl.when(i == 0)
        def _():
            acc[...] = now

        @pl.when(i > 0)
        def _():
            acc[...] += now

        @pl.when(i == blocks - 1)
        def _():
            spread(wide, own[0], acc, kept, sent, item)

    gn1[...] = (mt(dq[...], wq[...]) + mt(dk[...], wk[...]) + mt(dv[...], wv[...])).astype(bf16)


def gate_kernel(wide, narrow, own, packed, att, n1, wg, wo, kept, sent, acc, acc_out):
    width = n1.shape[1]
    grads = packed[:, :width]
    extra = packed[:, width:].astype(f32)
    inverse = extra[:, 0:1] + extra[:, 1:2] + extra[:, 2:3]
    normed = n1[...]
    act = sigmoid(mm(normed, wg[...]))
    scaled = att[...].astype(f32) * inverse
    gated = (scaled * act).astype(bf16)
    gg = mt(grads, wo[...])
    ggl = (gg * scaled * act * (1.0 - act)).astype(bf16)
    acc[...] = tm(normed, ggl)
    spread(wide, own[0], acc, kept, sent, 0)
    acc_out[...] = tm(gated, grads)
    cols = gated.shape[1]
    short = cols // wide
    for j in range(wide):
        at = pl.ds(pl.multiple_of((own[0] ^ j) * short, short), short)
        out = kept if j % 2 == 0 else sent
        for i in range(narrow):
            out[j // 2, 1, i * short : (i + 1) * short, :] = acc_out[
                at, i * cols : (i + 1) * cols
            ].astype(bf16)


def ffn_grad_kernel(wide, own, n2, cot, product, gf, gs, kept, sent, acc):
    item = pl.program_id(0)
    for i, (left, right) in enumerate(((n2, gf), (n2, gs), (cot, product))):
        @pl.when(item == i)
        def _():
            acc[...] = tm(left[...], right[...])

    spread(wide, own[0], acc, kept, sent, 0)


def tokens_kernel(gn1, ggl, wg, tok, gh, out):
    grad = gn1[...].astype(f32) + mt(ggl[...], wg[...])
    values = tok[...].astype(f32)
    out[...] = gh[...] + rms_back(values, inv_rms(values), grad)


def exchange(values, bit):
    size = lax.axis_size("wide")
    return lax.ppermute(values, "wide", [(i, i ^ (1 << bit)) for i in range(size)])


def reduce_over_wide(kept, sent):
    bits = (lax.axis_size("wide") - 1).bit_length()
    total = kept + exchange(sent, 0)
    rest = total.shape[1:]
    half = rest[-2] // 2

    def run(part, order):
        part = part.reshape((2,) * (bits - 1) + part.shape[1:])
        left = list(range(bits - 1, 0, -1))
        for bit in order:
            axis = left.index(bit)
            mine = lax.index_in_dim(part, 0, axis, keepdims=False)
            part = mine + exchange(lax.index_in_dim(part, 1, axis, keepdims=False), bit)
            left.remove(bit)
        return part

    up = list(range(1, bits))
    return (run(total[..., :half, :], up), run(total[..., half:, :], up[::-1]))


def gather_over_wide(lower, upper):
    bits = (lax.axis_size("wide") - 1).bit_length()

    def run(part, order):
        full = part[None]
        for bit in order:
            full = jnp.concatenate([full, exchange(full, bit)], axis=0)
        return full

    up = list(range(1, bits))
    low, high = run(lower, up[::-1]), run(upper, up)
    return (low, high, exchange(low, 0), exchange(high, 0))


def reversed_bits(value, count):
    out = 0
    for i in range(count):
        out = out | (((value >> i) & 1) << (count - 1 - i))
    return out


def slot_specs(wide, shape):
    bits = (wide - 1).bit_length() - 1
    zeros = (0,) * len(shape)
    last = wide // 2 - 1

    def spec(other, flip):
        def index(c, s, own):
            at = reversed_bits(s, bits) if flip else s
            stay = reversed_bits(last, bits) if not other else 0
            return (jnp.where(c == other, at, stay), *zeros)

        return pl.BlockSpec((1, *shape), index)

    return [spec(0, True), spec(0, False), spec(1, True), spec(1, False)]


def place(low, high, c, write):
    @pl.when(c == 0)
    def _():
        write(low[0], high[0])

    @pl.when(c == 1)
    def _():
        write(low[1], high[1])


def widen_square_kernel(count, narrow, own, low, high, low_other, high_other, *outs):
    def write(source_low, source_high):
        half = source_low.shape[-2]
        cols = source_low.shape[-1]
        for item in range(count):
            for n in range(narrow):
                at = slice(n * cols, (n + 1) * cols)
                outs[item][:half, at] = source_low[0, n, item].astype(f32)
                outs[item][half:, at] = source_high[0, n, item].astype(f32)

    place((low, low_other), (high, high_other), pl.program_id(0), write)


def widen_gate_kernel(narrow, own, low, high, low_other, high_other, gate, out):
    def write(source_low, source_high):
        half = source_low.shape[-2]
        cols = source_low.shape[-1]
        short = 2 * half // narrow
        for n in range(narrow):
            at = slice(n * cols, (n + 1) * cols)
            gate[:half, at] = source_low[0, n, 0].astype(f32)
            gate[half:, at] = source_high[0, n, 0].astype(f32)
            for i in range(narrow):
                source = source_low if i * short < half else source_high
                start = i * short % half
                out[n, :, i * cols : (i + 1) * cols] = source[
                    0, n, 1, start : start + short, :
                ].astype(f32)

    place((low, low_other), (high, high_other), pl.program_id(0), write)


def widen_ffn_kernel(own, low, high, low_other, high_other, *outs):
    def write(source_low, source_high):
        half = source_low.shape[-2]
        for item in range(3):
            outs[item][:half] = source_low[0, item].astype(f32)
            outs[item][half:] = source_high[0, item].astype(f32)

    place((low, low_other), (high, high_other), pl.program_id(0), write)


def ones_like_product(factors, own, first):
    count = factors.shape[0]
    j = jnp.arange(count)[:, None]
    i = jnp.arange(count)[None, :]
    if first:
        between = (i > j) & (i < own)
        wanted = j[:, 0] < own
    else:
        between = (i < j) & (i > own)
        wanted = j[:, 0] > own
    terms = jnp.where(between[:, :, None], factors[None], 1.0)
    return jnp.where(wanted[:, None], jnp.prod(terms, axis=1), 0.0)


def body(tokens, log_decay, lengths, pad_counts, w_query, w_key, w_value, w_gate, w_out,
         w_first, w_second, w_third, cotangent):
    wide, narrow = lax.axis_size("wide"), lax.axis_size("narrow")
    own_wide, own_narrow = lax.axis_index("wide"), lax.axis_index("narrow")
    heads, local = log_decay.shape
    share, width = tokens.shape
    hn, cols, hd = heads // narrow, width // narrow, width // heads
    blocks = local // BLOCK
    sds = jax.ShapeDtypeStruct

    tok = lax.all_gather(tokens, "narrow", axis=0, tiled=True)
    cot = lax.all_gather(cotangent, "narrow", axis=0, tiled=True)

    live, opening = token_layout(lengths, pad_counts, own_wide * local, local)
    live = live[:, None]
    keep = 1.0 - opening.reshape(blocks, BLOCK)[:, 0]
    own_decay = lax.dynamic_slice_in_dim(log_decay, own_narrow * hn, hn, 0)
    summed = jnp.cumsum(own_decay.reshape(hn, blocks, BLOCK), axis=2)
    last = summed[:, :, -1:]
    grow = summed.transpose(1, 0, 2)
    gcol = summed.reshape(hn, local).T
    rise = jnp.exp(summed).reshape(hn, local).T
    tail = jnp.exp(last - summed).reshape(hn, local).T
    decay = (jnp.exp(last[:, :, 0]) * keep[None]).T
    factors = lax.all_gather(jnp.prod(decay, axis=0), "wide", axis=0)
    coef_in = ones_like_product(factors, own_wide, True)
    coef_out = ones_like_product(factors, own_wide, False)

    def own_cols(weight):
        return lax.dynamic_slice_in_dim(weight, own_narrow * cols, cols, 1)

    wq, wk, wv, wg = (own_cols(w) for w in (w_query, w_key, w_value, w_gate))
    wo = lax.dynamic_slice_in_dim(w_out, own_narrow * cols, cols, 0)
    own_tok = tokens.astype(f32)
    own_n1 = (own_tok * inv_rms(own_tok)).astype(bf16)
    gate = jax.nn.sigmoid(jnp.dot(own_n1, w_gate, preferred_element_type=f32))

    up = lambda b: b
    down = lambda b: blocks - 1 - b

    def blk(w, index, size=BLOCK):
        return rows((size, w), index)

    def states(index):
        return rows((1, hn, hd, hd), index)

    state_spec = whole((hn, hd, hd))
    state_scratch = pltpu.VMEM((hn, hd, hd), f32)
    n1, ql, kl, q, k, v, intra, contrib, final = pl.pallas_call(
        functools.partial(forward_kernel, hn, hd),
        grid=(blocks,),
        in_specs=[SMEM, blk(width, up), *[whole((width, cols))] * 3, blk(1, up), blk(hn, up),
                  rows((1, hn, BLOCK), up), blk(hn, up)],
        out_specs=[blk(width, up), *[blk(cols, up)] * 6, states(up), state_spec],
        out_shape=[sds((local, width), bf16), *[sds((local, cols), f32)] * 2,
                   *[sds((local, cols), bf16)] * 3, sds((local, cols), f32),
                   sds((blocks, hn, hd, hd), f32), sds((hn, hd, hd), bf16)],
        scratch_shapes=[state_scratch],
        compiler_params=PARAMS,
        name="mixer_forward",
    )(decay, tok, wq, wk, wv, live, gcol, grow, tail)

    gathered = lax.all_gather(final, "wide", axis=0)
    att, kent = pl.pallas_call(
        functools.partial(attend_kernel, hn, hd, wide),
        grid=(blocks,),
        in_specs=[SMEM, SMEM, SMEM, whole((wide, hn, hd, hd)), states(up), blk(cols, up),
                  blk(cols, up), blk(hn, up)],
        out_specs=[blk(cols, up), states(up)],
        out_shape=[sds((local, cols), bf16), sds((blocks, hn, hd, hd), bf16)],
        scratch_shapes=[state_scratch],
        compiler_params=PARAMS,
        name="mixer_attend",
    )(decay, keep, coef_in, gathered, contrib, q, intra, rise)

    att_own = lax.all_to_all(att.reshape(narrow, share, cols), "narrow", 0, 0)
    hidden, n2 = pl.pallas_call(
        hidden_kernel,
        out_shape=[sds((share, width), f32), sds((share, width), bf16)],
        compiler_params=pltpu.CompilerParams(vmem_limit_bytes=56 << 20),
        name="mixer_out",
    )(att_own, gate, tokens, w_out)

    n2_all = lax.all_gather(n2, "narrow", axis=0, tiled=True)
    ff = w_first.shape[1]
    product, gf, gs, gn2_part = pl.pallas_call(
        ffn_kernel,
        grid=(blocks,),
        in_specs=[blk(width, up), blk(width, up), whole((width, ff)), whole((width, ff)),
                  whole((ff, width))],
        out_specs=[blk(ff, up)] * 3 + [blk(width, up)],
        out_shape=[sds((local, ff), bf16)] * 3 + [sds((local, width), bf16)],
        compiler_params=PARAMS,
        name="ffn",
    )(n2_all, cot, w_first, w_second, w_third)
    gn2 = lax.psum_scatter(gn2_part, "narrow", scatter_dimension=0, tiled=True)
    ffn_part = jnp.dot(product, w_third, preferred_element_type=f32).astype(bf16)
    ffn_own = lax.psum_scatter(ffn_part, "narrow", scatter_dimension=0, tiled=True)
    output = (hidden + ffn_own.astype(f32)).astype(bf16)
    tall = width // wide
    own_ref = own_wide.astype(jnp.int32)[None]
    kept, sent = pl.pallas_call(
        functools.partial(ffn_grad_kernel, wide),
        grid=(3,),
        in_specs=[SMEM, *[whole((local, width))] * 2, *[whole((local, ff))] * 3],
        out_specs=[pl.BlockSpec((wide // 2, 1, tall, ff), lambda i: (0, i, 0, 0))] * 2,
        out_shape=[sds((wide // 2, 3, tall, ff), bf16)] * 2,
        scratch_shapes=[pltpu.VMEM((width, ff), f32)],
        compiler_params=PARAMS,
        name="ffn_grads",
    )(own_ref, n2_all, cot, product, gf, gs)
    ff_pieces = gather_over_wide(*reduce_over_wide(kept, sent))
    widened = pltpu.CompilerParams(dimension_semantics=("arbitrary", "arbitrary"))

    def out_row(c, s, own):
        return own[0] ^ (2 * s + c)

    grad_first, grad_second, third_turned = pl.pallas_call(
        widen_ffn_kernel,
        grid_spec=pltpu.PrefetchScalarGridSpec(
            num_scalar_prefetch=1,
            grid=(2, wide // 2),
            in_specs=slot_specs(wide, (3, tall // 2, ff)),
            out_specs=[pl.BlockSpec((tall, ff), lambda c, s, own: (out_row(c, s, own), 0))] * 3,
        ),
        out_shape=[sds((width, ff), f32)] * 3,
        compiler_params=widened,
        name="widen_ffn",
    )(own_ref, *ff_pieces)
    grad_third = third_turned.T

    grad_hidden, packed, ga, ggl = pl.pallas_call(
        functools.partial(residual_kernel, narrow),
        out_shape=[sds((share, width), f32), sds((share, width + 128), bf16),
                   sds((narrow, share, cols), bf16), sds((share, width), bf16)],
        compiler_params=pltpu.CompilerParams(vmem_limit_bytes=56 << 20),
        name="residual_back",
    )(gn2, hidden, cotangent, w_out, att_own, gate)
    ga_cols = lax.all_to_all(ga, "narrow", 0, 0).reshape(local, cols)
    packed_all = lax.all_gather(packed, "narrow", axis=0, tiled=True)

    dq, gk, gv, direct, first = pl.pallas_call(
        functools.partial(query_kernel, hn, hd, blocks),
        grid=(blocks,),
        in_specs=[SMEM, SMEM, *[blk(cols, down)] * 5, states(down), blk(hn, down),
                  rows((1, hn, BLOCK), down), blk(hn, down)],
        out_specs=[*[blk(cols, down)] * 3, states(down), state_spec],
        out_shape=[sds((local, cols), bf16), *[sds((local, cols), f32)] * 2,
                   sds((blocks, hn, hd, hd), f32), sds((hn, hd, hd), bf16)],
        scratch_shapes=[state_scratch],
        compiler_params=PARAMS,
        name="mixer_query_back",
    )(decay, keep, ga_cols, q, k, v, ql, kent, gcol, grow, rise)

    arrived = lax.all_gather(first, "wide", axis=0)
    pair = (wide // 2, 3, tall, cols)
    kept, sent, gn1_part = pl.pallas_call(
        functools.partial(key_kernel, hn, hd, wide, blocks),
        grid=(blocks,),
        in_specs=[SMEM, SMEM, SMEM, whole((wide, hn, hd, hd)), states(down), blk(width, down),
                  *[blk(cols, down)] * 6, blk(hn, down), blk(1, down),
                  *[whole((width, cols))] * 3],
        out_specs=[*[whole(pair)] * 2, blk(width, down)],
        out_shape=[*[sds(pair, bf16)] * 2, sds((local, width), bf16)],
        scratch_shapes=[state_scratch, *[pltpu.VMEM((BLOCK, cols), bf16)] * 2,
                        *[pltpu.VMEM((width, cols), f32)] * 3],
        compiler_params=PARAMS,
        name="mixer_key_back",
    )(own_ref, decay, coef_out, arrived, direct, n1, dq, k, v, kl, gk, gv, tail, live, wq, wk, wv)

    def collect(kept, sent):
        lower, upper = reduce_over_wide(kept, sent)
        both = lax.all_gather(jnp.stack([lower, upper]), "narrow", axis=0)
        return gather_over_wide(both[:, 0], both[:, 1])

    square_pieces = collect(kept, sent)
    pair = (wide // 2, 2, tall, cols)
    kept, sent = pl.pallas_call(
        functools.partial(gate_kernel, wide, narrow),
        in_specs=[SMEM, *[pl.BlockSpec(memory_space=pltpu.VMEM)] * 5],
        out_shape=[sds(pair, bf16)] * 2,
        scratch_shapes=[pltpu.VMEM((width, cols), f32), pltpu.VMEM((cols, width), f32)],
        compiler_params=pltpu.CompilerParams(vmem_limit_bytes=56 << 20),
        name="gate_back",
    )(own_ref, packed_all, att, n1, wg, wo)
    gate_pieces = collect(kept, sent)

    gn1 = lax.psum_scatter(gn1_part, "narrow", scatter_dimension=0, tiled=True)
    grad_tokens = pl.pallas_call(
        tokens_kernel,
        out_shape=sds((share, width), f32),
        compiler_params=pltpu.CompilerParams(vmem_limit_bytes=56 << 20),
        name="tokens_back",
    )(gn1, ggl, w_gate, tokens, grad_hidden)

    grad_query, grad_key, grad_value = pl.pallas_call(
        functools.partial(widen_square_kernel, 3, narrow),
        grid_spec=pltpu.PrefetchScalarGridSpec(
            num_scalar_prefetch=1,
            grid=(2, wide // 2),
            in_specs=slot_specs(wide, (narrow, 3, tall // 2, cols)),
            out_specs=[pl.BlockSpec((tall, width), lambda c, s, own: (out_row(c, s, own), 0))] * 3,
        ),
        out_shape=[sds((width, width), f32)] * 3,
        compiler_params=widened,
        name="widen_square",
    )(own_ref, *square_pieces)
    short = cols // wide
    grad_gate, grad_out = pl.pallas_call(
        functools.partial(widen_gate_kernel, narrow),
        grid_spec=pltpu.PrefetchScalarGridSpec(
            num_scalar_prefetch=1,
            grid=(2, wide // 2),
            in_specs=slot_specs(wide, (narrow, 2, tall // 2, cols)),
            out_specs=[
                pl.BlockSpec((tall, width), lambda c, s, own: (out_row(c, s, own), 0)),
                pl.BlockSpec((narrow, short, width), lambda c, s, own: (0, out_row(c, s, own), 0)),
            ],
        ),
        out_shape=[sds((width, width), f32), sds((narrow, cols, width), f32)],
        compiler_params=widened,
        name="widen_gate",
    )(own_ref, *gate_pieces)
    mixer = (grad_query, grad_key, grad_value, grad_gate, grad_out.reshape(width, width))
    return (output, grad_tokens, *mixer, grad_first, grad_second, grad_third)


def solution(mesh):
    both = P(("wide", "narrow"), None)
    in_specs = (both, P(None, "wide"), P(), P(), P(), P(), P(), P(), P(),
                P(None, "narrow"), P(None, "narrow"), P("narrow", None), both)
    out_specs = (both, both, P(), P(), P(), P(), P(),
                 P(None, "narrow"), P(None, "narrow"), P("narrow", None))
    return jax.shard_map(body, mesh=mesh, in_specs=in_specs, out_specs=out_specs, check_vma=False)
```

```python
import functools

import jax
import jax.numpy as jnp
from jax import lax
from jax.experimental import pallas as pl
from jax.experimental.pallas import tpu as pltpu
from jax.sharding import PartitionSpec as P

BLOCK = 256
epsilon = 1e-06
bf16 = jnp.bfloat16
f32 = jnp.float32
SMEM = pl.BlockSpec(memory_space=pltpu.SMEM)
ANY = pl.BlockSpec(memory_space=pl.ANY)
PARAMS = pltpu.CompilerParams(dimension_semantics=("arbitrary",), vmem_limit_bytes=56 << 20)
sds = jax.ShapeDtypeStruct


def mm(a, b):
    return lax.dot_general(a, b, (((1,), (0,)), ((), ())), preferred_element_type=f32)


def mt(a, b):
    return lax.dot_general(a, b, (((1,), (1,)), ((), ())), preferred_element_type=f32)


def tm(a, b):
    return lax.dot_general(a, b, (((0,), (0,)), ((), ())), preferred_element_type=f32)


def inv_rms(values):
    return lax.rsqrt(jnp.mean(values * values, axis=-1, keepdims=True) + epsilon)


def sigmoid(values):
    return 1.0 / (1.0 + jnp.exp(-values))


def slope(values):
    squashed = sigmoid(values)
    return squashed * (1.0 + values * (1.0 - squashed))


def rms_back(values, inverse, gradient):
    normed = values * inverse
    return inverse * (gradient - normed * jnp.mean(gradient * normed, axis=-1, keepdims=True))


def whole(shape):
    zeros = (0,) * len(shape)
    return pl.BlockSpec(shape, lambda *_: zeros)


def rows(shape, index):
    rest = (0,) * (len(shape) - 1)
    return pl.BlockSpec(shape, lambda b, *_: (index(b), *rest))


def causal_of(size, flip):
    return (lax.broadcasted_iota(jnp.int32, (size, size), 0) ^ flip) >= (
        lax.broadcasted_iota(jnp.int32, (size, size), 1) ^ flip
    )


def decay_weights(causal, g_col, g_row):
    return jnp.where(causal, jnp.exp(jnp.where(causal, g_col - g_row, 0.0)), 0.0)


def flip_of(own, share):
    return share * (own[1] & (BLOCK // share - 1))


def forward_kernel(hn, hd, share, own, tok_a, tok_b, wq, wk, wv, wg, live, gcol, grow, tail, *refs):
    n1, tok, ql, kl, q, k, v, act, intra, contrib = refs[-10:]
    i = pl.program_id(0)

    @pl.when(i == 0)
    def _():
        for part, source in enumerate((tok_a, tok_b)):
            at = slice(part * share, (part + 1) * share)
            tok[at, :] = source[...]
            values = source[...].astype(f32)
            n1[at, :] = (values * inv_rms(values)).astype(bf16)

    normed = n1[...]
    q_lin = mm(normed, wq[...])
    k_lin = mm(normed, wk[...])

    @pl.when(i == own[1])
    def _():
        ql[...] = q_lin
        kl[...] = k_lin

    q[...] = (q_lin * sigmoid(q_lin)).astype(bf16)
    k[...] = (k_lin * sigmoid(k_lin) * live[...]).astype(bf16)
    v[...] = mm(normed, wv[...]).astype(bf16)
    act[...] = sigmoid(mm(normed, wg[...]))
    causal = causal_of(BLOCK, flip_of(own, share))
    for h in range(hn):
        at = slice(h * hd, (h + 1) * hd)
        qh, kh, vh = q[:, at], k[:, at], v[:, at]
        weights = decay_weights(causal, gcol[0, :, h : h + 1], grow[0, h : h + 1, :])
        scores = (mt(qh, kh) * weights).astype(bf16)
        intra[:, at] = mm(scores, vh)
        key_tail = (kh.astype(f32) * tail[0, :, h : h + 1]).astype(bf16)
        contrib[0, h] = tm(key_tail, vh)


def out_kernel(heads, hn, hd, share, own, keep, enter, other, *refs):
    narrow = heads // hn
    states = refs[:narrow]
    contrib, q, intra, act, tok, rise, wo, att, inverse, hidden, n2, kent = refs[narrow:]
    b = pl.program_id(0)
    for h in range(heads):
        at = slice(h * hd, (h + 1) * hd)
        part = own[1] ^ (h // hn)
        base = states[0][h % hn].astype(f32)
        for j in range(1, narrow):
            base = jnp.where(part == j, states[j][h % hn].astype(f32), base)
        entering = enter[b, h] * base + other[b, h] * contrib[1 - b, h]
        kept = (keep[b] * entering).astype(bf16)

        @pl.when(part == 0)
        def _():
            kent[0, h % hn] = kept

        att[:, at] = (intra[:, at] + rise[h // hn, :, h % hn : h % hn + 1] * mm(q[:, at], kept)).astype(bf16)
    values = att[...].astype(f32)
    scale = inv_rms(values)
    inverse[...] = scale
    gated = (values * scale * act[...]).astype(bf16)
    hid = tok[...].astype(f32) + mm(gated, wo[...])

    @pl.when(b == 0)
    def _():
        hidden[...] = hid[:share]

    n2[...] = (hid * inv_rms(hid)).astype(bf16)


def ffn_kernel(share, n2, cot, w1, w2, w3, product, gf, gs, *pieces):
    b = pl.program_id(0)
    normed = n2[...]
    first = mt(normed, w1[...])
    second = mt(normed, w2[...])
    product[...] = (first * second).astype(bf16)
    grad = mt(cot[...], w3[...])
    gf[...] = (grad * second).astype(bf16)
    gs[...] = (grad * first).astype(bf16)
    back = (mm(gf[...], w1[...]) + mm(gs[...], w2[...])).astype(bf16)
    per = BLOCK // share
    for i, piece in enumerate(pieces):
        @pl.when(b == i // per)
        def _():
            piece[...] = back[(i % per) * share : (i % per + 1) * share]


def reversed_bits(value, count):
    out = 0
    for i in range(count):
        out = out | (((value >> i) & 1) << (count - 1 - i))
    return out


def position(offset, parity, wide):
    bits = (wide - 1).bit_length() - 1
    high = offset >> 1
    return jnp.where(parity == 0, reversed_bits(high, bits), high)


def scatter(wide, own, kept, sent, item, piece_of):
    for t in range(wide):
        offset = own[0] ^ t
        parity = own[0] & 1

        @pl.when(offset & 1 == 0)
        def _():
            kept[position(offset, parity, wide), item] = piece_of(t).astype(bf16)

        @pl.when(offset & 1 == 1)
        def _():
            sent[position(offset, 1 - parity, wide), item] = piece_of(t).astype(bf16)


def ffn_cut(wide, ff, width):
    across = min(wide, width // 128)
    return ff // (wide // across), width // across, across


def ffn_grad_kernel(wide, share, own, n2, cot, product, gf, gs, w3, kept, sent, *refs):
    pieces, acc = refs[:-1], refs[-1]
    item = pl.program_id(0)
    for i, (left, right) in enumerate(((gf, n2), (gs, n2), (product, cot))):
        @pl.when(item == i)
        def _():
            acc[...] = tm(left[...], right[...])

    tall, cols, across = ffn_cut(wide, *acc.shape)

    def piece_of(t):
        row, col = t // across * tall, t % across * cols
        return acc[row : row + tall, col : col + cols]

    scatter(wide, own, kept, sent, 0, piece_of)

    @pl.when(item == 2)
    def _():
        for i, piece in enumerate(pieces):
            piece[...] = mm(product[i * share : (i + 1) * share, :], w3[...]).astype(bf16)


def residual_kernel(narrow, own, *refs):
    parts = refs[:narrow]
    hidden, cot, wo, att, inverse, act, grad_hidden, low_out, ggl = refs[narrow : narrow + 9]
    ga = refs[narrow + 9 :]
    gn2 = parts[0][...].astype(f32)
    for part in parts[1:]:
        gn2 = gn2 + part[...].astype(f32)
    hid = hidden[...]
    gh = cot[...].astype(f32) + rms_back(hid, inv_rms(hid), gn2)
    grad_hidden[...] = gh
    low = gh.astype(bf16)
    low_out[...] = low
    gg = mt(low, wo[...])
    values = att[...].astype(f32)
    gate = act[...]
    ggl[...] = (gg * (values * inverse[...]) * gate * (1.0 - gate)).astype(bf16)
    back = rms_back(values, inverse[...], gg * gate).astype(bf16)
    size = back.shape[1] // narrow
    for i in range(narrow):
        for k in range(narrow):
            @pl.when(own[1] ^ i == k)
            def _():
                ga[k][...] = back[:, i * size : (i + 1) * size]


def query_kernel(hn, hd, share, own, keep, ahead, *refs):
    per = BLOCK // share
    ga = refs[: -14]
    q, k, v, ql, kent, gcol, grow, rise, dq, gk, gv, direct, first, grad = refs[-14:]
    b = pl.program_id(0)
    for i, piece in enumerate(ga):
        @pl.when(b == i // per)
        def _():
            grad[(i % per) * share : (i % per + 1) * share, :] = piece[...]

    causal = causal_of(BLOCK, flip_of(own, share))
    for h in range(hn):
        at = slice(h * hd, (h + 1) * hd)
        g, qh, kh, vh = grad[:, at], q[:, at], k[:, at], v[:, at]
        weights = decay_weights(causal, gcol[:, h : h + 1], grow[0, h : h + 1, :])
        scores = (mt(qh, kh) * weights).astype(bf16)
        raw = (mt(g, vh) * weights).astype(bf16)
        up = rise[:, h : h + 1]
        gq = mm(raw, kh) + up * mt(g, kent[0, h])
        dq[:, at] = (gq * slope(ql[:, at])).astype(bf16)
        gk[:, at] = tm(raw, qh)
        gv[:, at] = tm(scores, g)
        now = keep[b] * tm((qh.astype(f32) * up).astype(bf16), g)
        direct[0, h] = now

        @pl.when(b == 0)
        def _():
            first[h] = ahead[b, h] * now

        @pl.when(b > 0)
        def _():
            first[h] += ahead[b, h] * now


def key_kernel(hn, hd, wide, share, own, leave, other, arrived, direct, n1, dq, k, v, kl, gk, gv,
               tail, live, wq, wk, wv, kept, sent, *refs):
    pieces = refs[:-5]
    dk, dv, aq, ak, av = refs[-5:]
    per = BLOCK // share
    b = pl.program_id(0)
    last = pl.num_programs(0) - 1
    for h in range(hn):
        at = slice(h * hd, (h + 1) * hd)
        low = (leave[b, h] * arrived[h] + other[b, h] * direct[1 - b, h]).astype(bf16)
        down = tail[:, h : h + 1]
        grad_key = gk[:, at] + down * mt(v[:, at], low)
        dk[:, at] = (grad_key * live[...] * slope(kl[:, at])).astype(bf16)
        dv[:, at] = (gv[:, at] + down * mm(k[:, at], low)).astype(bf16)
    normed = n1[...]
    tall = normed.shape[1] // wide
    for item, (acc, part) in enumerate(((aq, dq), (ak, dk), (av, dv))):
        now = tm(normed, part[...])

        @pl.when(b == 0)
        def _():
            acc[...] = now

        @pl.when(b > 0)
        def _():
            acc[...] += now

        @pl.when(b == last)
        def _():
            scatter(wide, own, kept, sent, item, lambda t: acc[t * tall : (t + 1) * tall, :])

    back = (mt(dq[...], wq[...]) + mt(dk[...], wk[...]) + mt(dv[...], wv[...])).astype(bf16)
    for i, piece in enumerate(pieces):
        @pl.when(b == i // per)
        def _():
            piece[...] = back[(i % per) * share : (i % per + 1) * share]


def gate_kernel(wide, narrow, share, own, *refs):
    lows = refs[:narrow]
    att, inverse, act, n1, wo, kept, sent, grads, acc, acc_out = refs[narrow:]
    for i, piece in enumerate(lows):
        grads[i * share : (i + 1) * share, :] = piece[...]
    gate = act[...]
    scaled = att[...].astype(f32) * inverse[...]
    gated = (scaled * gate).astype(bf16)
    gg = mt(grads[...], wo[...])
    ggl = (gg * scaled * gate * (1.0 - gate)).astype(bf16)
    acc[...] = tm(n1[...], ggl)
    tall = acc.shape[0] // wide
    scatter(wide, own, kept, sent, 0, lambda t: acc[t * tall : (t + 1) * tall, :])
    acc_out[...] = tm(gated, grads[...])
    cols = gated.shape[1]
    short = cols // wide

    def piece_of(t):
        mine = acc_out[t * short : (t + 1) * short, :]
        return jnp.concatenate([mine[:, i * cols : (i + 1) * cols] for i in range(narrow)], axis=0)

    scatter(wide, own, kept, sent, 1, piece_of)


def tokens_kernel(narrow, *refs):
    parts = refs[:narrow]
    ggl, wg, tok, gh, out = refs[narrow:]
    grad = mt(ggl[...], wg[...])
    for part in parts:
        grad = grad + part[...].astype(f32)
    values = tok[...].astype(f32)
    out[...] = gh[...] + rms_back(values, inv_rms(values), grad)


def output_kernel(narrow, *refs):
    hidden, out = refs[narrow:]
    total = hidden[...]
    for part in refs[:narrow]:
        total = total + part[...].astype(f32)
    out[...] = total.astype(bf16)


def swap_narrow(values, k):
    size = lax.axis_size("narrow")
    return lax.ppermute(values, "narrow", [(i, i ^ k) for i in range(size)])


def gather_narrow(values):
    return [values] + [swap_narrow(values, k) for k in range(1, lax.axis_size("narrow"))]


def trade_narrow(pieces):
    return [pieces[0]] + [swap_narrow(pieces[k], k) for k in range(1, len(pieces))]


def swap_core(values):
    size = lax.axis_size("wide")
    return lax.ppermute(values, "wide", [(i, i ^ 1) for i in range(size)])


def swap_step(values, step):
    size = lax.axis_size("wide")
    bits = (size - 1).bit_length()
    flip = lambda i: i ^ (1 << (1 + step if i % 2 == 0 else bits - 1 - step))
    return lax.ppermute(values, "wide", [(i, flip(i)) for i in range(size)])


def reduce_wide(kept, sent):
    got = swap_core(sent)
    steps = (lax.axis_size("wide") - 1).bit_length() - 1
    low, high = kept, got
    for step in range(steps):
        half = low.shape[0] // 2
        away = low[half:] + high[half:]
        low, high = low[:half] + high[:half], swap_step(away, step)
    return (low + high)[0]


def gather_wide(piece):
    steps = (lax.axis_size("wide") - 1).bit_length() - 1
    full = [piece]
    for step in reversed(range(steps)):
        full = full + [swap_step(part, step) for part in full]
    return full, [swap_core(part) for part in full]


def target(own, place, other, wide):
    bits = (wide - 1).bit_length() - 1
    parity = (own[0] & 1) ^ other
    high = jnp.where(parity == 0, reversed_bits(place, bits), place)
    return own[0] ^ other ^ (2 * high)


def widen_square_kernel(count, narrow, places, own, *refs):
    pieces, outs = refs[:places], refs[-count:]
    for j, piece in enumerate(pieces):
        @pl.when(pl.program_id(0) == j)
        def _():
            cols = piece.shape[-1]
            for item in range(count):
                for n in range(narrow):
                    outs[item][:, n * cols : (n + 1) * cols] = piece[own[1] ^ n, item].astype(f32)


def widen_gate_kernel(narrow, places, own, *refs):
    pieces, (gate, out) = refs[:places], refs[-2:]
    for j, piece in enumerate(pieces):
        @pl.when(pl.program_id(0) == j)
        def _():
            cols = piece.shape[-1]
            short = piece.shape[-2] // narrow
            for n in range(narrow):
                gate[:, n * cols : (n + 1) * cols] = piece[own[1] ^ n, 0].astype(f32)
                for i in range(narrow):
                    out[n, :, i * cols : (i + 1) * cols] = piece[
                        own[1] ^ n, 1, i * short : (i + 1) * short, :
                    ].astype(f32)


def widen_ffn_kernel(places, own, *refs):
    pieces, outs = refs[:places], refs[-3:]
    for j, piece in enumerate(pieces):
        @pl.when(pl.program_id(0) == j)
        def _():
            for item in range(3):
                outs[item][...] = piece[item].astype(f32)


def widen(kernel, own, halves, blocks, shapes, name):
    outs = []
    for other, pieces in enumerate(halves):
        places = len(pieces)

        def spec(shape, index):
            return pl.BlockSpec(shape, lambda i, own: index(target(own, i, other, 2 * places)))

        outs = pl.pallas_call(
            functools.partial(kernel, places),
            grid_spec=pltpu.PrefetchScalarGridSpec(
                num_scalar_prefetch=1,
                grid=(places,),
                in_specs=[whole(p.shape) for p in pieces] + [ANY] * len(outs),
                out_specs=[spec(*block) for block in blocks],
            ),
            out_shape=[sds(shape, f32) for shape in shapes],
            input_output_aliases={1 + places + i: i for i in range(len(outs))},
            compiler_params=PARAMS,
            name=f"{name}_{other}",
        )(own, *pieces, *outs)
    return outs


def xor_order(values, own, axis):
    count = values.shape[axis]
    for bit in range((count - 1).bit_length()):
        step = 1 << bit
        shape = values.shape
        split = values.reshape(shape[:axis] + (count // (2 * step), 2, step) + shape[axis + 1 :])
        flipped = jnp.flip(split, axis + 1)
        values = jnp.where((own >> bit) & 1 == 1, flipped, split).reshape(shape)
    return values


def gather_factors(values):
    size, own = lax.axis_size("wide"), lax.axis_index("wide")
    full = values[None]
    for bit in range((size - 1).bit_length()):
        got = lax.ppermute(full, "wide", [(i, i ^ (1 << bit)) for i in range(size)])
        full = jnp.concatenate([full, got], axis=0)
    return xor_order(full, own, 0)


def between(factors, own, before):
    count = factors.shape[0]
    j = jnp.arange(count)[:, None]
    i = jnp.arange(count)[None, :]
    if before:
        inner, wanted = (i > j) & (i < own), j[:, 0] < own
    else:
        inner, wanted = (i < j) & (i > own), j[:, 0] > own
    terms = jnp.where(inner[:, :, None], factors[None], 1.0)
    return jnp.where(wanted[:, None], jnp.prod(terms, axis=1), 0.0)


def pass_states(message, coef):
    gathered = lax.all_gather(message, "wide", axis=0)
    return jnp.sum(coef[:, :, None, None] * gathered.astype(f32), axis=0)


def body(tokens, log_decay, lengths, pad_counts, w_query, w_key, w_value, w_gate, w_out,
         w_first, w_second, w_third, cotangent):
    wide, narrow = lax.axis_size("wide"), lax.axis_size("narrow")
    own_wide, own_narrow = lax.axis_index("wide"), lax.axis_index("narrow")
    heads, local = log_decay.shape
    share, width = tokens.shape
    hn, cols, hd = heads // narrow, width // narrow, width // heads
    blocks, per = local // BLOCK, BLOCK // share
    own = jnp.stack([own_wide, own_narrow]).astype(jnp.int32)

    tok = gather_narrow(tokens)
    cot = gather_narrow(cotangent)
    cot_all = jnp.concatenate(cot, axis=0)

    ends = jnp.cumsum(lengths, dtype=jnp.int32)
    starts = ends - lengths
    place = jnp.arange(local, dtype=jnp.int32)
    spot = own_wide * local + ((place // share) ^ own_narrow) * share + place % share
    inside = (spot[:, None] >= starts[None, :]) & (spot[:, None] < ends[None, :])
    limit = jnp.sum(jnp.where(inside, (ends - pad_counts)[None, :], 0), axis=1, dtype=jnp.int32)
    live = (spot < limit).astype(f32)[:, None]
    first_spot = own_wide * local + BLOCK * jnp.arange(blocks, dtype=jnp.int32)
    keep_seq = 1.0 - jnp.any(first_spot[:, None] == starts[None, :], axis=1).astype(f32)
    summed = jnp.cumsum(log_decay.reshape(heads, blocks, BLOCK), axis=2)
    last = summed[:, :, -1]
    decay = (jnp.exp(last) * keep_seq[None]).T
    factors = gather_factors(jnp.prod(decay, axis=0))
    factors = lax.dynamic_slice_in_dim(factors, own_narrow * hn, hn, 1)
    coef_in, coef_out = between(factors, own_wide, True), between(factors, own_wide, False)

    def slots(first, second):
        return jnp.where(own_narrow // per == 0, jnp.stack([first, second]), jnp.stack([second, first]))

    def own_heads(values):
        return lax.dynamic_slice_in_dim(values, own_narrow * hn, hn, 1)

    one, zero = jnp.ones_like(decay[0]), jnp.zeros_like(decay[0])
    keep = slots(keep_seq[0], keep_seq[1])
    ends_in = slots(decay[1], one)
    enter, enter_other = slots(one, decay[0]), slots(zero, one)
    ahead, leave_other = own_heads(slots(one, decay[0])), own_heads(slots(one, zero))
    leave = own_heads(ends_in)
    g = xor_order(summed.reshape(heads, narrow, share), own_narrow, 1).reshape(heads, local)
    last_of = jnp.where(own_narrow // per == 0, last, last[:, ::-1])

    def columns(values):
        return values.reshape(narrow, hn, local).transpose(0, 2, 1)

    gcol, rise = columns(g), columns(jnp.exp(g))
    tail = columns(jnp.exp(jnp.repeat(last_of, BLOCK, axis=1) - g))
    grow = g.reshape(narrow, hn, blocks, BLOCK).transpose(2, 0, 1, 3).reshape(blocks * narrow, hn, BLOCK)

    shapes = [sds((local, width), bf16), sds((local, width), bf16), *[sds((local, cols), f32)] * 2,
              *[sds((local, width), bf16)] * 3, *[sds((local, width), f32)] * 2,
              sds((blocks, heads, hd, hd), f32)]
    made = []
    for s in range(blocks):
        weight = pl.BlockSpec((width, cols), lambda i, own: (0, i))
        column = pl.BlockSpec((1, BLOCK, hn), lambda i, own, s=s: (i, s, 0))
        full = pl.BlockSpec((BLOCK, width), lambda i, own, s=s: (s, 0))
        mine = pl.BlockSpec((BLOCK, cols), lambda i, own, s=s: (s, 0))
        part = pl.BlockSpec((BLOCK, cols), lambda i, own, s=s: (s, i))
        made = pl.pallas_call(
            functools.partial(forward_kernel, hn, hd, share),
            grid_spec=pltpu.PrefetchScalarGridSpec(
                num_scalar_prefetch=1,
                grid=(narrow,),
                in_specs=[*[whole((share, width))] * 2, *[weight] * 4,
                          pl.BlockSpec((BLOCK, 1), lambda i, own, s=s: (s, 0)), column,
                          pl.BlockSpec((1, hn, BLOCK), lambda i, own, s=s: (s * narrow + i, 0, 0)),
                          column, *[ANY] * len(made)],
                out_specs=[full, full, mine, mine, *[part] * 5,
                           pl.BlockSpec((1, hn, hd, hd), lambda i, own, s=s: (s, i, 0, 0))],
            ),
            out_shape=shapes,
            input_output_aliases={11 + i: i for i in range(len(made))},
            compiler_params=PARAMS,
            name=f"mixer_forward_{s}",
        )(own, tok[per * s], tok[per * s + 1], w_query, w_key, w_value, w_gate, live, gcol, grow, tail, *made)
    n1, tok_all, ql, kl, q, k, v, act, intra, contrib = made

    message = own_heads(contrib)
    message = jnp.sum(own_heads(ends_in)[:, :, None, None] * message, axis=0).astype(bf16)
    states = gather_narrow(pass_states(message, coef_in).astype(bf16))

    up = lambda b: b
    all_blk, part_blk = rows((BLOCK, width), up), rows((BLOCK, cols), up)
    own_blk = pl.BlockSpec((BLOCK, cols), lambda b, own: (b, own[1]))
    own_kent = rows((1, hn, hd, hd), up)
    att, inverse, hidden, n2, kent = pl.pallas_call(
        functools.partial(out_kernel, heads, hn, hd, share),
        grid_spec=pltpu.PrefetchScalarGridSpec(
            num_scalar_prefetch=1,
            grid=(blocks,),
            in_specs=[SMEM, SMEM, SMEM, *[whole((hn, hd, hd))] * narrow, whole((blocks, heads, hd, hd)),
                      *[all_blk] * 4, pl.BlockSpec((narrow, BLOCK, hn), lambda b, own: (0, b, 0)),
                      whole((width, width))],
            out_specs=[all_blk, rows((BLOCK, 1), up), whole((share, width)), all_blk, own_kent],
        ),
        out_shape=[sds((local, width), bf16), sds((local, 1), f32), sds((share, width), f32),
                   sds((local, width), bf16), sds((blocks, hn, hd, hd), bf16)],
        compiler_params=PARAMS,
        name="mixer_out",
    )(own, keep, enter, enter_other, *states, contrib, q, intra, act, tok_all, rise, w_out)

    ff = w_first.shape[1]
    first_t, second_t = w_first.T, w_second.T
    ff_blk = rows((BLOCK, ff), up)
    piece_spec, piece_shape = whole((share, width)), sds((share, width), bf16)
    product, gf, gs, *gn2 = pl.pallas_call(
        functools.partial(ffn_kernel, share),
        grid=(blocks,),
        in_specs=[all_blk, all_blk, *[whole((ff, width))] * 3],
        out_specs=[*[ff_blk] * 3, *[piece_spec] * narrow],
        out_shape=[*[sds((local, ff), bf16)] * 3, *[piece_shape] * narrow],
        compiler_params=PARAMS,
        name="ffn",
    )(n2, cot_all, first_t, second_t, w_third)
    gn2 = trade_narrow(gn2)

    tall, across = ffn_cut(wide, ff, width)[:2]
    slot = (wide // 2, 3, tall, across)
    slot_spec = pl.BlockSpec((wide // 2, 1, tall, across), lambda i, own: (0, i, 0, 0))
    kept, sent, *ffn_part = pl.pallas_call(
        functools.partial(ffn_grad_kernel, wide, share),
        grid_spec=pltpu.PrefetchScalarGridSpec(
            num_scalar_prefetch=1,
            grid=(3,),
            in_specs=[*[whole((local, width))] * 2, *[whole((local, ff))] * 3, whole((ff, width))],
            out_specs=[slot_spec, slot_spec, *[piece_spec] * narrow],
            scratch_shapes=[pltpu.VMEM((ff, width), f32)],
        ),
        out_shape=[sds(slot, bf16), sds(slot, bf16), *[piece_shape] * narrow],
        compiler_params=PARAMS,
        name="ffn_grads",
    )(own, n2, cot_all, product, gf, gs, w_third)
    ff_halves = gather_wide(reduce_wide(kept, sent))
    ffn_part = trade_narrow(ffn_part)
    output = pl.pallas_call(
        functools.partial(output_kernel, narrow),
        out_shape=sds((share, width), bf16),
        compiler_params=pltpu.CompilerParams(vmem_limit_bytes=56 << 20),
        name="output",
    )(*ffn_part, hidden)

    def single(shape, index=None):
        where = index or (lambda own: (0,) * len(shape))
        return pl.BlockSpec(shape, lambda b, own: where(own))

    row_spec = single((share, width))
    grad_hidden, low, ggl, *ga = pl.pallas_call(
        functools.partial(residual_kernel, narrow),
        grid_spec=pltpu.PrefetchScalarGridSpec(
            num_scalar_prefetch=1,
            grid=(1,),
            in_specs=[*[row_spec] * (narrow + 2), single((width, width)), row_spec, single((share, 1)), row_spec],
            out_specs=[row_spec] * 3 + [single((share, cols))] * narrow,
        ),
        out_shape=[sds((share, width), f32), sds((share, width), bf16), sds((share, width), bf16),
                   *[sds((share, cols), bf16)] * narrow],
        compiler_params=PARAMS,
        name="residual_back",
    )(own, *gn2, hidden, cotangent, w_out, att, inverse, act)
    ga = trade_narrow(ga)
    lows = gather_narrow(low)

    own_col = pl.BlockSpec((None, BLOCK, hn), lambda b, own: (own[1], b, 0))
    own_row = pl.BlockSpec((1, hn, BLOCK), lambda b, own: (b * narrow + own[1], 0, 0))
    dq, gk, gv, direct, message = pl.pallas_call(
        functools.partial(query_kernel, hn, hd, share),
        grid_spec=pltpu.PrefetchScalarGridSpec(
            num_scalar_prefetch=1,
            grid=(blocks,),
            in_specs=[SMEM, SMEM, *[whole((share, cols))] * narrow, *[own_blk] * 3, part_blk, own_kent,
                      own_col, own_row, own_col],
            out_specs=[*[part_blk] * 3, own_kent, whole((hn, hd, hd))],
            scratch_shapes=[pltpu.VMEM((BLOCK, cols), bf16)],
        ),
        out_shape=[sds((local, cols), bf16), *[sds((local, cols), f32)] * 2,
                   sds((blocks, hn, hd, hd), f32), sds((hn, hd, hd), f32)],
        compiler_params=PARAMS,
        name="mixer_query_back",
    )(own, keep, ahead, *ga, q, k, v, ql, kent, gcol, grow, rise)

    arrived = pass_states(message.astype(bf16), coef_out)
    pair = (wide // 2, 3, width // wide, cols)
    own_weight = pl.BlockSpec((width, cols), lambda b, own: (0, own[1]))
    kept, sent, *gn1 = pl.pallas_call(
        functools.partial(key_kernel, hn, hd, wide, share),
        grid_spec=pltpu.PrefetchScalarGridSpec(
            num_scalar_prefetch=1,
            grid=(blocks,),
            in_specs=[SMEM, SMEM, whole((hn, hd, hd)), whole((blocks, hn, hd, hd)), all_blk, part_blk,
                      own_blk, own_blk, *[part_blk] * 3, own_col, rows((BLOCK, 1), up), *[own_weight] * 3],
            out_specs=[*[whole(pair)] * 2, *[piece_spec] * narrow],
            scratch_shapes=[*[pltpu.VMEM((BLOCK, cols), bf16)] * 2, *[pltpu.VMEM((width, cols), f32)] * 3],
        ),
        out_shape=[*[sds(pair, bf16)] * 2, *[piece_shape] * narrow],
        compiler_params=PARAMS,
        name="mixer_key_back",
    )(own, leave, leave_other, arrived, direct, n1, dq, k, v, kl, gk, gv, tail, live, w_query, w_key, w_value)

    def collect(kept, sent):
        return gather_wide(jnp.stack(gather_narrow(reduce_wide(kept, sent))))

    pair = (wide // 2, 2, width // wide, cols)
    own_cols = single((local, cols), lambda own: (0, own[1]))
    gate_kept, gate_sent = pl.pallas_call(
        functools.partial(gate_kernel, wide, narrow, share),
        grid_spec=pltpu.PrefetchScalarGridSpec(
            num_scalar_prefetch=1,
            grid=(1,),
            in_specs=[*[row_spec] * narrow, own_cols, single((local, 1)), own_cols, single((local, width)),
                      single((cols, width), lambda own: (own[1], 0))],
            out_specs=[single(pair)] * 2,
            scratch_shapes=[pltpu.VMEM((local, width), bf16), pltpu.VMEM((width, cols), f32),
                            pltpu.VMEM((cols, width), f32)],
        ),
        out_shape=[sds(pair, bf16)] * 2,
        compiler_params=PARAMS,
        name="gate_back",
    )(own, *lows, att, inverse, act, n1, w_out)
    gate_halves = collect(gate_kept, gate_sent)
    square_halves = collect(kept, sent)

    gn1 = trade_narrow(gn1)
    grad_tokens = pl.pallas_call(
        functools.partial(tokens_kernel, narrow),
        out_shape=sds((share, width), f32),
        compiler_params=pltpu.CompilerParams(vmem_limit_bytes=56 << 20),
        name="tokens_back",
    )(*gn1, ggl, w_gate, tokens, grad_hidden)

    chunks = width // across
    grad_first, grad_second, grad_third = widen(
        widen_ffn_kernel, own, ff_halves, [((tall, across), lambda t: (t // chunks, t % chunks))] * 3,
        [(ff, width)] * 3, "widen_ffn",
    )
    square = ((width // wide, width), lambda t: (t, 0))
    grad_gate, grad_out = widen(
        functools.partial(widen_gate_kernel, narrow), own, gate_halves,
        [square, ((narrow, cols // wide, width), lambda t: (0, t, 0))],
        [(width, width), (narrow, cols, width)], "widen_gate",
    )
    mixer = widen(
        functools.partial(widen_square_kernel, 3, narrow), own, square_halves, [square] * 3,
        [(width, width)] * 3, "widen_square",
    )
    return (output, grad_tokens, *mixer, grad_gate, grad_out.reshape(width, width),
            grad_first.T, grad_second.T, grad_third)


def solution(mesh):
    both = P(("wide", "narrow"), None)
    in_specs = (both, P(None, "wide"), P(), P(), P(), P(), P(), P(), P(),
                P(None, "narrow"), P(None, "narrow"), P("narrow", None), both)
    out_specs = (both, both, P(), P(), P(), P(), P(),
                 P(None, "narrow"), P(None, "narrow"), P("narrow", None))
    return jax.shard_map(body, mesh=mesh, in_specs=in_specs, out_specs=out_specs, check_vma=False)
```

```python
import functools

import jax
import jax.numpy as jnp
from jax import lax
from jax.experimental import pallas as pl
from jax.experimental.pallas import tpu as pltpu
from jax.sharding import PartitionSpec as P

BLOCK = 256
epsilon = 1e-06
bf16 = jnp.bfloat16
f32 = jnp.float32
SMEM = pl.BlockSpec(memory_space=pltpu.SMEM)
ANY = pl.BlockSpec(memory_space=pl.ANY)
PARAMS = pltpu.CompilerParams(dimension_semantics=("arbitrary",), vmem_limit_bytes=56 << 20)
sds = jax.ShapeDtypeStruct


def cost(micros):
    return pl.CostEstimate(flops=0, transcendentals=0, bytes_accessed=int(micros * 3.2e6))


def mm(a, b):
    return lax.dot_general(a, b, (((1,), (0,)), ((), ())), preferred_element_type=f32)


def mt(a, b):
    return lax.dot_general(a, b, (((1,), (1,)), ((), ())), preferred_element_type=f32)


def tm(a, b):
    return lax.dot_general(a, b, (((0,), (0,)), ((), ())), preferred_element_type=f32)


def inv_rms(values):
    return lax.rsqrt(jnp.mean(values * values, axis=-1, keepdims=True) + epsilon)


def sigmoid(values):
    return 1.0 / (1.0 + jnp.exp(-values))


def slope(values):
    squashed = sigmoid(values)
    return squashed * (1.0 + values * (1.0 - squashed))


def rms_back(values, inverse, gradient):
    normed = values * inverse
    return inverse * (gradient - normed * jnp.mean(gradient * normed, axis=-1, keepdims=True))


def whole(shape):
    zeros = (0,) * len(shape)
    return pl.BlockSpec(shape, lambda *_: zeros)


def rows(shape, index):
    rest = (0,) * (len(shape) - 1)
    return pl.BlockSpec(shape, lambda b, *_: (index(b), *rest))


def causal_of(size, flip):
    return (lax.broadcasted_iota(jnp.int32, (size, size), 0) ^ flip) >= (
        lax.broadcasted_iota(jnp.int32, (size, size), 1) ^ flip
    )


def decay_weights(causal, g_col, g_row):
    return jnp.where(causal, jnp.exp(jnp.where(causal, g_col - g_row, 0.0)), 0.0)


def flip_of(own, share):
    return share * (own[1] & (BLOCK // share - 1))


def forward_kernel(hn, hd, share, own, tok_a, tok_b, wq, wk, wv, wg, live, gcol, grow, tail, *refs):
    n1, tok, ql, kl, q, k, v, act, intra, contrib = refs[-10:]
    i = pl.program_id(0)

    @pl.when(i == 0)
    def _():
        for part, source in enumerate((tok_a, tok_b)):
            at = slice(part * share, (part + 1) * share)
            tok[at, :] = source[...]
            values = source[...].astype(f32)
            n1[at, :] = (values * inv_rms(values)).astype(bf16)

    normed = n1[...]
    q_lin = mm(normed, wq[...])
    k_lin = mm(normed, wk[...])

    @pl.when(i == own[1])
    def _():
        ql[...] = q_lin
        kl[...] = k_lin

    q[...] = (q_lin * sigmoid(q_lin)).astype(bf16)
    k[...] = (k_lin * sigmoid(k_lin) * live[...]).astype(bf16)
    v[...] = mm(normed, wv[...]).astype(bf16)
    act[...] = sigmoid(mm(normed, wg[...]))
    causal = causal_of(BLOCK, flip_of(own, share))
    for h in range(hn):
        at = slice(h * hd, (h + 1) * hd)
        qh, kh, vh = q[:, at], k[:, at], v[:, at]
        weights = decay_weights(causal, gcol[0, :, h : h + 1], grow[0, h : h + 1, :])
        scores = (mt(qh, kh) * weights).astype(bf16)
        intra[:, at] = mm(scores, vh)
        key_tail = (kh.astype(f32) * tail[0, :, h : h + 1]).astype(bf16)
        contrib[0, h] = tm(key_tail, vh)


def out_kernel(heads, hn, hd, share, own, keep, enter, other, *refs):
    narrow = heads // hn
    states = refs[:narrow]
    contrib, q, intra, act, tok, rise, wo, att, inverse, gated, hidden, n2, kent = refs[narrow:]
    b = pl.program_id(0)
    for h in range(heads):
        at = slice(h * hd, (h + 1) * hd)
        part = own[1] ^ (h // hn)
        base = states[0][h % hn].astype(f32)
        for j in range(1, narrow):
            base = jnp.where(part == j, states[j][h % hn].astype(f32), base)
        entering = enter[b, h] * base + other[b, h] * contrib[1 - b, h]
        kept = (keep[b] * entering).astype(bf16)

        @pl.when(part == 0)
        def _():
            kent[0, h % hn] = kept

        att[:, at] = (intra[:, at] + rise[h // hn, :, h % hn : h % hn + 1] * mm(q[:, at], kept)).astype(bf16)
    values = att[...].astype(f32)
    scale = inv_rms(values)
    inverse[...] = scale
    gated[...] = (values * scale * act[...]).astype(bf16)
    hid = tok[...].astype(f32) + mm(gated[...], wo[...])

    @pl.when(b == 0)
    def _():
        hidden[...] = hid[:share]

    n2[...] = (hid * inv_rms(hid)).astype(bf16)


def ffn_kernel(share, n2, cot, w1, w2, w3, product, gf, gs, *pieces):
    b = pl.program_id(0)
    normed = n2[...]
    first = mt(normed, w1[...])
    second = mt(normed, w2[...])
    product[...] = (first * second).astype(bf16)
    grad = mt(cot[...], w3[...])
    gf[...] = (grad * second).astype(bf16)
    gs[...] = (grad * first).astype(bf16)
    back = (mm(gf[...], w1[...]) + mm(gs[...], w2[...])).astype(bf16)
    per = BLOCK // share
    for i, piece in enumerate(pieces):
        @pl.when(b == i // per)
        def _():
            piece[...] = back[(i % per) * share : (i % per + 1) * share]


def reversed_bits(value, count):
    out = 0
    for i in range(count):
        out = out | (((value >> i) & 1) << (count - 1 - i))
    return out


def position(offset, parity, wide):
    bits = (wide - 1).bit_length() - 1
    high = offset >> 1
    return jnp.where(parity == 0, reversed_bits(high, bits), high)


def scatter(wide, own, kept, sent, item, piece_of):
    for t in range(wide):
        offset = own[0] ^ t
        parity = own[0] & 1

        @pl.when(offset & 1 == 0)
        def _():
            kept[position(offset, parity, wide), item] = piece_of(t).astype(bf16)

        @pl.when(offset & 1 == 1)
        def _():
            sent[position(offset, 1 - parity, wide), item] = piece_of(t).astype(bf16)


def ffn_cut(wide, ff, width):
    across = min(wide, width // 128)
    return ff // (wide // across), width // across, across


def ffn_grad_kernel(wide, share, own, n2, cot, product, gf, gs, w3, kept, sent, *refs):
    pieces, acc = refs[:-1], refs[-1]
    item = pl.program_id(0)
    for i, (left, right) in enumerate(((gf, n2), (gs, n2), (product, cot))):
        @pl.when(item == i)
        def _():
            acc[...] = tm(left[...], right[...])

    tall, cols, across = ffn_cut(wide, *acc.shape)

    def piece_of(t):
        row, col = t // across * tall, t % across * cols
        return acc[row : row + tall, col : col + cols]

    scatter(wide, own, kept, sent, 0, piece_of)

    @pl.when(item == 2)
    def _():
        for i, piece in enumerate(pieces):
            piece[...] = mm(product[i * share : (i + 1) * share, :], w3[...]).astype(bf16)


def residual_kernel(narrow, own, *refs):
    parts = refs[:narrow]
    hidden, cot, wo, att, inverse, act, grad_hidden, ggl = refs[narrow : narrow + 8]
    trios = refs[narrow + 8 :]
    gn2 = parts[0][...].astype(f32)
    for part in parts[1:]:
        gn2 = gn2 + part[...].astype(f32)
    hid = hidden[...]
    gh = cot[...].astype(f32) + rms_back(hid, inv_rms(hid), gn2)
    grad_hidden[...] = gh
    low = gh.astype(bf16)
    gg = mt(low, wo[...])
    values = att[...].astype(f32)
    gate = act[...]
    ggl[...] = (gg * (values * inverse[...]) * gate * (1.0 - gate)).astype(bf16)
    back = rms_back(values, inverse[...], gg * gate).astype(bf16)
    size = back.shape[1] // narrow
    for i in range(narrow):
        for k in range(narrow):
            @pl.when(own[1] ^ i == k)
            def _():
                at = slice(i * size, (i + 1) * size)
                trios[k][:, :size] = back[:, at]
                trios[k][:, size : 2 * size] = ggl[:, at]
                trios[k][:, 2 * size :] = low[:, at]


def query_kernel(hn, hd, share, own, keep, ahead, *refs):
    per = BLOCK // share
    ga = refs[: -14]
    q, k, v, ql, kent, gcol, grow, rise, dq, gk, gv, direct, first, grad = refs[-14:]
    b = pl.program_id(0)
    for i, piece in enumerate(ga):
        @pl.when(b == i // per)
        def _():
            grad[(i % per) * share : (i % per + 1) * share, :] = piece[:, : grad.shape[1]]

    causal = causal_of(BLOCK, flip_of(own, share))
    for h in range(hn):
        at = slice(h * hd, (h + 1) * hd)
        g, qh, kh, vh = grad[:, at], q[:, at], k[:, at], v[:, at]
        weights = decay_weights(causal, gcol[:, h : h + 1], grow[0, h : h + 1, :])
        scores = (mt(qh, kh) * weights).astype(bf16)
        raw = (mt(g, vh) * weights).astype(bf16)
        up = rise[:, h : h + 1]
        gq = mm(raw, kh) + up * mt(g, kent[0, h])
        dq[:, at] = (gq * slope(ql[:, at])).astype(bf16)
        gk[:, at] = tm(raw, qh)
        gv[:, at] = tm(scores, g)
        now = keep[b] * tm((qh.astype(f32) * up).astype(bf16), g)
        direct[0, h] = now

        @pl.when(b == 0)
        def _():
            first[h] = ahead[b, h] * now

        @pl.when(b > 0)
        def _():
            first[h] += ahead[b, h] * now


def key_kernel(hn, hd, wide, share, own, leave, other, arrived, direct, n1, dq, k, v, kl, gk, gv,
               tail, live, _kept, _sent, kept, sent, *refs):
    pieces = refs[:-5]
    dk, dv, aq, ak, av = refs[-5:]
    per = BLOCK // share
    b = pl.program_id(0)
    last = pl.num_programs(0) - 1
    for h in range(hn):
        at = slice(h * hd, (h + 1) * hd)
        low = (leave[b, h] * arrived[h] + other[b, h] * direct[1 - b, h]).astype(bf16)
        down = tail[:, h : h + 1]
        grad_key = gk[:, at] + down * mt(v[:, at], low)
        dk[:, at] = (grad_key * live[...] * slope(kl[:, at])).astype(bf16)
        dv[:, at] = (gv[:, at] + down * mm(k[:, at], low)).astype(bf16)
    normed = n1[...]
    tall = normed.shape[1] // wide
    for item, (acc, part) in enumerate(((aq, dq), (ak, dk), (av, dv))):
        now = tm(normed, part[...])

        @pl.when(b == 0)
        def _():
            acc[...] = now

        @pl.when(b > 0)
        def _():
            acc[...] += now

        @pl.when(b == last)
        def _():
            scatter(wide, own, kept, sent, item, lambda t: acc[t * tall : (t + 1) * tall, :])

    cols = dq.shape[1]
    for i, piece in enumerate(pieces):
        @pl.when(b == i // per)
        def _():
            for item, part in enumerate((dq, dk, dv)):
                piece[:, item * cols : (item + 1) * cols] = part[(i % per) * share : (i % per + 1) * share, :]


def gate_kernel(wide, share, own, *refs):
    trios = refs[:-6]
    n1, gated, kept, sent, grads, acc = refs[-6:]
    item = pl.program_id(0)
    cols = acc.shape[1]
    tall = acc.shape[0] // wide
    for step, left in enumerate((n1, gated)):
        @pl.when(item == step)
        def _():
            at = slice((step + 1) * cols, (step + 2) * cols)
            for i, piece in enumerate(trios):
                grads[i * share : (i + 1) * share, :] = piece[:, at]
            acc[...] = tm(left[...], grads[...])

    scatter(wide, own, kept, sent, 0, lambda t: acc[t * tall : (t + 1) * tall, :])


def tokens_kernel(narrow, own, *refs):
    parts = refs[:narrow]
    ggl, wq, wk, wv, wg, tok, gh, out, *grads = refs[narrow:]
    cols = parts[0].shape[1] // 3
    for i in range(narrow):
        for k in range(narrow):
            @pl.when(own[1] ^ i == k)
            def _():
                for item, full in enumerate(grads):
                    full[:, i * cols : (i + 1) * cols] = parts[k][:, item * cols : (item + 1) * cols]

    grad = mt(ggl[...], wg[...])
    for full, weight in zip(grads, (wq, wk, wv)):
        grad = grad + mt(full[...], weight[...])
    values = tok[...].astype(f32)
    out[...] = gh[...] + rms_back(values, inv_rms(values), grad)


def output_kernel(narrow, *refs):
    hidden, out = refs[narrow:]
    total = hidden[...]
    for part in refs[:narrow]:
        total = total + part[...].astype(f32)
    out[...] = total.astype(bf16)


def swap_narrow(values, k):
    size = lax.axis_size("narrow")
    return lax.ppermute(values, "narrow", [(i, i ^ k) for i in range(size)])


def gather_narrow(values):
    return [values] + [swap_narrow(values, k) for k in range(1, lax.axis_size("narrow"))]


def trade_narrow(pieces):
    return [pieces[0]] + [swap_narrow(pieces[k], k) for k in range(1, len(pieces))]


def swap_core(values):
    size = lax.axis_size("wide")
    return lax.ppermute(values, "wide", [(i, i ^ 1) for i in range(size)])


def swap_step(values, step):
    size = lax.axis_size("wide")
    bits = (size - 1).bit_length()
    flip = lambda i: i ^ (1 << (1 + step if i % 2 == 0 else bits - 1 - step))
    return lax.ppermute(values, "wide", [(i, flip(i)) for i in range(size)])


def fence(*values):
    return lax.optimization_barrier(values)


def halved(low, high):
    half = low.shape[0] // 2
    return low[:half] + high[:half], low[half:] + high[half:]


def swap_all(parts, step):
    return [swap_step(part, step) for part in parts]


def swap_cores(parts):
    return [swap_core(part) for part in parts]


def target(own, place, other, wide):
    bits = (wide - 1).bit_length() - 1
    parity = (own[0] & 1) ^ other
    high = jnp.where(parity == 0, reversed_bits(place, bits), place)
    return own[0] ^ other ^ (2 * high)


def widen_square_kernel(count, narrow, places, own, *refs):
    pieces, outs = refs[:places], refs[-count:]
    for j, piece in enumerate(pieces):
        @pl.when(pl.program_id(0) == j)
        def _():
            cols = piece.shape[-1]
            for item in range(count):
                for n in range(narrow):
                    outs[item][:, n * cols : (n + 1) * cols] = piece[own[1] ^ n, item].astype(f32)


def widen_ffn_kernel(places, own, *refs):
    pieces, outs = refs[:places], refs[-3:]
    for j, piece in enumerate(pieces):
        @pl.when(pl.program_id(0) == j)
        def _():
            for item in range(3):
                outs[item][...] = piece[item].astype(f32)


def widen(kernel, own, other, pieces, block, cut, shape, outs, count, name):
    places = len(pieces)
    spec = pl.BlockSpec(block, lambda i, own: cut(target(own, i, other, 2 * places)))
    return pl.pallas_call(
        functools.partial(kernel, places),
        grid_spec=pltpu.PrefetchScalarGridSpec(
            num_scalar_prefetch=1,
            grid=(places,),
            in_specs=[whole(p.shape) for p in pieces] + [ANY] * len(outs),
            out_specs=[spec] * count,
        ),
        out_shape=[sds(shape, f32)] * count,
        input_output_aliases={1 + places + i: i for i in range(len(outs))},
        compiler_params=PARAMS,
        cost_estimate=cost(4),
        name=f"{name}_{other}",
    )(own, *pieces, *outs)


def xor_order(values, own, axis):
    count = values.shape[axis]
    for bit in range((count - 1).bit_length()):
        step = 1 << bit
        shape = values.shape
        split = values.reshape(shape[:axis] + (count // (2 * step), 2, step) + shape[axis + 1 :])
        flipped = jnp.flip(split, axis + 1)
        values = jnp.where((own >> bit) & 1 == 1, flipped, split).reshape(shape)
    return values


def gather_factors(values):
    size, own = lax.axis_size("wide"), lax.axis_index("wide")
    full = values[None]
    for bit in range((size - 1).bit_length()):
        got = lax.ppermute(full, "wide", [(i, i ^ (1 << bit)) for i in range(size)])
        full = jnp.concatenate([full, got], axis=0)
    return xor_order(full, own, 0)


def between(factors, own, before):
    count = factors.shape[0]
    j = jnp.arange(count)[:, None]
    i = jnp.arange(count)[None, :]
    if before:
        inner, wanted = (i > j) & (i < own), j[:, 0] < own
    else:
        inner, wanted = (i < j) & (i > own), j[:, 0] > own
    terms = jnp.where(inner[:, :, None], factors[None], 1.0)
    return jnp.where(wanted[:, None], jnp.prod(terms, axis=1), 0.0)


def pass_states(message, coef):
    gathered = lax.all_gather(message, "wide", axis=0)
    return jnp.sum(coef[:, :, None, None] * gathered.astype(f32), axis=0)


def body(tokens, log_decay, lengths, pad_counts, w_query, w_key, w_value, w_gate, w_out,
         w_first, w_second, w_third, cotangent):
    wide, narrow = lax.axis_size("wide"), lax.axis_size("narrow")
    own_wide, own_narrow = lax.axis_index("wide"), lax.axis_index("narrow")
    heads, local = log_decay.shape
    share, width = tokens.shape
    hn, cols, hd = heads // narrow, width // narrow, width // heads
    blocks, per = local // BLOCK, BLOCK // share
    own = jnp.stack([own_wide, own_narrow]).astype(jnp.int32)

    tok = gather_narrow(tokens)

    ends = jnp.cumsum(lengths, dtype=jnp.int32)
    starts = ends - lengths
    place = jnp.arange(local, dtype=jnp.int32)
    spot = own_wide * local + ((place // share) ^ own_narrow) * share + place % share
    inside = (spot[:, None] >= starts[None, :]) & (spot[:, None] < ends[None, :])
    limit = jnp.sum(jnp.where(inside, (ends - pad_counts)[None, :], 0), axis=1, dtype=jnp.int32)
    live = (spot < limit).astype(f32)[:, None]
    first_spot = own_wide * local + BLOCK * jnp.arange(blocks, dtype=jnp.int32)
    keep_seq = 1.0 - jnp.any(first_spot[:, None] == starts[None, :], axis=1).astype(f32)
    summed = jnp.cumsum(log_decay.reshape(heads, blocks, BLOCK), axis=2)
    last = summed[:, :, -1]
    decay = (jnp.exp(last) * keep_seq[None]).T

    def slots(first, second):
        return jnp.where(own_narrow // per == 0, jnp.stack([first, second]), jnp.stack([second, first]))

    def own_heads(values):
        return lax.dynamic_slice_in_dim(values, own_narrow * hn, hn, 1)

    one, zero = jnp.ones_like(decay[0]), jnp.zeros_like(decay[0])
    keep = slots(keep_seq[0], keep_seq[1])
    ends_in = slots(decay[1], one)
    enter, enter_other = slots(one, decay[0]), slots(zero, one)
    ahead, leave_other = own_heads(slots(one, decay[0])), own_heads(slots(one, zero))
    leave = own_heads(ends_in)
    g = xor_order(summed.reshape(heads, narrow, share), own_narrow, 1).reshape(heads, local)
    last_of = jnp.where(own_narrow // per == 0, last, last[:, ::-1])

    def columns(values):
        return values.reshape(narrow, hn, local).transpose(0, 2, 1)

    gcol, rise = columns(g), columns(jnp.exp(g))
    tail = columns(jnp.exp(jnp.repeat(last_of, BLOCK, axis=1) - g))
    grow = g.reshape(narrow, hn, blocks, BLOCK).transpose(2, 0, 1, 3).reshape(blocks * narrow, hn, BLOCK)

    shapes = [sds((local, width), bf16), sds((local, width), bf16), *[sds((local, cols), f32)] * 2,
              *[sds((local, width), bf16)] * 3, *[sds((local, width), f32)] * 2,
              sds((blocks, heads, hd, hd), f32)]
    made = []
    for s in range(blocks):
        if s == 1:
            made, later, cotangent_now, product_now = fence(made, tok[per:], cotangent, jnp.prod(decay, axis=0))
            tok = tok[:per] + list(later)
        weight = pl.BlockSpec((width, cols), lambda i, own: (0, i))
        column = pl.BlockSpec((1, BLOCK, hn), lambda i, own, s=s: (i, s, 0))
        full = pl.BlockSpec((BLOCK, width), lambda i, own, s=s: (s, 0))
        mine = pl.BlockSpec((BLOCK, cols), lambda i, own, s=s: (s, 0))
        part = pl.BlockSpec((BLOCK, cols), lambda i, own, s=s: (s, i))
        made = pl.pallas_call(
            functools.partial(forward_kernel, hn, hd, share),
            grid_spec=pltpu.PrefetchScalarGridSpec(
                num_scalar_prefetch=1,
                grid=(narrow,),
                in_specs=[*[whole((share, width))] * 2, *[weight] * 4,
                          pl.BlockSpec((BLOCK, 1), lambda i, own, s=s: (s, 0)), column,
                          pl.BlockSpec((1, hn, BLOCK), lambda i, own, s=s: (s * narrow + i, 0, 0)),
                          column, *[ANY] * len(made)],
                out_specs=[full, full, mine, mine, *[part] * 5,
                           pl.BlockSpec((1, hn, hd, hd), lambda i, own, s=s: (s, i, 0, 0))],
            ),
            out_shape=shapes,
            input_output_aliases={11 + i: i for i in range(len(made))},
            compiler_params=PARAMS,
            cost_estimate=cost(10),
            name=f"mixer_forward_{s}",
        )(own, tok[per * s], tok[per * s + 1], w_query, w_key, w_value, w_gate, live, gcol, grow, tail, *made)
    n1, tok_all, ql, kl, q, k, v, act, intra, contrib = made

    cot = gather_narrow(cotangent_now)
    factors = gather_factors(product_now)
    factors = lax.dynamic_slice_in_dim(factors, own_narrow * hn, hn, 1)
    coef_in, coef_out = between(factors, own_wide, True), between(factors, own_wide, False)
    message = own_heads(contrib)
    message = jnp.sum(own_heads(ends_in)[:, :, None, None] * message, axis=0).astype(bf16)
    entering, cot = fence(pass_states(message, coef_in).astype(bf16), cot)
    cot_all = jnp.concatenate(cot, axis=0)
    states = gather_narrow(entering)

    up = lambda b: b
    all_blk, part_blk = rows((BLOCK, width), up), rows((BLOCK, cols), up)
    own_blk = pl.BlockSpec((BLOCK, cols), lambda b, own: (b, own[1]))
    own_kent = rows((1, hn, hd, hd), up)
    att, inverse, gated, hidden, n2, kent = pl.pallas_call(
        functools.partial(out_kernel, heads, hn, hd, share),
        grid_spec=pltpu.PrefetchScalarGridSpec(
            num_scalar_prefetch=1,
            grid=(blocks,),
            in_specs=[SMEM, SMEM, SMEM, *[whole((hn, hd, hd))] * narrow, whole((blocks, heads, hd, hd)),
                      *[all_blk] * 4, pl.BlockSpec((narrow, BLOCK, hn), lambda b, own: (0, b, 0)),
                      whole((width, width))],
            out_specs=[all_blk, rows((BLOCK, 1), up), all_blk, whole((share, width)), all_blk, own_kent],
        ),
        out_shape=[sds((local, width), bf16), sds((local, 1), f32), sds((local, width), bf16), sds((share, width), f32),
                   sds((local, width), bf16), sds((blocks, hn, hd, hd), bf16)],
        compiler_params=PARAMS,
        cost_estimate=cost(9.5),
        name="mixer_out",
    )(own, keep, enter, enter_other, *states, contrib, q, intra, act, tok_all, rise, w_out)

    ff = w_first.shape[1]
    first_t, second_t = w_first.T, w_second.T
    ff_blk = rows((BLOCK, ff), up)
    piece_spec, piece_shape = whole((share, width)), sds((share, width), bf16)
    product, gf, gs, *gn2 = pl.pallas_call(
        functools.partial(ffn_kernel, share),
        grid=(blocks,),
        in_specs=[all_blk, all_blk, *[whole((ff, width))] * 3],
        out_specs=[*[ff_blk] * 3, *[piece_spec] * narrow],
        out_shape=[*[sds((local, ff), bf16)] * 3, *[piece_shape] * narrow],
        compiler_params=PARAMS,
        cost_estimate=cost(10),
        name="ffn",
    )(n2, cot_all, first_t, second_t, w_third)

    gn2 = trade_narrow(gn2)
    product_now, _ = fence(product, gn2[1])
    tall, across = ffn_cut(wide, ff, width)[:2]
    slot = (wide // 2, 3, tall, across)
    slot_spec = pl.BlockSpec((wide // 2, 1, tall, across), lambda i, own: (0, i, 0, 0))
    kept, sent, *ffn_part = pl.pallas_call(
        functools.partial(ffn_grad_kernel, wide, share),
        grid_spec=pltpu.PrefetchScalarGridSpec(
            num_scalar_prefetch=1,
            grid=(3,),
            in_specs=[*[whole((local, width))] * 2, *[whole((local, ff))] * 3, whole((ff, width))],
            out_specs=[slot_spec, slot_spec, *[piece_spec] * narrow],
            scratch_shapes=[pltpu.VMEM((ff, width), f32)],
        ),
        out_shape=[sds(slot, bf16), sds(slot, bf16), *[piece_shape] * narrow],
        compiler_params=PARAMS,
        cost_estimate=cost(10),
        name="ffn_grads",
    )(own, n2, cot_all, product_now, gf, gs, w_third)
    gn2, kept, sent = fence(gn2, kept, sent)
    steps = (wide - 1).bit_length() - 1

    def single(shape, index=None):
        where = index or (lambda own: (0,) * len(shape))
        return pl.BlockSpec(shape, lambda b, own: where(own))

    row_spec = single((share, width))
    grad_hidden, ggl, *trios = pl.pallas_call(
        functools.partial(residual_kernel, narrow),
        grid_spec=pltpu.PrefetchScalarGridSpec(
            num_scalar_prefetch=1,
            grid=(1,),
            in_specs=[*[row_spec] * (narrow + 2), single((width, width)), row_spec, single((share, 1)), row_spec],
            out_specs=[row_spec] * 2 + [single((share, 3 * cols))] * narrow,
        ),
        out_shape=[sds((share, width), f32), sds((share, width), bf16),
                   *[sds((share, 3 * cols), bf16)] * narrow],
        compiler_params=PARAMS,
        cost_estimate=cost(5),
        name="residual_back",
    )(own, *gn2, hidden, cotangent, w_out, att, inverse, act)
    trios, kept, sent = fence(trios, kept, sent)
    trios, kept, got = fence(trade_narrow(trios), kept, swap_core(sent))
    low, away = halved(kept, got)
    got = swap_step(away, 0)

    own_col = pl.BlockSpec((None, BLOCK, hn), lambda b, own: (own[1], b, 0))
    own_row = pl.BlockSpec((1, hn, BLOCK), lambda b, own: (b * narrow + own[1], 0, 0))
    dq, gk, gv, direct, message = pl.pallas_call(
        functools.partial(query_kernel, hn, hd, share),
        grid_spec=pltpu.PrefetchScalarGridSpec(
            num_scalar_prefetch=1,
            grid=(blocks,),
            in_specs=[SMEM, SMEM, *[whole((share, 3 * cols))] * narrow, *[own_blk] * 3, part_blk, own_kent,
                      own_col, own_row, own_col],
            out_specs=[*[part_blk] * 3, own_kent, whole((hn, hd, hd))],
            scratch_shapes=[pltpu.VMEM((BLOCK, cols), bf16)],
        ),
        out_shape=[sds((local, cols), bf16), *[sds((local, cols), f32)] * 2,
                   sds((blocks, hn, hd, hd), f32), sds((hn, hd, hd), f32)],
        compiler_params=PARAMS,
        cost_estimate=cost(5.4),
        name="mixer_query_back",
    )(own, keep, ahead, *trios, q, k, v, ql, kent, gcol, grow, rise)

    arrived, low, got = fence(pass_states(message.astype(bf16), coef_out), low, got)
    low_ff, away_ff = halved(low, got)

    five = (wide // 2, 5, width // wide, cols)
    one = pl.BlockSpec((wide // 2, 1, width // wide, cols), lambda i, own: (0, 3 + i, 0, 0))
    kept, sent = pl.pallas_call(
        functools.partial(gate_kernel, wide, share),
        grid_spec=pltpu.PrefetchScalarGridSpec(
            num_scalar_prefetch=1,
            grid=(2,),
            in_specs=[*[single((share, 3 * cols))] * narrow, *[single((local, width))] * 2],
            out_specs=[one] * 2,
            scratch_shapes=[pltpu.VMEM((local, cols), bf16), pltpu.VMEM((width, cols), f32)],
        ),
        out_shape=[sds(five, bf16)] * 2,
        compiler_params=PARAMS,
        cost_estimate=cost(5),
        name="gate_back",
    )(own, *trios, n1, gated)
    three = whole((wide // 2, 3, width // wide, cols))
    trio_spec, trio_shape = whole((share, 3 * cols)), sds((share, 3 * cols), bf16)
    kept, sent, *dqkv = pl.pallas_call(
        functools.partial(key_kernel, hn, hd, wide, share),
        grid_spec=pltpu.PrefetchScalarGridSpec(
            num_scalar_prefetch=1,
            grid=(blocks,),
            in_specs=[SMEM, SMEM, whole((hn, hd, hd)), whole((blocks, hn, hd, hd)), all_blk, part_blk,
                      own_blk, own_blk, *[part_blk] * 3, own_col, rows((BLOCK, 1), up), ANY, ANY],
            out_specs=[three, three, *[trio_spec] * narrow],
            scratch_shapes=[*[pltpu.VMEM((BLOCK, cols), bf16)] * 2, *[pltpu.VMEM((width, cols), f32)] * 3],
        ),
        out_shape=[*[sds(five, bf16)] * 2, *[trio_shape] * narrow],
        input_output_aliases={14: 0, 15: 1},
        compiler_params=PARAMS,
        cost_estimate=cost(9),
        name="mixer_key_back",
    )(own, leave, leave_other, arrived, direct, n1, dq, k, v, kl, gk, gv, tail, live, kept, sent)

    low, away = halved(kept, swap_core(sent))
    low, away, dqkv, away_ff = fence(low, away, dqkv, away_ff)
    low, high, dqkv, high_ff = fence(low, swap_step(away, 0), trade_narrow(dqkv), swap_step(away_ff, 1))
    for step in range(1, steps):
        low, away = halved(low, high)
        high = swap_step(away, step)
    for step in range(2, steps):
        low_ff, away_ff = halved(low_ff, high_ff)
        high_ff = swap_step(away_ff, step)
    piece = (low + high)[0]
    ff_piece = [(low_ff + high_ff)[0]]

    for step in reversed(range(1, steps)):
        ff_piece = ff_piece + swap_all(ff_piece, step)
    gate_piece, piece, ff_piece = fence(jnp.stack(gather_narrow(piece[3:])), piece[:3], ff_piece)
    chunks = width // across
    ffn_form = (tall, across), lambda t: (t // chunks, t % chunks), (ff, width)
    square_form = (width // wide, width), lambda t: (t, 0), (width, width)
    gate_kernels = functools.partial(widen_square_kernel, 2, narrow)
    square_kernels = functools.partial(widen_square_kernel, 3, narrow)

    zs = gather_narrow(piece)
    ff_piece = ff_piece + swap_all(ff_piece, 0)
    gate_piece = [gate_piece]
    for step in reversed(range(1, steps)):
        gate_piece = gate_piece + swap_all(gate_piece, step)
    half = len(gate_piece) // 2
    gate_more = swap_all(gate_piece, 0)
    dqkv, _ = fence(dqkv, zs[1])
    grad_tokens = pl.pallas_call(
        functools.partial(tokens_kernel, narrow),
        grid_spec=pltpu.PrefetchScalarGridSpec(
            num_scalar_prefetch=1,
            grid=(1,),
            in_specs=[*[single((share, 3 * cols))] * narrow, row_spec, *[single((width, width))] * 4,
                      row_spec, row_spec],
            out_specs=row_spec,
            scratch_shapes=[pltpu.VMEM((share, width), bf16)] * 3,
        ),
        out_shape=sds((share, width), f32),
        compiler_params=PARAMS,
        cost_estimate=cost(8),
        name="tokens_back",
    )(own, *dqkv, ggl, w_query, w_key, w_value, w_gate, tokens, grad_hidden)
    square_piece, gate_piece, ff_piece, ffn_part, grad_tokens = fence(
        jnp.stack(zs), gate_piece + gate_more, ff_piece, ffn_part, grad_tokens
    )

    square_piece = [square_piece]
    for step in reversed(range(1, steps)):
        square_piece = square_piece + swap_all(square_piece, step)
    square_more = swap_all(square_piece[:half], 0)
    ffn_out = widen(widen_ffn_kernel, own, 0, ff_piece, *ffn_form, [], 3, "widen_ffn")
    gate_out = widen(gate_kernels, own, 0, gate_piece, *square_form, [], 2, "widen_gate")
    square_piece, square_more, ffn_out, gate_out, gate_other, ff_other, ffn_part = fence(
        square_piece, square_more, ffn_out, gate_out, swap_cores(gate_piece), swap_cores(ff_piece), ffn_part
    )

    ffn_part = trade_narrow(ffn_part)
    square_last = swap_all(square_piece[half:], 0)
    ffn_out = widen(widen_ffn_kernel, own, 1, ff_other, *ffn_form, ffn_out, 3, "widen_ffn")
    gate_out = widen(gate_kernels, own, 1, gate_other, *square_form, gate_out, 2, "widen_gate")
    square_piece, ffn_out, gate_out, ffn_part = fence(
        square_piece + square_more + square_last, ffn_out, gate_out, ffn_part
    )

    output = pl.pallas_call(
        functools.partial(output_kernel, narrow),
        out_shape=sds((share, width), bf16),
        compiler_params=pltpu.CompilerParams(vmem_limit_bytes=56 << 20),
        cost_estimate=cost(2),
        name="output",
    )(*ffn_part, hidden)
    mixer = widen(square_kernels, own, 0, square_piece, *square_form, [], 3, "widen_square")
    square_other = swap_cores(square_piece)
    mixer = widen(square_kernels, own, 1, square_other, *square_form, mixer, 3, "widen_square")
    grad_first, grad_second, grad_third = ffn_out
    grad_gate, grad_out = gate_out
    return (output, grad_tokens, *mixer, grad_gate, grad_out, grad_first.T, grad_second.T, grad_third)


def solution(mesh):
    both = P(("wide", "narrow"), None)
    in_specs = (both, P(None, "wide"), P(), P(), P(), P(), P(), P(), P(),
                P(None, "narrow"), P(None, "narrow"), P("narrow", None), both)
    out_specs = (both, both, P(), P(), P(), P(), P(),
                 P(None, "narrow"), P(None, "narrow"), P("narrow", None))
    return jax.shard_map(body, mesh=mesh, in_specs=in_specs, out_specs=out_specs, check_vma=False)
```

```python
import functools

import jax
import jax.numpy as jnp
from jax import lax
from jax.experimental import pallas as pl
from jax.experimental.pallas import tpu as pltpu
from jax.sharding import PartitionSpec as P

BLOCK = 256
epsilon = 1e-06
bf16 = jnp.bfloat16
f32 = jnp.float32
SMEM = pl.BlockSpec(memory_space=pltpu.SMEM)
ANY = pl.BlockSpec(memory_space=pl.ANY)
PARAMS = pltpu.CompilerParams(dimension_semantics=("arbitrary",), vmem_limit_bytes=56 << 20)
sds = jax.ShapeDtypeStruct


def cost(micros):
    return pl.CostEstimate(flops=0, transcendentals=0, bytes_accessed=int(micros * 3.2e6))


def mm(a, b):
    return lax.dot_general(a, b, (((1,), (0,)), ((), ())), preferred_element_type=f32)


def mt(a, b):
    return lax.dot_general(a, b, (((1,), (1,)), ((), ())), preferred_element_type=f32)


def tm(a, b):
    return lax.dot_general(a, b, (((0,), (0,)), ((), ())), preferred_element_type=f32)


def inv_rms(values):
    return lax.rsqrt(jnp.mean(values * values, axis=-1, keepdims=True) + epsilon)


def sigmoid(values):
    return 1.0 / (1.0 + jnp.exp(-values))


def slope(values):
    squashed = sigmoid(values)
    return squashed * (1.0 + values * (1.0 - squashed))


def rms_back(values, inverse, gradient):
    normed = values * inverse
    return inverse * (gradient - normed * jnp.mean(gradient * normed, axis=-1, keepdims=True))


def whole(shape):
    zeros = (0,) * len(shape)
    return pl.BlockSpec(shape, lambda *_: zeros)


def rows(shape, index):
    rest = (0,) * (len(shape) - 1)
    return pl.BlockSpec(shape, lambda b, *_: (index(b), *rest))


def causal_of(size, flip):
    return (lax.broadcasted_iota(jnp.int32, (size, size), 0) ^ flip) >= (
        lax.broadcasted_iota(jnp.int32, (size, size), 1) ^ flip
    )


def decay_weights(causal, g_col, g_row):
    return jnp.where(causal, jnp.exp(jnp.where(causal, g_col - g_row, 0.0)), 0.0)


def flip_of(own, share):
    return share * (own[1] & (BLOCK // share - 1))


def exact(a, b, dims):
    return lax.dot_general(a, b, (dims, ((), ())), precision=lax.Precision.HIGHEST, preferred_element_type=f32)


KEEP, ENTER, ENDS, FIRST, SECOND = range(5)


def layout_kernel(narrow, share, own, lengths, pads, log_decay, gcol, rise, tail, grow, live, coefs, total):
    heads, local = log_decay.shape
    hn = heads // narrow
    per, blocks = BLOCK // share, local // BLOCK
    base = own[0] * local
    place = lax.broadcasted_iota(jnp.int32, (local, 1), 0)
    spot = base + ((place // share) ^ own[1]) * share + place % share
    alive = jnp.zeros((local, 1), f32)
    keeps = [jnp.float32(1.0)] * blocks
    end = jnp.int32(0)
    for s in range(lengths.shape[0]):
        start, end = end, end + lengths[s]
        alive = jnp.where((spot >= start) & (spot < end - pads[s]), 1.0, alive)
        keeps = [jnp.where(start == base + b * BLOCK, 0.0, keep) for b, keep in enumerate(keeps)]
    live[...] = alive

    size = (BLOCK, BLOCK)
    upper = (lax.broadcasted_iota(jnp.int32, size, 0) <= lax.broadcasted_iota(jnp.int32, size, 1)).astype(f32)
    eye = (lax.broadcasted_iota(jnp.int32, (heads, heads), 0)
           == lax.broadcasted_iota(jnp.int32, (heads, heads), 1)).astype(f32)
    turned = own[1] // per > 0
    rows_of, ends_of, decay_of, keep_of = [], [], [], []
    for b in range(blocks):
        part = log_decay[:, b * BLOCK : (b + 1) * BLOCK]
        g = exact(part, upper, ((1,), (0,)))
        for bit in range((per - 1).bit_length()):
            step = share << bit
            flipped = [g[:, (i ^ 1) * step : ((i ^ 1) + 1) * step] for i in range(BLOCK // step)]
            g = jnp.where((own[1] >> bit) & 1 == 1, jnp.concatenate(flipped, axis=1), g)
        end_row = exact(jnp.ones_like(part), part, ((1,), (1,)))[0:1]
        rows_of.append(g)
        ends_of.append(end_row)
        decay_of.append(jnp.exp(end_row) * keeps[b])
        keep_of.append(jnp.full((1, heads), 1.0, f32) * keeps[b])
    total[...] = decay_of[0] * decay_of[1]
    one = jnp.ones((1, heads), f32)
    kinds = (keep_of, (one, decay_of[0]), (decay_of[1], one), (one, 0.0 * one), (0.0 * one, one))
    for s in range(blocks):
        def mine(pair):
            return jnp.where(turned, pair[1 - s], pair[s])

        for kind, pair in enumerate(kinds):
            coefs[kind, s : s + 1, :] = mine(pair)
        g = mine(rows_of)
        column = exact(g, eye, ((0,), (0,)))
        up, down = jnp.exp(column), jnp.exp(mine(ends_of) - column)
        at = slice(s * BLOCK, (s + 1) * BLOCK)
        for n in range(narrow):
            group = slice(n * hn, (n + 1) * hn)
            gcol[n, at, :] = column[:, group]
            rise[n, at, :] = up[:, group]
            tail[n, at, :] = down[:, group]
            grow[s * narrow + n] = g[group, :]


def forward_kernel(hn, hd, share, own, tok_a, tok_b, wq, wk, wv, wg, live, gcol, grow, tail, *refs):
    n1, tok, ql, kl, q, k, v, act, intra, contrib = refs[-10:]
    i = pl.program_id(0)

    @pl.when(i == 0)
    def _():
        for part, source in enumerate((tok_a, tok_b)):
            at = slice(part * share, (part + 1) * share)
            tok[at, :] = source[...]
            values = source[...].astype(f32)
            n1[at, :] = (values * inv_rms(values)).astype(bf16)

    normed = n1[...]
    q_lin = mm(normed, wq[...])
    k_lin = mm(normed, wk[...])

    @pl.when(i == own[1])
    def _():
        ql[...] = q_lin
        kl[...] = k_lin

    q[...] = (q_lin * sigmoid(q_lin)).astype(bf16)
    k[...] = (k_lin * sigmoid(k_lin) * live[...]).astype(bf16)
    v[...] = mm(normed, wv[...]).astype(bf16)
    act[...] = sigmoid(mm(normed, wg[...]))
    causal = causal_of(BLOCK, flip_of(own, share))
    for h in range(hn):
        at = slice(h * hd, (h + 1) * hd)
        qh, kh, vh = q[:, at], k[:, at], v[:, at]
        weights = decay_weights(causal, gcol[0, :, h : h + 1], grow[0, h : h + 1, :])
        scores = (mt(qh, kh) * weights).astype(bf16)
        intra[:, at] = mm(scores, vh)
        key_tail = (kh.astype(f32) * tail[0, :, h : h + 1]).astype(bf16)
        contrib[0, h] = tm(key_tail, vh)


def out_kernel(heads, hn, hd, share, own, coefs, *refs):
    narrow = heads // hn
    states = refs[:narrow]
    contrib, q, intra, act, tok, rise, wo, att, inverse, gated, hidden, n2, kent = refs[narrow:]
    b = pl.program_id(0)
    for h in range(heads):
        at = slice(h * hd, (h + 1) * hd)
        part = own[1] ^ (h // hn)
        base = states[0][h % hn].astype(f32)
        for j in range(1, narrow):
            base = jnp.where(part == j, states[j][h % hn].astype(f32), base)
        entering = coefs[ENTER, b, h] * base + coefs[SECOND, b, h] * contrib[1 - b, h]
        kept = (coefs[KEEP, b, h] * entering).astype(bf16)

        @pl.when(part == 0)
        def _():
            kent[0, h % hn] = kept

        att[:, at] = (intra[:, at] + rise[h // hn, :, h % hn : h % hn + 1] * mm(q[:, at], kept)).astype(bf16)
    values = att[...].astype(f32)
    scale = inv_rms(values)
    inverse[...] = scale
    gated[...] = (values * scale * act[...]).astype(bf16)
    hid = tok[...].astype(f32) + mm(gated[...], wo[...])

    @pl.when(b == 0)
    def _():
        hidden[...] = hid[:share]

    n2[...] = (hid * inv_rms(hid)).astype(bf16)


def ffn_kernel(share, n2, cot, w1, w2, w3, product, gf, gs, *pieces):
    normed = n2[...]
    first = mt(normed, w1[...])
    second = mt(normed, w2[...])
    product[...] = (first * second).astype(bf16)
    grad = mt(cot[...], w3[...])
    gf[...] = (grad * second).astype(bf16)
    gs[...] = (grad * first).astype(bf16)
    back = (mm(gf[...], w1[...]) + mm(gs[...], w2[...])).astype(bf16)
    for i, piece in enumerate(pieces):
        piece[...] = back[i * share : (i + 1) * share]


def reversed_bits(value, count):
    out = 0
    for i in range(count):
        out = out | (((value >> i) & 1) << (count - 1 - i))
    return out


def position(offset, parity, wide):
    bits = (wide - 1).bit_length() - 1
    high = offset >> 1
    return jnp.where(parity == 0, reversed_bits(high, bits), high)


def scatter(wide, own, kept, sent, item, piece_of):
    for t in range(wide):
        offset = own[0] ^ t
        parity = own[0] & 1

        @pl.when(offset & 1 == 0)
        def _():
            kept[position(offset, parity, wide), item] = piece_of(t).astype(bf16)

        @pl.when(offset & 1 == 1)
        def _():
            sent[position(offset, 1 - parity, wide), item] = piece_of(t).astype(bf16)


def ffn_cut(wide, ff, width):
    across = min(wide, width // 128)
    return ff // (wide // across), width // across, across


def ffn_grad_kernel(wide, share, own, n2, cot, product, gf, gs, w3, kept, sent, *refs):
    pieces, acc = refs[:-1], refs[-1]
    item = pl.program_id(0)
    for i, (left, right) in enumerate(((gf, n2), (gs, n2), (product, cot))):
        @pl.when(item == i)
        def _():
            acc[...] = tm(left[...], right[...])

    tall, cols, across = ffn_cut(wide, *acc.shape)

    def piece_of(t):
        row, col = t // across * tall, t % across * cols
        return acc[row : row + tall, col : col + cols]

    scatter(wide, own, kept, sent, 0, piece_of)

    @pl.when(item == 2)
    def _():
        for i, piece in enumerate(pieces):
            piece[...] = mm(product[i * share : (i + 1) * share, :], w3[...]).astype(bf16)


def residual_kernel(narrow, own, *refs):
    parts = refs[:narrow]
    hidden, cot, wo, att, inverse, act, grad_hidden, ggl = refs[narrow : narrow + 8]
    trios = refs[narrow + 8 :]
    gn2 = parts[0][...].astype(f32)
    for part in parts[1:]:
        gn2 = gn2 + part[...].astype(f32)
    hid = hidden[...]
    gh = cot[...].astype(f32) + rms_back(hid, inv_rms(hid), gn2)
    grad_hidden[...] = gh
    low = gh.astype(bf16)
    gg = mt(low, wo[...])
    values = att[...].astype(f32)
    gate = act[...]
    ggl[...] = (gg * (values * inverse[...]) * gate * (1.0 - gate)).astype(bf16)
    back = rms_back(values, inverse[...], gg * gate).astype(bf16)
    size = back.shape[1] // narrow
    for i in range(narrow):
        for k in range(narrow):
            @pl.when(own[1] ^ i == k)
            def _():
                at = slice(i * size, (i + 1) * size)
                trios[k][:, :size] = back[:, at]
                trios[k][:, size : 2 * size] = ggl[:, at]
                trios[k][:, 2 * size :] = low[:, at]


def query_kernel(hn, hd, share, own, coefs, *refs):
    per = BLOCK // share
    ga = refs[: -14]
    q, k, v, ql, kent, gcol, grow, rise, dq, gk, gv, direct, first, grad = refs[-14:]
    b = pl.program_id(0)
    for i, piece in enumerate(ga):
        @pl.when(b == i // per)
        def _():
            grad[(i % per) * share : (i % per + 1) * share, :] = piece[:, : grad.shape[1]]

    causal = causal_of(BLOCK, flip_of(own, share))
    for h in range(hn):
        at = slice(h * hd, (h + 1) * hd)
        g, qh, kh, vh = grad[:, at], q[:, at], k[:, at], v[:, at]
        weights = decay_weights(causal, gcol[:, h : h + 1], grow[0, h : h + 1, :])
        scores = (mt(qh, kh) * weights).astype(bf16)
        raw = (mt(g, vh) * weights).astype(bf16)
        up = rise[:, h : h + 1]
        gq = mm(raw, kh) + up * mt(g, kent[0, h])
        dq[:, at] = (gq * slope(ql[:, at])).astype(bf16)
        gk[:, at] = tm(raw, qh)
        gv[:, at] = tm(scores, g)
        head = own[1] * hn + h
        now = coefs[KEEP, b, head] * tm((qh.astype(f32) * up).astype(bf16), g)
        direct[0, h] = now

        @pl.when(b == 0)
        def _():
            first[h] = coefs[ENTER, b, head] * now

        @pl.when(b > 0)
        def _():
            first[h] += coefs[ENTER, b, head] * now


def key_kernel(hn, hd, wide, share, own, coefs, arrived, direct, n1, dq, k, v, kl, gk, gv,
               tail, live, _kept, _sent, kept, sent, *refs):
    pieces = refs[:-5]
    dk, dv, aq, ak, av = refs[-5:]
    per = BLOCK // share
    b = pl.program_id(0)
    last = pl.num_programs(0) - 1
    for h in range(hn):
        at = slice(h * hd, (h + 1) * hd)
        head = own[1] * hn + h
        low = (coefs[ENDS, b, head] * arrived[h] + coefs[FIRST, b, head] * direct[1 - b, h]).astype(bf16)
        down = tail[:, h : h + 1]
        grad_key = gk[:, at] + down * mt(v[:, at], low)
        dk[:, at] = (grad_key * live[...] * slope(kl[:, at])).astype(bf16)
        dv[:, at] = (gv[:, at] + down * mm(k[:, at], low)).astype(bf16)
    normed = n1[...]
    tall = normed.shape[1] // wide
    for item, (acc, part) in enumerate(((aq, dq), (ak, dk), (av, dv))):
        now = tm(normed, part[...])

        @pl.when(b == 0)
        def _():
            acc[...] = now

        @pl.when(b > 0)
        def _():
            acc[...] += now

        @pl.when(b == last)
        def _():
            scatter(wide, own, kept, sent, item, lambda t: acc[t * tall : (t + 1) * tall, :])

    cols = dq.shape[1]
    for i, piece in enumerate(pieces):
        @pl.when(b == i // per)
        def _():
            for item, part in enumerate((dq, dk, dv)):
                piece[:, item * cols : (item + 1) * cols] = part[(i % per) * share : (i % per + 1) * share, :]


def gate_kernel(wide, share, own, *refs):
    trios = refs[:-6]
    n1, gated, kept, sent, grads, acc = refs[-6:]
    item = pl.program_id(0)
    cols = acc.shape[1]
    tall = acc.shape[0] // wide
    for step, left in enumerate((n1, gated)):
        @pl.when(item == step)
        def _():
            at = slice((step + 1) * cols, (step + 2) * cols)
            for i, piece in enumerate(trios):
                grads[i * share : (i + 1) * share, :] = piece[:, at]
            acc[...] = tm(left[...], grads[...])

    scatter(wide, own, kept, sent, 0, lambda t: acc[t * tall : (t + 1) * tall, :])


def tokens_kernel(narrow, own, *refs):
    parts = refs[:narrow]
    ggl, wq, wk, wv, wg, tok, gh, out, *grads = refs[narrow:]
    cols = parts[0].shape[1] // 3
    for i in range(narrow):
        for k in range(narrow):
            @pl.when(own[1] ^ i == k)
            def _():
                for item, full in enumerate(grads):
                    full[:, i * cols : (i + 1) * cols] = parts[k][:, item * cols : (item + 1) * cols]

    grad = mt(ggl[...], wg[...])
    for full, weight in zip(grads, (wq, wk, wv)):
        grad = grad + mt(full[...], weight[...])
    values = tok[...].astype(f32)
    out[...] = gh[...] + rms_back(values, inv_rms(values), grad)


def output_kernel(narrow, *refs):
    hidden, out = refs[narrow:]
    total = hidden[...]
    for part in refs[:narrow]:
        total = total + part[...].astype(f32)
    out[...] = total.astype(bf16)


def swap_narrow(values, k):
    size = lax.axis_size("narrow")
    return lax.ppermute(values, "narrow", [(i, i ^ k) for i in range(size)])


def gather_narrow(values):
    return [values] + [swap_narrow(values, k) for k in range(1, lax.axis_size("narrow"))]


def trade_narrow(pieces):
    return [pieces[0]] + [swap_narrow(pieces[k], k) for k in range(1, len(pieces))]


def swap_core(values):
    size = lax.axis_size("wide")
    return lax.ppermute(values, "wide", [(i, i ^ 1) for i in range(size)])


def swap_step(values, step):
    size = lax.axis_size("wide")
    bits = (size - 1).bit_length()
    flip = lambda i: i ^ (1 << (1 + step if i % 2 == 0 else bits - 1 - step))
    return lax.ppermute(values, "wide", [(i, flip(i)) for i in range(size)])


def fence(*values):
    return lax.optimization_barrier(values)


def halved(low, high):
    half = low.shape[0] // 2
    return low[:half] + high[:half], low[half:] + high[half:]


def swap_all(parts, step):
    return [swap_step(part, step) for part in parts]


def swap_cores(parts):
    return [swap_core(part) for part in parts]


def target(own, place, other, wide):
    bits = (wide - 1).bit_length() - 1
    parity = (own[0] & 1) ^ other
    high = jnp.where(parity == 0, reversed_bits(place, bits), place)
    return own[0] ^ other ^ (2 * high)


def widen_square_kernel(count, narrow, places, own, *refs):
    pieces, outs = refs[:places], refs[-count:]
    for j, piece in enumerate(pieces):
        @pl.when(pl.program_id(0) == j)
        def _():
            cols = piece.shape[-1]
            for item in range(count):
                for n in range(narrow):
                    outs[item][:, n * cols : (n + 1) * cols] = piece[own[1] ^ n, item].astype(f32)


def widen_ffn_kernel(places, own, *refs):
    pieces, outs = refs[:places], refs[-3:]
    for j, piece in enumerate(pieces):
        @pl.when(pl.program_id(0) == j)
        def _():
            for item in range(3):
                outs[item][...] = piece[item].astype(f32)


def widen(kernel, own, other, first, total, pieces, block, cut, shape, outs, count, name):
    places = len(pieces)
    spec = pl.BlockSpec(block, lambda i, own: cut(target(own, first + i, other, 2 * total)))
    return pl.pallas_call(
        functools.partial(kernel, places),
        grid_spec=pltpu.PrefetchScalarGridSpec(
            num_scalar_prefetch=1,
            grid=(places,),
            in_specs=[whole(p.shape) for p in pieces] + [ANY] * len(outs),
            out_specs=[spec] * count,
        ),
        out_shape=[sds(shape, f32)] * count,
        input_output_aliases={1 + places + i: i for i in range(len(outs))},
        compiler_params=PARAMS,
        cost_estimate=cost(4),
        name=f"{name}_{other}",
    )(own, *pieces, *outs)


def xor_order(values, own, axis):
    count = values.shape[axis]
    for bit in range((count - 1).bit_length()):
        step = 1 << bit
        shape = values.shape
        split = values.reshape(shape[:axis] + (count // (2 * step), 2, step) + shape[axis + 1 :])
        flipped = jnp.flip(split, axis + 1)
        values = jnp.where((own >> bit) & 1 == 1, flipped, split).reshape(shape)
    return values


def gather_factors(values):
    size, own = lax.axis_size("wide"), lax.axis_index("wide")
    full = values[None]
    for bit in range((size - 1).bit_length()):
        got = lax.ppermute(full, "wide", [(i, i ^ (1 << bit)) for i in range(size)])
        full = jnp.concatenate([full, got], axis=0)
    return xor_order(full, own, 0)


def between(factors, own, before):
    count = factors.shape[0]
    j = jnp.arange(count)[:, None]
    i = jnp.arange(count)[None, :]
    if before:
        inner, wanted = (i > j) & (i < own), j[:, 0] < own
    else:
        inner, wanted = (i < j) & (i > own), j[:, 0] > own
    terms = jnp.where(inner[:, :, None], factors[None], 1.0)
    return jnp.where(wanted[:, None], jnp.prod(terms, axis=1), 0.0)


def pass_states(message, coef):
    gathered = lax.all_gather(message, "wide", axis=0)
    return jnp.sum(coef[:, :, None, None] * gathered.astype(f32), axis=0)


def body(tokens, log_decay, lengths, pad_counts, w_query, w_key, w_value, w_gate, w_out,
         w_first, w_second, w_third, cotangent):
    wide, narrow = lax.axis_size("wide"), lax.axis_size("narrow")
    own_wide, own_narrow = lax.axis_index("wide"), lax.axis_index("narrow")
    heads, local = log_decay.shape
    share, width = tokens.shape
    hn, cols, hd = heads // narrow, width // narrow, width // heads
    blocks, per = local // BLOCK, BLOCK // share
    own = jnp.stack([own_wide, own_narrow]).astype(jnp.int32)

    tok = gather_narrow(tokens)

    columns = sds((narrow, local, hn), f32)
    gcol, rise, tail, grow, live, coefs, total = pl.pallas_call(
        functools.partial(layout_kernel, narrow, share),
        in_specs=[SMEM, SMEM, SMEM, pl.BlockSpec(memory_space=pltpu.VMEM)],
        out_shape=[columns, columns, columns, sds((blocks * narrow, hn, BLOCK), f32), sds((local, 1), f32),
                   sds((5, blocks, heads), f32), sds((1, heads), f32)],
        cost_estimate=cost(3),
        name="layout",
    )(own, lengths, pad_counts, log_decay)

    def own_heads(values):
        return lax.dynamic_slice_in_dim(values, own_narrow * hn, hn, 1)

    shapes = [sds((local, width), bf16), sds((local, width), bf16), *[sds((local, cols), f32)] * 2,
              *[sds((local, width), bf16)] * 3, *[sds((local, width), f32)] * 2,
              sds((blocks, heads, hd, hd), f32)]
    made = []
    for s in range(blocks):
        if s == 1:
            made, later, cotangent_now, product_now = fence(made, tok[per:], cotangent, total)
            tok = tok[:per] + list(later)
        weight = pl.BlockSpec((width, cols), lambda i, own: (0, i))
        column = pl.BlockSpec((1, BLOCK, hn), lambda i, own, s=s: (i, s, 0))
        full = pl.BlockSpec((BLOCK, width), lambda i, own, s=s: (s, 0))
        mine = pl.BlockSpec((BLOCK, cols), lambda i, own, s=s: (s, 0))
        part = pl.BlockSpec((BLOCK, cols), lambda i, own, s=s: (s, i))
        made = pl.pallas_call(
            functools.partial(forward_kernel, hn, hd, share),
            grid_spec=pltpu.PrefetchScalarGridSpec(
                num_scalar_prefetch=1,
                grid=(narrow,),
                in_specs=[*[whole((share, width))] * 2, *[weight] * 4,
                          pl.BlockSpec((BLOCK, 1), lambda i, own, s=s: (s, 0)), column,
                          pl.BlockSpec((1, hn, BLOCK), lambda i, own, s=s: (s * narrow + i, 0, 0)),
                          column, *[ANY] * len(made)],
                out_specs=[full, full, mine, mine, *[part] * 5,
                           pl.BlockSpec((1, hn, hd, hd), lambda i, own, s=s: (s, i, 0, 0))],
            ),
            out_shape=shapes,
            input_output_aliases={11 + i: i for i in range(len(made))},
            compiler_params=PARAMS,
            cost_estimate=cost(10),
            name=f"mixer_forward_{s}",
        )(own, tok[per * s], tok[per * s + 1], w_query, w_key, w_value, w_gate, live, gcol, grow, tail, *made)
    n1, tok_all, ql, kl, q, k, v, act, intra, contrib = made

    cot = gather_narrow(cotangent_now)
    factors = gather_factors(product_now[0])
    factors = lax.dynamic_slice_in_dim(factors, own_narrow * hn, hn, 1)
    coef_in, coef_out = between(factors, own_wide, True), between(factors, own_wide, False)
    message = own_heads(contrib)
    message = jnp.sum(own_heads(coefs[ENDS])[:, :, None, None] * message, axis=0).astype(bf16)
    entering, cot = fence(pass_states(message, coef_in).astype(bf16), cot)
    cot_all = jnp.concatenate(cot, axis=0)
    states = gather_narrow(entering)

    up = lambda b: b
    all_blk, part_blk = rows((BLOCK, width), up), rows((BLOCK, cols), up)
    own_blk = pl.BlockSpec((BLOCK, cols), lambda b, own: (b, own[1]))
    own_kent = rows((1, hn, hd, hd), up)
    att, inverse, gated, hidden, n2, kent = pl.pallas_call(
        functools.partial(out_kernel, heads, hn, hd, share),
        grid_spec=pltpu.PrefetchScalarGridSpec(
            num_scalar_prefetch=1,
            grid=(blocks,),
            in_specs=[SMEM, *[whole((hn, hd, hd))] * narrow, whole((blocks, heads, hd, hd)),
                      *[all_blk] * 4, pl.BlockSpec((narrow, BLOCK, hn), lambda b, own: (0, b, 0)),
                      whole((width, width))],
            out_specs=[all_blk, rows((BLOCK, 1), up), all_blk, whole((share, width)), all_blk, own_kent],
        ),
        out_shape=[sds((local, width), bf16), sds((local, 1), f32), sds((local, width), bf16), sds((share, width), f32),
                   sds((local, width), bf16), sds((blocks, hn, hd, hd), bf16)],
        compiler_params=PARAMS,
        cost_estimate=cost(9.5),
        name="mixer_out",
    )(own, coefs, *states, contrib, q, intra, act, tok_all, rise, w_out)

    ff = w_first.shape[1]
    first_t, second_t = w_first.T, w_second.T
    ff_blk = rows((BLOCK, ff), up)
    piece_spec, piece_shape = whole((share, width)), sds((share, width), bf16)
    product, gf, gs, *gn2 = pl.pallas_call(
        functools.partial(ffn_kernel, share),
        out_shape=[*[sds((local, ff), bf16)] * 3, *[piece_shape] * narrow],
        compiler_params=pltpu.CompilerParams(vmem_limit_bytes=56 << 20),
        cost_estimate=cost(10),
        name="ffn",
    )(n2, cot_all, first_t, second_t, w_third)

    gn2 = trade_narrow(gn2)
    product_now, _ = fence(product, gn2[1])
    tall, across = ffn_cut(wide, ff, width)[:2]
    slot = (wide // 2, 3, tall, across)
    slot_spec = pl.BlockSpec((wide // 2, 1, tall, across), lambda i, own: (0, i, 0, 0))
    kept, sent, *ffn_part = pl.pallas_call(
        functools.partial(ffn_grad_kernel, wide, share),
        grid_spec=pltpu.PrefetchScalarGridSpec(
            num_scalar_prefetch=1,
            grid=(3,),
            in_specs=[*[whole((local, width))] * 2, *[whole((local, ff))] * 3, whole((ff, width))],
            out_specs=[slot_spec, slot_spec, *[piece_spec] * narrow],
            scratch_shapes=[pltpu.VMEM((ff, width), f32)],
        ),
        out_shape=[sds(slot, bf16), sds(slot, bf16), *[piece_shape] * narrow],
        compiler_params=PARAMS,
        cost_estimate=cost(10),
        name="ffn_grads",
    )(own, n2, cot_all, product_now, gf, gs, w_third)
    gn2, kept, sent = fence(gn2, kept, sent)
    steps = (wide - 1).bit_length() - 1

    def single(shape, index=None):
        where = index or (lambda own: (0,) * len(shape))
        return pl.BlockSpec(shape, lambda b, own: where(own))

    row_spec = single((share, width))
    grad_hidden, ggl, *trios = pl.pallas_call(
        functools.partial(residual_kernel, narrow),
        grid_spec=pltpu.PrefetchScalarGridSpec(
            num_scalar_prefetch=1,
            grid=(1,),
            in_specs=[*[row_spec] * (narrow + 2), single((width, width)), row_spec, single((share, 1)), row_spec],
            out_specs=[row_spec] * 2 + [single((share, 3 * cols))] * narrow,
        ),
        out_shape=[sds((share, width), f32), sds((share, width), bf16),
                   *[sds((share, 3 * cols), bf16)] * narrow],
        compiler_params=PARAMS,
        cost_estimate=cost(5),
        name="residual_back",
    )(own, *gn2, hidden, cotangent, w_out, att, inverse, act)
    trios, kept, sent = fence(trios, kept, sent)
    trios, kept, got, ffn_part = fence(trade_narrow(trios), kept, swap_core(sent), ffn_part)
    low, away = halved(kept, got)
    got = swap_step(away, 0)

    own_col = pl.BlockSpec((None, BLOCK, hn), lambda b, own: (own[1], b, 0))
    own_row = pl.BlockSpec((1, hn, BLOCK), lambda b, own: (b * narrow + own[1], 0, 0))
    dq, gk, gv, direct, message = pl.pallas_call(
        functools.partial(query_kernel, hn, hd, share),
        grid_spec=pltpu.PrefetchScalarGridSpec(
            num_scalar_prefetch=1,
            grid=(blocks,),
            in_specs=[SMEM, *[whole((share, 3 * cols))] * narrow, *[own_blk] * 3, part_blk, own_kent,
                      own_col, own_row, own_col],
            out_specs=[*[part_blk] * 3, own_kent, whole((hn, hd, hd))],
            scratch_shapes=[pltpu.VMEM((BLOCK, cols), bf16)],
        ),
        out_shape=[sds((local, cols), bf16), *[sds((local, cols), f32)] * 2,
                   sds((blocks, hn, hd, hd), f32), sds((hn, hd, hd), f32)],
        compiler_params=PARAMS,
        cost_estimate=cost(5.4),
        name="mixer_query_back",
    )(own, coefs, *trios, q, k, v, ql, kent, gcol, grow, rise)

    part_two = swap_narrow(ffn_part[2], 2)
    arrived, low, got, part_two = fence(pass_states(message.astype(bf16), coef_out), low, got, part_two)
    low_ff, away_ff = halved(low, got)

    five = (wide // 2, 5, width // wide, cols)
    one = pl.BlockSpec((wide // 2, 1, width // wide, cols), lambda i, own: (0, 3 + i, 0, 0))
    kept, sent = pl.pallas_call(
        functools.partial(gate_kernel, wide, share),
        grid_spec=pltpu.PrefetchScalarGridSpec(
            num_scalar_prefetch=1,
            grid=(2,),
            in_specs=[*[single((share, 3 * cols))] * narrow, *[single((local, width))] * 2],
            out_specs=[one] * 2,
            scratch_shapes=[pltpu.VMEM((local, cols), bf16), pltpu.VMEM((width, cols), f32)],
        ),
        out_shape=[sds(five, bf16)] * 2,
        compiler_params=PARAMS,
        cost_estimate=cost(5),
        name="gate_back",
    )(own, *trios, n1, gated)
    three = whole((wide // 2, 3, width // wide, cols))
    trio_spec, trio_shape = whole((share, 3 * cols)), sds((share, 3 * cols), bf16)
    kept, sent, *dqkv = pl.pallas_call(
        functools.partial(key_kernel, hn, hd, wide, share),
        grid_spec=pltpu.PrefetchScalarGridSpec(
            num_scalar_prefetch=1,
            grid=(blocks,),
            in_specs=[SMEM, whole((hn, hd, hd)), whole((blocks, hn, hd, hd)), all_blk, part_blk,
                      own_blk, own_blk, *[part_blk] * 3, own_col, rows((BLOCK, 1), up), ANY, ANY],
            out_specs=[three, three, *[trio_spec] * narrow],
            scratch_shapes=[*[pltpu.VMEM((BLOCK, cols), bf16)] * 2, *[pltpu.VMEM((width, cols), f32)] * 3],
        ),
        out_shape=[*[sds(five, bf16)] * 2, *[trio_shape] * narrow],
        input_output_aliases={13: 0, 14: 1},
        compiler_params=PARAMS,
        cost_estimate=cost(9),
        name="mixer_key_back",
    )(own, coefs, arrived, direct, n1, dq, k, v, kl, gk, gv, tail, live, kept, sent)

    low, away = halved(kept, swap_core(sent))
    low, away, dqkv, away_ff = fence(low, away, dqkv, away_ff)
    low, high, dqkv, high_ff = fence(low, swap_step(away, 0), trade_narrow(dqkv), swap_step(away_ff, 1))
    for step in range(1, steps):
        low, away = halved(low, high)
        high = swap_step(away, step)
    for step in range(2, steps):
        low_ff, away_ff = halved(low_ff, high_ff)
        high_ff = swap_step(away_ff, step)
    piece = (low + high)[0]
    ff_piece = [(low_ff + high_ff)[0]]

    for step in reversed(range(1, steps)):
        ff_first = len(ff_piece)
        ff_piece = ff_piece + swap_all(ff_piece, step)
    ff_more = swap_all(ff_piece[:ff_first], 0)
    gate_piece, piece, ff_piece, ff_more = fence(
        jnp.stack(gather_narrow(piece[3:])), piece[:3], ff_piece, ff_more
    )
    chunks = width // across
    ffn_form = (tall, across), lambda t: (t // chunks, t % chunks), (ff, width)
    square_form = (width // wide, width), lambda t: (t, 0), (width, width)
    gate_kernels = functools.partial(widen_square_kernel, 2, narrow)
    square_kernels = functools.partial(widen_square_kernel, 3, narrow)

    zs = gather_narrow(piece)
    ff_piece = ff_piece + ff_more + swap_all(ff_piece[ff_first:], 0)
    gate_piece = [gate_piece]
    for step in reversed(range(1, steps)):
        gate_piece = gate_piece + swap_all(gate_piece, step)
    half = len(gate_piece) // 2
    gate_more = swap_all(gate_piece, 0)
    dqkv, _ = fence(dqkv, zs[1])
    grad_tokens = pl.pallas_call(
        functools.partial(tokens_kernel, narrow),
        grid_spec=pltpu.PrefetchScalarGridSpec(
            num_scalar_prefetch=1,
            grid=(1,),
            in_specs=[*[single((share, 3 * cols))] * narrow, row_spec, *[single((width, width))] * 4,
                      row_spec, row_spec],
            out_specs=row_spec,
            scratch_shapes=[pltpu.VMEM((share, width), bf16)] * 3,
        ),
        out_shape=sds((share, width), f32),
        compiler_params=PARAMS,
        cost_estimate=cost(8),
        name="tokens_back",
    )(own, *dqkv, ggl, w_query, w_key, w_value, w_gate, tokens, grad_hidden)
    square_piece, gate_piece, ff_piece, ffn_part, grad_tokens = fence(
        jnp.stack(zs), gate_piece + gate_more, ff_piece, ffn_part, grad_tokens
    )

    square_piece = [square_piece]
    for step in reversed(range(1, steps)):
        square_piece = square_piece + swap_all(square_piece, step)
    square_piece = square_piece + swap_all(square_piece[:half], 0)
    places = wide // 2
    ffn_out = widen(widen_ffn_kernel, own, 0, 0, places, ff_piece, *ffn_form, [], 3, "widen_ffn")
    gate_out = widen(gate_kernels, own, 0, 0, places, gate_piece, *square_form, [], 2, "widen_gate")
    ff_other = swap_cores(ff_piece)
    ffn_out = widen(widen_ffn_kernel, own, 1, 0, places, ff_other, *ffn_form, ffn_out, 3, "widen_ffn")
    square_piece, ffn_out, gate_out, gate_other, ffn_part = fence(
        square_piece, ffn_out, gate_out, swap_cores(gate_piece), ffn_part
    )

    part_three, part_one = swap_narrow(ffn_part[3], 3), swap_narrow(ffn_part[1], 1)
    square_last = swap_all(square_piece[half : places // 2], 0)
    done = len(square_piece)
    gate_out = widen(gate_kernels, own, 1, 0, places, gate_other, *square_form, gate_out, 2, "widen_gate")
    mixer = widen(square_kernels, own, 0, 0, places, square_piece, *square_form, [], 3, "widen_square")
    square_last, gate_out, mixer, square_piece, part_three, part_one = fence(
        square_last, gate_out, mixer, square_piece, part_three, part_one
    )

    output = pl.pallas_call(
        functools.partial(output_kernel, narrow),
        out_shape=sds((share, width), bf16),
        compiler_params=pltpu.CompilerParams(vmem_limit_bytes=56 << 20),
        cost_estimate=cost(2),
        name="output",
    )(ffn_part[0], part_one, part_two, part_three, hidden)
    mixer = widen(square_kernels, own, 0, done, places, square_last, *square_form, mixer, 3, "widen_last")
    square_other = swap_cores(square_piece + square_last)
    mixer = widen(square_kernels, own, 1, 0, places, square_other, *square_form, mixer, 3, "widen_square")
    grad_first, grad_second, grad_third = ffn_out
    grad_gate, grad_out = gate_out
    return (output, grad_tokens, *mixer, grad_gate, grad_out, grad_first.T, grad_second.T, grad_third)


def solution(mesh):
    both = P(("wide", "narrow"), None)
    in_specs = (both, P(None, "wide"), P(), P(), P(), P(), P(), P(), P(),
                P(None, "narrow"), P(None, "narrow"), P("narrow", None), both)
    out_specs = (both, both, P(), P(), P(), P(), P(),
                 P(None, "narrow"), P(None, "narrow"), P("narrow", None))
    return jax.shard_map(body, mesh=mesh, in_specs=in_specs, out_specs=out_specs, check_vma=False)
```

```python
import functools

import jax
import jax.numpy as jnp
from jax import lax
from jax.experimental import pallas as pl
from jax.experimental.pallas import tpu as pltpu
from jax.sharding import PartitionSpec as P

BLOCK = 256
epsilon = 1e-06
bf16 = jnp.bfloat16
f32 = jnp.float32
SMEM = pl.BlockSpec(memory_space=pltpu.SMEM)
ANY = pl.BlockSpec(memory_space=pl.ANY)
sds = jax.ShapeDtypeStruct


def budget(mebibytes):
    return pltpu.CompilerParams(vmem_limit_bytes=mebibytes << 20)


def cost(micros):
    return pl.CostEstimate(flops=0, transcendentals=0, bytes_accessed=int(micros * 3.2e6))


def mm(a, b):
    return lax.dot_general(a, b, (((1,), (0,)), ((), ())), preferred_element_type=f32)


def mt(a, b):
    return lax.dot_general(a, b, (((1,), (1,)), ((), ())), preferred_element_type=f32)


def tm(a, b):
    return lax.dot_general(a, b, (((0,), (0,)), ((), ())), preferred_element_type=f32)


def inv_rms(values):
    return lax.rsqrt(jnp.mean(values * values, axis=-1, keepdims=True) + epsilon)


def sigmoid(values):
    return 0.5 * jnp.tanh(0.5 * values) + 0.5


def slope(values):
    squashed = sigmoid(values)
    return squashed * (1.0 + values * (1.0 - squashed))


def rms_back(values, inverse, gradient):
    normed = values * inverse
    return inverse * (gradient - normed * jnp.mean(gradient * normed, axis=-1, keepdims=True))


def whole(shape):
    zeros = (0,) * len(shape)
    return pl.BlockSpec(shape, lambda *_: zeros)


def rows(shape, index):
    rest = (0,) * (len(shape) - 1)
    return pl.BlockSpec(shape, lambda b, *_: (index(b), *rest))


def causal_of(size, flip):
    return (lax.broadcasted_iota(jnp.int32, (size, size), 0) ^ flip) >= (
        lax.broadcasted_iota(jnp.int32, (size, size), 1) ^ flip
    )


def decay_weights(causal, g_col, g_row):
    return jnp.exp(jnp.where(causal, g_col - g_row, -1e30))


def flip_of(own, share):
    return share * (own[1] & (BLOCK // share - 1))


def exact(a, b, dims):
    return lax.dot_general(a, b, (dims, ((), ())), precision=lax.Precision.HIGHEST, preferred_element_type=f32)


KEEP, ENTER, ENDS, FIRST, SECOND = range(5)


def layout_kernel(narrow, share, own, lengths, pads, log_decay, gcol, rise, tail, grow, live, coefs, total):
    heads, local = log_decay.shape
    hn = heads // narrow
    per, blocks = BLOCK // share, local // BLOCK
    base = own[0] * local
    place = lax.broadcasted_iota(jnp.int32, (local, 1), 0)
    spot = base + ((place // share) ^ own[1]) * share + place % share
    alive = jnp.zeros((local, 1), f32)
    keeps = [jnp.float32(1.0)] * blocks
    end = jnp.int32(0)
    for s in range(lengths.shape[0]):
        start, end = end, end + lengths[s]
        alive = jnp.where((spot >= start) & (spot < end - pads[s]), 1.0, alive)
        keeps = [jnp.where(start == base + b * BLOCK, 0.0, keep) for b, keep in enumerate(keeps)]
    live[...] = alive

    size = (BLOCK, BLOCK)
    upper = (lax.broadcasted_iota(jnp.int32, size, 0) <= lax.broadcasted_iota(jnp.int32, size, 1)).astype(f32)
    eye = (lax.broadcasted_iota(jnp.int32, (heads, heads), 0)
           == lax.broadcasted_iota(jnp.int32, (heads, heads), 1)).astype(f32)
    turned = own[1] // per > 0
    rows_of, ends_of, decay_of, keep_of = [], [], [], []
    for b in range(blocks):
        part = log_decay[:, b * BLOCK : (b + 1) * BLOCK]
        g = exact(part, upper, ((1,), (0,)))
        for bit in range((per - 1).bit_length()):
            step = share << bit
            flipped = [g[:, (i ^ 1) * step : ((i ^ 1) + 1) * step] for i in range(BLOCK // step)]
            g = jnp.where((own[1] >> bit) & 1 == 1, jnp.concatenate(flipped, axis=1), g)
        end_row = exact(jnp.ones_like(part), part, ((1,), (1,)))[0:1]
        rows_of.append(g)
        ends_of.append(end_row)
        decay_of.append(jnp.exp(end_row) * keeps[b])
        keep_of.append(jnp.full((1, heads), 1.0, f32) * keeps[b])
    total[...] = decay_of[0] * decay_of[1]
    one = jnp.ones((1, heads), f32)
    kinds = (keep_of, (one, decay_of[0]), (decay_of[1], one), (one, 0.0 * one), (0.0 * one, one))
    for s in range(blocks):
        def mine(pair):
            return jnp.where(turned, pair[1 - s], pair[s])

        for kind, pair in enumerate(kinds):
            coefs[kind, s : s + 1, :] = mine(pair)
        g = mine(rows_of)
        column = exact(g, eye, ((0,), (0,)))
        up, down = jnp.exp(column), jnp.exp(mine(ends_of) - column)
        at = slice(s * BLOCK, (s + 1) * BLOCK)
        for n in range(narrow):
            group = slice(n * hn, (n + 1) * hn)
            gcol[n, at, :] = column[:, group]
            rise[n, at, :] = up[:, group]
            tail[n, at, :] = down[:, group]
            grow[s * narrow + n] = g[group, :]


def forward_kernel(hn, hd, share, own, tok_a, tok_b, wq, wk, wv, wg, live, gcol, grow, tail, *refs):
    n1, tok, ql, kl, q, k, v, act, intra, contrib = refs[-10:]
    i = pl.program_id(0)

    @pl.when(i == 0)
    def _():
        for part, source in enumerate((tok_a, tok_b)):
            at = slice(part * share, (part + 1) * share)
            tok[at, :] = source[...]
            values = source[...].astype(f32)
            n1[at, :] = (values * inv_rms(values)).astype(bf16)

    normed = n1[...]
    q_lin = mm(normed, wq[...])
    k_lin = mm(normed, wk[...])

    ql[...] = q_lin
    kl[...] = k_lin
    q[...] = (q_lin * sigmoid(q_lin)).astype(bf16)
    k[...] = (k_lin * sigmoid(k_lin) * live[...]).astype(bf16)
    v[...] = mm(normed, wv[...]).astype(bf16)
    act[...] = sigmoid(mm(normed, wg[...]))
    causal = causal_of(BLOCK, flip_of(own, share))
    for h in range(hn):
        at = slice(h * hd, (h + 1) * hd)
        qh, kh, vh = q[:, at], k[:, at], v[:, at]
        weights = decay_weights(causal, gcol[0, :, h : h + 1], grow[0, h : h + 1, :])
        scores = (mt(qh, kh) * weights).astype(bf16)
        intra[:, at] = mm(scores, vh)
        key_tail = (kh.astype(f32) * tail[0, :, h : h + 1]).astype(bf16)
        contrib[0, h] = tm(key_tail, vh)


def out_kernel(heads, hn, hd, share, own, coefs, *refs):
    narrow = heads // hn
    states = refs[:narrow]
    contrib, q, intra, act, tok, rise, wo, att, inverse, gated, hidden, n2, kent = refs[narrow:]
    b = pl.program_id(0)
    for h in range(heads):
        at = slice(h * hd, (h + 1) * hd)
        part = own[1] ^ (h // hn)
        base = states[0][h % hn].astype(f32)
        for j in range(1, narrow):
            base = jnp.where(part == j, states[j][h % hn].astype(f32), base)
        entering = coefs[ENTER, b, h] * base + coefs[SECOND, b, h] * contrib[1 - b, h]
        kept = (coefs[KEEP, b, h] * entering).astype(bf16)
        kent[0, h] = kept
        att[:, at] = (intra[:, at] + rise[h // hn, :, h % hn : h % hn + 1] * mm(q[:, at], kept)).astype(bf16)
    values = att[...].astype(f32)
    scale = inv_rms(values)
    inverse[...] = scale
    gated[...] = (values * scale * act[...]).astype(bf16)
    hid = tok[...].astype(f32) + mm(gated[...], wo[...])

    @pl.when(b == 0)
    def _():
        hidden[...] = hid[:share]

    n2[...] = (hid * inv_rms(hid)).astype(bf16)


def ffn_kernel(share, n2, cot, w1, w2, w3, product, gf, gs, *pieces):
    normed = n2[...]
    first = mt(normed, w1[...])
    second = mt(normed, w2[...])
    product[...] = (first * second).astype(bf16)
    grad = mt(cot[...], w3[...])
    gf[...] = (grad * second).astype(bf16)
    gs[...] = (grad * first).astype(bf16)
    back = (mm(gf[...], w1[...]) + mm(gs[...], w2[...])).astype(bf16)
    for i, piece in enumerate(pieces):
        piece[...] = back[i * share : (i + 1) * share]


def reversed_bits(value, count):
    out = 0
    for i in range(count):
        out = out | (((value >> i) & 1) << (count - 1 - i))
    return out


def position(offset, parity, wide):
    bits = (wide - 1).bit_length() - 1
    high = offset >> 1
    return jnp.where(parity == 0, reversed_bits(high, bits), high)


def scatter(wide, own, kept, sent, item, piece_of):
    for t in range(wide):
        offset = own[0] ^ t
        parity = own[0] & 1

        @pl.when(offset & 1 == 0)
        def _():
            kept[position(offset, parity, wide), item] = piece_of(t).astype(bf16)

        @pl.when(offset & 1 == 1)
        def _():
            sent[position(offset, 1 - parity, wide), item] = piece_of(t).astype(bf16)


def ffn_cut(wide, ff, width):
    across = min(wide, width // 128)
    return ff // (wide // across), width // across, across


def ffn_grad_kernel(wide, share, own, n2, cot, product, gf, gs, w3, kept, sent, *refs):
    pieces, acc = refs[:-1], refs[-1]
    item = pl.program_id(0)
    for i, (left, right) in enumerate(((gf, n2), (gs, n2), (product, cot))):
        @pl.when(item == i)
        def _():
            acc[...] = tm(left[...], right[...])

    tall, cols, across = ffn_cut(wide, *acc.shape)

    def piece_of(t):
        row, col = t // across * tall, t % across * cols
        return acc[row : row + tall, col : col + cols]

    scatter(wide, own, kept, sent, 0, piece_of)

    @pl.when(item == 2)
    def _():
        for i, piece in enumerate(pieces):
            piece[...] = mm(product[i * share : (i + 1) * share, :], w3[...]).astype(bf16)


def residual_kernel(narrow, own, *refs):
    parts = refs[:narrow]
    hidden, cot, wo, att, inverse, act, grad_hidden, ggl = refs[narrow : narrow + 8]
    trios = refs[narrow + 8 :]
    gn2 = parts[0][...].astype(f32)
    for part in parts[1:]:
        gn2 = gn2 + part[...].astype(f32)
    hid = hidden[...]
    gh = cot[...].astype(f32) + rms_back(hid, inv_rms(hid), gn2)
    grad_hidden[...] = gh
    low = gh.astype(bf16)
    gg = mt(low, wo[...])
    values = att[...].astype(f32)
    gate = act[...]
    ggl[...] = (gg * (values * inverse[...]) * gate * (1.0 - gate)).astype(bf16)
    back = rms_back(values, inverse[...], gg * gate).astype(bf16)
    size = back.shape[1] // narrow
    for i in range(narrow):
        for k in range(narrow):
            @pl.when(own[1] ^ i == k)
            def _():
                at = slice(i * size, (i + 1) * size)
                trios[k][:, :size] = back[:, at]
                trios[k][:, size : 2 * size] = ggl[:, at]
                trios[k][:, 2 * size :] = low[:, at]


def query_kernel(hn, hd, share, own, coefs, *refs):
    per = BLOCK // share
    ga = refs[: -14]
    q, k, v, ql, kent, gcol, grow, rise, dq, gk, gv, direct, first, grad = refs[-14:]
    b = pl.program_id(0)
    for i, piece in enumerate(ga):
        @pl.when(b == i // per)
        def _():
            grad[(i % per) * share : (i % per + 1) * share, :] = piece[:, : grad.shape[1]]

    causal = causal_of(BLOCK, flip_of(own, share))
    for h in range(hn):
        at = slice(h * hd, (h + 1) * hd)
        g, qh, kh, vh = grad[:, at], q[:, at], k[:, at], v[:, at]
        weights = decay_weights(causal, gcol[:, h : h + 1], grow[0, h : h + 1, :])
        scores = (mt(qh, kh) * weights).astype(bf16)
        raw = (mt(g, vh) * weights).astype(bf16)
        up = rise[:, h : h + 1]
        gq = mm(raw, kh) + up * mt(g, kent[0, h])
        dq[:, at] = (gq * slope(ql[:, at])).astype(bf16)
        gk[:, at] = tm(raw, qh)
        gv[:, at] = tm(scores, g)
        head = own[1] * hn + h
        now = coefs[KEEP, b, head] * tm((qh.astype(f32) * up).astype(bf16), g)
        direct[0, h] = now

        first[h] = jnp.where(b == 0, 0.0, first[h]) + coefs[ENTER, b, head] * now


def key_kernel(hn, hd, wide, share, own, coefs, arrived, direct, n1, dq, k, v, kl, gk, gv,
               tail, live, _kept, _sent, kept, sent, *refs):
    pieces = refs[:-5]
    dk, dv, aq, ak, av = refs[-5:]
    per = BLOCK // share
    b = pl.program_id(0)
    last = pl.num_programs(0) - 1
    for h in range(hn):
        at = slice(h * hd, (h + 1) * hd)
        head = own[1] * hn + h
        low = (coefs[ENDS, b, head] * arrived[h] + coefs[FIRST, b, head] * direct[1 - b, h]).astype(bf16)
        down = tail[:, h : h + 1]
        grad_key = gk[:, at] + down * mt(v[:, at], low)
        dk[:, at] = (grad_key * live[...] * slope(kl[:, at])).astype(bf16)
        dv[:, at] = (gv[:, at] + down * mm(k[:, at], low)).astype(bf16)
    normed = n1[...]
    tall = normed.shape[1] // wide
    for acc, part in ((aq, dq), (ak, dk), (av, dv)):
        acc[...] = jnp.where(b == 0, 0.0, acc[...]) + tm(normed, part[...])

    for item, acc in enumerate((aq, ak, av)):
        @pl.when(b == last)
        def _():
            scatter(wide, own, kept, sent, item, lambda t: acc[t * tall : (t + 1) * tall, :])

    cols = dq.shape[1]
    for i, piece in enumerate(pieces):
        @pl.when(b == i // per)
        def _():
            for item, part in enumerate((dq, dk, dv)):
                piece[:, item * cols : (item + 1) * cols] = part[(i % per) * share : (i % per + 1) * share, :]


def gate_kernel(wide, share, own, *refs):
    trios = refs[:-6]
    n1, gated, kept, sent, grads, acc = refs[-6:]
    item = pl.program_id(0)
    cols = acc.shape[1]
    tall = acc.shape[0] // wide
    for step, left in enumerate((n1, gated)):
        @pl.when(item == step)
        def _():
            at = slice((step + 1) * cols, (step + 2) * cols)
            for i, piece in enumerate(trios):
                grads[i * share : (i + 1) * share, :] = piece[:, at]
            acc[...] = tm(left[...], grads[...])

    scatter(wide, own, kept, sent, 0, lambda t: acc[t * tall : (t + 1) * tall, :])


def tokens_kernel(narrow, own, *refs):
    parts = refs[:narrow]
    ggl, wq, wk, wv, wg, tok, gh, out, *grads, total = refs[narrow:]
    step = pl.program_id(0)
    cols = parts[0].shape[1] // 3

    @pl.when(step == 0)
    def _():
        for i in range(narrow):
            for k in range(narrow):
                @pl.when(own[1] ^ i == k)
                def _():
                    for item, full in enumerate(grads):
                        full[:, i * cols : (i + 1) * cols] = parts[k][:, item * cols : (item + 1) * cols]

    grad = mt(ggl[...], wg[...])
    for full, weight in zip(grads, (wq, wk, wv)):
        grad = grad + mt(full[...], weight[...])
    total[step] = grad

    @pl.when(step == narrow - 1)
    def _():
        grad = jnp.concatenate([total[i] for i in range(narrow)], axis=1)
        values = tok[...].astype(f32)
        out[...] = gh[...] + rms_back(values, inv_rms(values), grad)


def output_kernel(narrow, *refs):
    hidden, out = refs[narrow:]
    total = hidden[...]
    for part in refs[:narrow]:
        total = total + part[...].astype(f32)
    out[...] = total.astype(bf16)


def swap_narrow(values, k):
    size = lax.axis_size("narrow")
    return lax.ppermute(values, "narrow", [(i, i ^ k) for i in range(size)])


def gather_narrow(values):
    return [values] + [swap_narrow(values, k) for k in range(1, lax.axis_size("narrow"))]


def trade_narrow(pieces):
    return [pieces[0]] + [swap_narrow(pieces[k], k) for k in range(1, len(pieces))]


def swap_core(values):
    size = lax.axis_size("wide")
    return lax.ppermute(values, "wide", [(i, i ^ 1) for i in range(size)])


def swap_step(values, step):
    size = lax.axis_size("wide")
    bits = (size - 1).bit_length()
    flip = lambda i: i ^ (1 << (1 + step if i % 2 == 0 else bits - 1 - step))
    return lax.ppermute(values, "wide", [(i, flip(i)) for i in range(size)])


def fence(*values):
    return lax.optimization_barrier(values)


def halved(low, high):
    half = low.shape[0] // 2
    return low[:half] + high[:half], low[half:] + high[half:]


def swap_all(parts, step):
    return [swap_step(part, step) for part in parts]


def swap_cores(parts):
    return [swap_core(part) for part in parts]


def target(own, place, other, wide):
    bits = (wide - 1).bit_length() - 1
    parity = (own[0] & 1) ^ other
    high = jnp.where(parity == 0, reversed_bits(place, bits), place)
    return own[0] ^ other ^ (2 * high)


def widen_square_kernel(count, narrow, places, own, *refs):
    pieces, outs = refs[:places], refs[-count:]
    for j, piece in enumerate(pieces):
        @pl.when(pl.program_id(0) == j)
        def _():
            cols = piece.shape[-1]
            for item in range(count):
                for n in range(narrow):
                    outs[item][:, n * cols : (n + 1) * cols] = piece[own[1] ^ n, item].astype(f32)


def widen_ffn_kernel(places, own, *refs):
    pieces, outs = refs[:places], refs[-3:]
    for j, piece in enumerate(pieces):
        @pl.when(pl.program_id(0) == j)
        def _():
            for item in range(3):
                outs[item][...] = piece[item].astype(f32)


def widen(kernel, own, other, first, total, pieces, block, cut, shape, outs, count, name):
    places = len(pieces)
    spec = pl.BlockSpec(block, lambda i, own: cut(target(own, first + i, other, 2 * total)))
    return pl.pallas_call(
        functools.partial(kernel, places),
        grid_spec=pltpu.PrefetchScalarGridSpec(
            num_scalar_prefetch=1,
            grid=(places,),
            in_specs=[whole(p.shape) for p in pieces] + [ANY] * len(outs),
            out_specs=[spec] * count,
        ),
        out_shape=[sds(shape, f32)] * count,
        input_output_aliases={1 + places + i: i for i in range(len(outs))},
        compiler_params=budget(16),
        cost_estimate=cost(4),
        name=f"{name}_{other}",
    )(own, *pieces, *outs)


def xor_order(values, own, axis):
    count = values.shape[axis]
    for bit in range((count - 1).bit_length()):
        step = 1 << bit
        shape = values.shape
        split = values.reshape(shape[:axis] + (count // (2 * step), 2, step) + shape[axis + 1 :])
        flipped = jnp.flip(split, axis + 1)
        values = jnp.where((own >> bit) & 1 == 1, flipped, split).reshape(shape)
    return values


def gather_factors(values):
    size, own = lax.axis_size("wide"), lax.axis_index("wide")
    full = values[None]
    for bit in range((size - 1).bit_length()):
        got = lax.ppermute(full, "wide", [(i, i ^ (1 << bit)) for i in range(size)])
        full = jnp.concatenate([full, got], axis=0)
    return xor_order(full, own, 0)


def between(factors, own, before):
    count = factors.shape[0]
    j = jnp.arange(count)[:, None]
    i = jnp.arange(count)[None, :]
    if before:
        inner, wanted = (i > j) & (i < own), j[:, 0] < own
    else:
        inner, wanted = (i < j) & (i > own), j[:, 0] > own
    terms = jnp.where(inner[:, :, None], factors[None], 1.0)
    return jnp.where(wanted[:, None], jnp.prod(terms, axis=1), 0.0)


def pass_states(message, coef):
    gathered = lax.all_gather(message, "wide", axis=0)
    return jnp.sum(coef[:, :, None, None] * gathered.astype(f32), axis=0)


def body(tokens, log_decay, lengths, pad_counts, w_query, w_key, w_value, w_gate, w_out,
         w_first, w_second, w_third, cotangent):
    wide, narrow = lax.axis_size("wide"), lax.axis_size("narrow")
    own_wide, own_narrow = lax.axis_index("wide"), lax.axis_index("narrow")
    heads, local = log_decay.shape
    share, width = tokens.shape
    hn, cols, hd = heads // narrow, width // narrow, width // heads
    blocks, per = local // BLOCK, BLOCK // share
    own = jnp.stack([own_wide, own_narrow]).astype(jnp.int32)

    tok = gather_narrow(tokens)

    columns = sds((narrow, local, hn), f32)
    gcol, rise, tail, grow, live, coefs, total = pl.pallas_call(
        functools.partial(layout_kernel, narrow, share),
        in_specs=[SMEM, SMEM, SMEM, pl.BlockSpec(memory_space=pltpu.VMEM)],
        out_shape=[columns, columns, columns, sds((blocks * narrow, hn, BLOCK), f32), sds((local, 1), f32),
                   sds((5, blocks, heads), f32), sds((1, heads), f32)],
        compiler_params=budget(16),
        cost_estimate=cost(3),
        name="layout",
    )(own, lengths, pad_counts, log_decay)

    def own_heads(values):
        return lax.dynamic_slice_in_dim(values, own_narrow * hn, hn, 1)

    shapes = [sds((local, width), bf16), sds((local, width), bf16), *[sds((local, width), f32)] * 2,
              *[sds((local, width), bf16)] * 3, *[sds((local, width), f32)] * 2,
              sds((blocks, heads, hd, hd), f32)]
    made = []
    for s in range(blocks):
        if s == 1:
            made, later, cotangent_now, product_now = fence(made, tok[per:], cotangent, total)
            tok = tok[:per] + list(later)
        weight = pl.BlockSpec((width, cols), lambda i, own: (0, i))
        column = pl.BlockSpec((1, BLOCK, hn), lambda i, own, s=s: (i, s, 0))
        full = pl.BlockSpec((BLOCK, width), lambda i, own, s=s: (s, 0))
        part = pl.BlockSpec((BLOCK, cols), lambda i, own, s=s: (s, i))
        made = pl.pallas_call(
            functools.partial(forward_kernel, hn, hd, share),
            grid_spec=pltpu.PrefetchScalarGridSpec(
                num_scalar_prefetch=1,
                grid=(narrow,),
                in_specs=[*[whole((share, width))] * 2, *[weight] * 4,
                          pl.BlockSpec((BLOCK, 1), lambda i, own, s=s: (s, 0)), column,
                          pl.BlockSpec((1, hn, BLOCK), lambda i, own, s=s: (s * narrow + i, 0, 0)),
                          column, *[ANY] * len(made)],
                out_specs=[full, full, *[part] * 7,
                           pl.BlockSpec((1, hn, hd, hd), lambda i, own, s=s: (s, i, 0, 0))],
            ),
            out_shape=shapes,
            input_output_aliases={11 + i: i for i in range(len(made))},
            compiler_params=budget(56),
            cost_estimate=cost(10),
            name=f"mixer_forward_{s}",
        )(own, tok[per * s], tok[per * s + 1], w_query, w_key, w_value, w_gate, live, gcol, grow, tail, *made)
    n1, tok_all, ql, kl, q, k, v, act, intra, contrib = made

    cot = gather_narrow(cotangent_now)
    factors = gather_factors(product_now[0])
    factors = lax.dynamic_slice_in_dim(factors, own_narrow * hn, hn, 1)
    coef_in, coef_out = between(factors, own_wide, True), between(factors, own_wide, False)
    message = own_heads(contrib)
    message = jnp.sum(own_heads(coefs[ENDS])[:, :, None, None] * message, axis=0).astype(bf16)
    entering, cot = fence(pass_states(message, coef_in).astype(bf16), cot)
    cot_all = jnp.concatenate(cot, axis=0)
    states = gather_narrow(entering)

    up = lambda b: b
    all_blk, part_blk = rows((BLOCK, width), up), rows((BLOCK, cols), up)
    own_blk = pl.BlockSpec((BLOCK, cols), lambda b, own: (b, own[1]))
    own_kent = pl.BlockSpec((1, hn, hd, hd), lambda b, own: (b, own[1], 0, 0))
    own_direct = rows((1, hn, hd, hd), up)
    att, inverse, gated, hidden, n2, kent = pl.pallas_call(
        functools.partial(out_kernel, heads, hn, hd, share),
        grid_spec=pltpu.PrefetchScalarGridSpec(
            num_scalar_prefetch=1,
            grid=(blocks,),
            in_specs=[SMEM, *[whole((hn, hd, hd))] * narrow, whole((blocks, heads, hd, hd)),
                      *[all_blk] * 4, pl.BlockSpec((narrow, BLOCK, hn), lambda b, own: (0, b, 0)),
                      whole((width, width))],
            out_specs=[all_blk, rows((BLOCK, 1), up), all_blk, whole((share, width)), all_blk, rows((1, heads, hd, hd), up)],
        ),
        out_shape=[sds((local, width), bf16), sds((local, 1), f32), sds((local, width), bf16), sds((share, width), f32),
                   sds((local, width), bf16), sds((blocks, heads, hd, hd), bf16)],
        compiler_params=budget(56),
        cost_estimate=cost(9.5),
        name="mixer_out",
    )(own, coefs, *states, contrib, q, intra, act, tok_all, rise, w_out)

    ff = w_first.shape[1]
    first_t, second_t = w_first.T, w_second.T
    ff_blk = rows((BLOCK, ff), up)
    piece_spec, piece_shape = whole((share, width)), sds((share, width), bf16)
    product, gf, gs, *gn2 = pl.pallas_call(
        functools.partial(ffn_kernel, share),
        out_shape=[*[sds((local, ff), bf16)] * 3, *[piece_shape] * narrow],
        compiler_params=budget(16),
        cost_estimate=cost(10),
        name="ffn",
    )(n2, cot_all, first_t, second_t, w_third)

    gn2 = trade_narrow(gn2)
    product_now, _ = fence(product, gn2[1])
    tall, across = ffn_cut(wide, ff, width)[:2]
    slot = (wide // 2, 3, tall, across)
    slot_spec = pl.BlockSpec((wide // 2, 1, tall, across), lambda i, own: (0, i, 0, 0))
    kept, sent, *ffn_part = pl.pallas_call(
        functools.partial(ffn_grad_kernel, wide, share),
        grid_spec=pltpu.PrefetchScalarGridSpec(
            num_scalar_prefetch=1,
            grid=(3,),
            in_specs=[*[whole((local, width))] * 2, *[whole((local, ff))] * 3, whole((ff, width))],
            out_specs=[slot_spec, slot_spec, *[piece_spec] * narrow],
            scratch_shapes=[pltpu.VMEM((ff, width), f32)],
        ),
        out_shape=[sds(slot, bf16), sds(slot, bf16), *[piece_shape] * narrow],
        compiler_params=budget(16),
        cost_estimate=cost(10),
        name="ffn_grads",
    )(own, n2, cot_all, product_now, gf, gs, w_third)
    gn2, kept, sent = fence(gn2, kept, sent)
    steps = (wide - 1).bit_length() - 1

    def single(shape, index=None):
        where = index or (lambda own: (0,) * len(shape))
        return pl.BlockSpec(shape, lambda b, own: where(own))

    row_spec = single((share, width))
    grad_hidden, ggl, *trios = pl.pallas_call(
        functools.partial(residual_kernel, narrow),
        grid_spec=pltpu.PrefetchScalarGridSpec(
            num_scalar_prefetch=1,
            grid=(1,),
            in_specs=[*[row_spec] * (narrow + 2), single((width, width)), row_spec, single((share, 1)), row_spec],
            out_specs=[row_spec] * 2 + [single((share, 3 * cols))] * narrow,
        ),
        out_shape=[sds((share, width), f32), sds((share, width), bf16),
                   *[sds((share, 3 * cols), bf16)] * narrow],
        compiler_params=budget(16),
        cost_estimate=cost(5),
        name="residual_back",
    )(own, *gn2, hidden, cotangent, w_out, att, inverse, act)
    trios, kept, sent = fence(trios, kept, sent)
    trios, kept, got, ffn_part = fence(trade_narrow(trios), kept, swap_core(sent), ffn_part)
    low, away = halved(kept, got)
    got = swap_step(away, 0)

    own_col = pl.BlockSpec((None, BLOCK, hn), lambda b, own: (own[1], b, 0))
    own_row = pl.BlockSpec((1, hn, BLOCK), lambda b, own: (b * narrow + own[1], 0, 0))
    dq, gk, gv, direct, message = pl.pallas_call(
        functools.partial(query_kernel, hn, hd, share),
        grid_spec=pltpu.PrefetchScalarGridSpec(
            num_scalar_prefetch=1,
            grid=(blocks,),
            in_specs=[SMEM, *[whole((share, 3 * cols))] * narrow, *[own_blk] * 4, own_kent,
                      own_col, own_row, own_col],
            out_specs=[*[part_blk] * 3, own_direct, whole((hn, hd, hd))],
            scratch_shapes=[pltpu.VMEM((BLOCK, cols), bf16)],
        ),
        out_shape=[sds((local, cols), bf16), *[sds((local, cols), f32)] * 2,
                   sds((blocks, hn, hd, hd), f32), sds((hn, hd, hd), f32)],
        compiler_params=budget(56),
        cost_estimate=cost(5.4),
        name="mixer_query_back",
    )(own, coefs, *trios, q, k, v, ql, kent, gcol, grow, rise)

    part_two = swap_narrow(ffn_part[2], 2)
    arrived, low, got, part_two = fence(pass_states(message.astype(bf16), coef_out), low, got, part_two)
    low_ff, away_ff = halved(low, got)

    five = (wide // 2, 5, width // wide, cols)
    one = pl.BlockSpec((wide // 2, 1, width // wide, cols), lambda i, own: (0, 3 + i, 0, 0))
    kept, sent = pl.pallas_call(
        functools.partial(gate_kernel, wide, share),
        grid_spec=pltpu.PrefetchScalarGridSpec(
            num_scalar_prefetch=1,
            grid=(2,),
            in_specs=[*[single((share, 3 * cols))] * narrow, *[single((local, width))] * 2],
            out_specs=[one] * 2,
            scratch_shapes=[pltpu.VMEM((local, cols), bf16), pltpu.VMEM((width, cols), f32)],
        ),
        out_shape=[sds(five, bf16)] * 2,
        compiler_params=budget(16),
        cost_estimate=cost(5),
        name="gate_back",
    )(own, *trios, n1, gated)
    three = whole((wide // 2, 3, width // wide, cols))
    trio_spec, trio_shape = whole((share, 3 * cols)), sds((share, 3 * cols), bf16)
    kept, sent, *dqkv = pl.pallas_call(
        functools.partial(key_kernel, hn, hd, wide, share),
        grid_spec=pltpu.PrefetchScalarGridSpec(
            num_scalar_prefetch=1,
            grid=(blocks,),
            in_specs=[SMEM, whole((hn, hd, hd)), whole((blocks, hn, hd, hd)), all_blk, part_blk,
                      *[own_blk] * 3, *[part_blk] * 2, own_col, rows((BLOCK, 1), up), ANY, ANY],
            out_specs=[three, three, *[trio_spec] * narrow],
            scratch_shapes=[*[pltpu.VMEM((BLOCK, cols), bf16)] * 2, *[pltpu.VMEM((width, cols), f32)] * 3],
        ),
        out_shape=[*[sds(five, bf16)] * 2, *[trio_shape] * narrow],
        input_output_aliases={13: 0, 14: 1},
        compiler_params=budget(56),
        cost_estimate=cost(9),
        name="mixer_key_back",
    )(own, coefs, arrived, direct, n1, dq, k, v, kl, gk, gv, tail, live, kept, sent)

    low, away = halved(kept, swap_core(sent))
    low, away, dqkv, away_ff = fence(low, away, dqkv, away_ff)
    low, high, dqkv, high_ff = fence(low, swap_step(away, 0), trade_narrow(dqkv), swap_step(away_ff, 1))
    for step in range(1, steps):
        low, away = halved(low, high)
        high = swap_step(away, step)
    for step in range(2, steps):
        low_ff, away_ff = halved(low_ff, high_ff)
        high_ff = swap_step(away_ff, step)
    piece = (low + high)[0]
    ff_piece = [(low_ff + high_ff)[0]]

    for step in reversed(range(1, steps)):
        ff_first = len(ff_piece)
        ff_piece = ff_piece + swap_all(ff_piece, step)
    ff_more = swap_all(ff_piece[:ff_first], 0)
    gate_piece, piece, ff_piece, ff_more = fence(
        jnp.stack(gather_narrow(piece[3:])), piece[:3], ff_piece, ff_more
    )
    chunks = width // across
    ffn_form = (tall, across), lambda t: (t // chunks, t % chunks), (ff, width)
    square_form = (width // wide, width), lambda t: (t, 0), (width, width)
    gate_kernels = functools.partial(widen_square_kernel, 2, narrow)
    square_kernels = functools.partial(widen_square_kernel, 3, narrow)

    zs = gather_narrow(piece)
    ff_piece = ff_piece + ff_more + swap_all(ff_piece[ff_first:], 0)
    gate_piece = [gate_piece]
    for step in reversed(range(1, steps)):
        gate_piece = gate_piece + swap_all(gate_piece, step)
    half = len(gate_piece) // 2
    gate_more = swap_all(gate_piece, 0)
    dqkv, _ = fence(dqkv, zs[1])
    grad_tokens = pl.pallas_call(
        functools.partial(tokens_kernel, narrow),
        grid_spec=pltpu.PrefetchScalarGridSpec(
            num_scalar_prefetch=1,
            grid=(narrow,),
            in_specs=[*[single((share, 3 * cols))] * narrow, row_spec, *[pl.BlockSpec((cols, width), lambda i, own: (i, 0))] * 4,
                      row_spec, row_spec],
            out_specs=row_spec,
            scratch_shapes=[*[pltpu.VMEM((share, width), bf16)] * 3, pltpu.VMEM((narrow, share, cols), f32)],
        ),
        out_shape=sds((share, width), f32),
        compiler_params=budget(16),
        cost_estimate=cost(8),
        name="tokens_back",
    )(own, *dqkv, ggl, w_query, w_key, w_value, w_gate, tokens, grad_hidden)
    square_piece, gate_piece, ff_piece, ffn_part, grad_tokens = fence(
        jnp.stack(zs), gate_piece + gate_more, ff_piece, ffn_part, grad_tokens
    )

    square_piece = [square_piece]
    for step in reversed(range(1, steps)):
        square_piece = square_piece + swap_all(square_piece, step)
    square_piece = square_piece + swap_all(square_piece[:half], 0)
    places = wide // 2
    ffn_out = widen(widen_ffn_kernel, own, 0, 0, places, ff_piece, *ffn_form, [], 3, "widen_ffn")
    gate_out = widen(gate_kernels, own, 0, 0, places, gate_piece, *square_form, [], 2, "widen_gate")
    ff_other = swap_cores(ff_piece)
    ffn_out = widen(widen_ffn_kernel, own, 1, 0, places, ff_other, *ffn_form, ffn_out, 3, "widen_ffn")
    square_piece, ffn_out, gate_out, gate_other, ffn_part = fence(
        square_piece, ffn_out, gate_out, swap_cores(gate_piece), ffn_part
    )

    part_three, part_one = swap_narrow(ffn_part[3], 3), swap_narrow(ffn_part[1], 1)
    square_last = swap_all(square_piece[half : places // 2], 0)
    done = len(square_piece)
    gate_out = widen(gate_kernels, own, 1, 0, places, gate_other, *square_form, gate_out, 2, "widen_gate")
    mixer = widen(square_kernels, own, 0, 0, places, square_piece, *square_form, [], 3, "widen_square")
    square_last, gate_out, mixer, square_piece, part_three, part_one = fence(
        square_last, gate_out, mixer, square_piece, part_three, part_one
    )

    output = pl.pallas_call(
        functools.partial(output_kernel, narrow),
        out_shape=sds((share, width), bf16),
        compiler_params=budget(16),
        cost_estimate=cost(2),
        name="output",
    )(ffn_part[0], part_one, part_two, part_three, hidden)
    mixer = widen(square_kernels, own, 0, done, places, square_last, *square_form, mixer, 3, "widen_last")
    square_other = swap_cores(square_piece + square_last)
    mixer = widen(square_kernels, own, 1, 0, places, square_other, *square_form, mixer, 3, "widen_square")
    grad_first, grad_second, grad_third = ffn_out
    grad_gate, grad_out = gate_out
    return (output, grad_tokens, *mixer, grad_gate, grad_out, grad_first.T, grad_second.T, grad_third)


def solution(mesh):
    both = P(("wide", "narrow"), None)
    in_specs = (both, P(None, "wide"), P(), P(), P(), P(), P(), P(), P(),
                P(None, "narrow"), P(None, "narrow"), P("narrow", None), both)
    out_specs = (both, both, P(), P(), P(), P(), P(),
                 P(None, "narrow"), P(None, "narrow"), P("narrow", None))
    return jax.shard_map(body, mesh=mesh, in_specs=in_specs, out_specs=out_specs, check_vma=False)
```

```python
import functools

import jax
import jax.numpy as jnp
from jax import lax
from jax.experimental import pallas as pl
from jax.experimental.pallas import tpu as pltpu
from jax.sharding import PartitionSpec as P

BLOCK = 256
epsilon = 1e-06
bf16 = jnp.bfloat16
f32 = jnp.float32
SMEM = pl.BlockSpec(memory_space=pltpu.SMEM)
ANY = pl.BlockSpec(memory_space=pl.ANY)
sds = jax.ShapeDtypeStruct


def budget(mebibytes):
    return pltpu.CompilerParams(vmem_limit_bytes=mebibytes << 20)


def cost(micros):
    return pl.CostEstimate(flops=0, transcendentals=0, bytes_accessed=int(micros * 3.2e6))


def mm(a, b):
    return lax.dot_general(a, b, (((1,), (0,)), ((), ())), preferred_element_type=f32)


def mt(a, b):
    return lax.dot_general(a, b, (((1,), (1,)), ((), ())), preferred_element_type=f32)


def tm(a, b):
    return lax.dot_general(a, b, (((0,), (0,)), ((), ())), preferred_element_type=f32)


def inv_rms(values):
    return lax.rsqrt(jnp.mean(values * values, axis=-1, keepdims=True) + epsilon)


def sigmoid(values):
    return 0.5 * jnp.tanh(0.5 * values) + 0.5


def slope(values):
    squashed = sigmoid(values)
    return squashed * (1.0 + values * (1.0 - squashed))


def rms_back(values, inverse, gradient):
    normed = values * inverse
    return inverse * (gradient - normed * jnp.mean(gradient * normed, axis=-1, keepdims=True))


def whole(shape):
    zeros = (0,) * len(shape)
    return pl.BlockSpec(shape, lambda *_: zeros)


def rows(shape, index):
    rest = (0,) * (len(shape) - 1)
    return pl.BlockSpec(shape, lambda b, *_: (index(b), *rest))


def causal_of(size, flip):
    return (lax.broadcasted_iota(jnp.int32, (size, size), 0) ^ flip) >= (
        lax.broadcasted_iota(jnp.int32, (size, size), 1) ^ flip
    )


def decay_weights(causal, g_col, g_row):
    return jnp.exp(jnp.where(causal, g_col - g_row, -1e30))


def flip_of(own, share):
    return share * (own[1] & (BLOCK // share - 1))


def exact(a, b, dims):
    return lax.dot_general(a, b, (dims, ((), ())), precision=lax.Precision.HIGHEST, preferred_element_type=f32)


KEEP, ENTER, ENDS, FIRST, SECOND = range(5)


def layout_kernel(narrow, share, own, lengths, pads, log_decay, gcol, rise, tail, grow, live, coefs, total):
    heads, local = log_decay.shape
    hn = heads // narrow
    per, blocks = BLOCK // share, local // BLOCK
    base = own[0] * local
    place = lax.broadcasted_iota(jnp.int32, (local, 1), 0)
    spot = base + ((place // share) ^ own[1]) * share + place % share
    alive = jnp.zeros((local, 1), f32)
    keeps = [jnp.float32(1.0)] * blocks
    end = jnp.int32(0)
    for s in range(lengths.shape[0]):
        start, end = end, end + lengths[s]
        alive = jnp.where((spot >= start) & (spot < end - pads[s]), 1.0, alive)
        keeps = [jnp.where(start == base + b * BLOCK, 0.0, keep) for b, keep in enumerate(keeps)]
    live[...] = alive

    size = (BLOCK, BLOCK)
    upper = (lax.broadcasted_iota(jnp.int32, size, 0) <= lax.broadcasted_iota(jnp.int32, size, 1)).astype(f32)
    eye = (lax.broadcasted_iota(jnp.int32, (heads, heads), 0)
           == lax.broadcasted_iota(jnp.int32, (heads, heads), 1)).astype(f32)
    turned = own[1] // per > 0
    rows_of, ends_of, decay_of, keep_of = [], [], [], []
    for b in range(blocks):
        part = log_decay[:, b * BLOCK : (b + 1) * BLOCK]
        g = exact(part, upper, ((1,), (0,)))
        for bit in range((per - 1).bit_length()):
            step = share << bit
            flipped = [g[:, (i ^ 1) * step : ((i ^ 1) + 1) * step] for i in range(BLOCK // step)]
            g = jnp.where((own[1] >> bit) & 1 == 1, jnp.concatenate(flipped, axis=1), g)
        end_row = exact(jnp.ones_like(part), part, ((1,), (1,)))[0:1]
        rows_of.append(g)
        ends_of.append(end_row)
        decay_of.append(jnp.exp(end_row) * keeps[b])
        keep_of.append(jnp.full((1, heads), 1.0, f32) * keeps[b])
    total[...] = decay_of[0] * decay_of[1]
    one = jnp.ones((1, heads), f32)
    kinds = (keep_of, (one, decay_of[0]), (decay_of[1], one), (one, 0.0 * one), (0.0 * one, one))
    for s in range(blocks):
        def mine(pair):
            return jnp.where(turned, pair[1 - s], pair[s])

        for kind, pair in enumerate(kinds):
            coefs[kind, s : s + 1, :] = mine(pair)
        g = mine(rows_of)
        column = exact(g, eye, ((0,), (0,)))
        up, down = jnp.exp(column), jnp.exp(mine(ends_of) - column)
        at = slice(s * BLOCK, (s + 1) * BLOCK)
        for n in range(narrow):
            group = slice(n * hn, (n + 1) * hn)
            gcol[n, at, :] = column[:, group]
            rise[n, at, :] = up[:, group]
            tail[n, at, :] = down[:, group]
            grow[s * narrow + n] = g[group, :]


def forward_kernel(hn, hd, share, own, tok_a, tok_b, wq, wk, wv, wg, live, gcol, grow, tail, *refs):
    n1, tok, ql, kl, q, k, v, act, intra, contrib = refs[-10:]
    i = pl.program_id(0)

    @pl.when(i == 0)
    def _():
        for part, source in enumerate((tok_a, tok_b)):
            at = slice(part * share, (part + 1) * share)
            tok[at, :] = source[...]
            values = source[...].astype(f32)
            n1[at, :] = (values * inv_rms(values)).astype(bf16)

    normed = n1[...]
    q_lin = mm(normed, wq[...])
    k_lin = mm(normed, wk[...])

    ql[...] = q_lin
    kl[...] = k_lin
    q[...] = (q_lin * sigmoid(q_lin)).astype(bf16)
    k[...] = (k_lin * sigmoid(k_lin) * live[...]).astype(bf16)
    v[...] = mm(normed, wv[...]).astype(bf16)
    act[...] = sigmoid(mm(normed, wg[...]))
    causal = causal_of(BLOCK, flip_of(own, share))
    for h in range(hn):
        at = slice(h * hd, (h + 1) * hd)
        qh, kh, vh = q[:, at], k[:, at], v[:, at]
        weights = decay_weights(causal, gcol[0, :, h : h + 1], grow[0, h : h + 1, :])
        scores = (mt(qh, kh) * weights).astype(bf16)
        intra[:, at] = mm(scores, vh)
        key_tail = (kh.astype(f32) * tail[0, :, h : h + 1]).astype(bf16)
        contrib[0, h] = tm(key_tail, vh)


def out_kernel(heads, hn, hd, share, own, coefs, *refs):
    narrow = heads // hn
    states = refs[:narrow]
    contrib, q, intra, act, tok, rise, wo, att, inverse, gated, hidden, n2, kent = refs[narrow:]
    b = pl.program_id(0)
    for h in range(heads):
        at = slice(h * hd, (h + 1) * hd)
        part = own[1] ^ (h // hn)
        base = states[0][h % hn].astype(f32)
        for j in range(1, narrow):
            base = jnp.where(part == j, states[j][h % hn].astype(f32), base)
        entering = coefs[ENTER, b, h] * base + coefs[SECOND, b, h] * contrib[1 - b, h]
        kept = (coefs[KEEP, b, h] * entering).astype(bf16)
        kent[0, h] = kept
        att[:, at] = (intra[:, at] + rise[h // hn, :, h % hn : h % hn + 1] * mm(q[:, at], kept)).astype(bf16)
    values = att[...].astype(f32)
    scale = inv_rms(values)
    inverse[...] = scale
    gated[...] = (values * scale * act[...]).astype(bf16)
    hid = tok[...].astype(f32) + mm(gated[...], wo[...])

    @pl.when(b == 0)
    def _():
        hidden[...] = hid[:share]

    n2[...] = (hid * inv_rms(hid)).astype(bf16)


def ffn_kernel(share, n2, cot, w1, w2, w3, product, gf, gs, *pieces):
    normed = n2[...]
    first = mt(normed, w1[...])
    second = mt(normed, w2[...])
    product[...] = (first * second).astype(bf16)
    grad = mt(cot[...], w3[...])
    gf[...] = (grad * second).astype(bf16)
    gs[...] = (grad * first).astype(bf16)
    back = (mm(gf[...], w1[...]) + mm(gs[...], w2[...])).astype(bf16)
    for i, piece in enumerate(pieces):
        piece[...] = back[i * share : (i + 1) * share]


def reversed_bits(value, count):
    out = 0
    for i in range(count):
        out = out | (((value >> i) & 1) << (count - 1 - i))
    return out


def position(offset, parity, wide):
    bits = (wide - 1).bit_length() - 1
    high = offset >> 1
    return jnp.where(parity == 0, reversed_bits(high, bits), high)


def scatter(wide, own, kept, sent, item, piece_of):
    for t in range(wide):
        offset = own[0] ^ t
        parity = own[0] & 1

        @pl.when(offset & 1 == 0)
        def _():
            kept[position(offset, parity, wide), item] = piece_of(t).astype(bf16)

        @pl.when(offset & 1 == 1)
        def _():
            sent[position(offset, 1 - parity, wide), item] = piece_of(t).astype(bf16)


def ffn_cut(wide, ff, width):
    across = min(wide, width // 128)
    return ff // (wide // across), width // across, across


def ffn_grad_kernel(wide, share, own, n2, cot, product, gf, gs, w3, kept, sent, *refs):
    pieces, acc = refs[:-1], refs[-1]
    item = pl.program_id(0)
    for i, (left, right) in enumerate(((gf, n2), (gs, n2), (product, cot))):
        @pl.when(item == i)
        def _():
            acc[...] = tm(left[...], right[...])

    tall, cols, across = ffn_cut(wide, *acc.shape)

    def piece_of(t):
        row, col = t // across * tall, t % across * cols
        return acc[row : row + tall, col : col + cols]

    scatter(wide, own, kept, sent, 0, piece_of)

    @pl.when(item == 2)
    def _():
        for i, piece in enumerate(pieces):
            piece[...] = mm(product[i * share : (i + 1) * share, :], w3[...]).astype(bf16)


def residual_kernel(narrow, own, *refs):
    parts = refs[:narrow]
    hidden, cot, wo, att, inverse, act, grad_hidden, ggl = refs[narrow : narrow + 8]
    trios = refs[narrow + 8 :]
    gn2 = parts[0][...].astype(f32)
    for part in parts[1:]:
        gn2 = gn2 + part[...].astype(f32)
    hid = hidden[...]
    gh = cot[...].astype(f32) + rms_back(hid, inv_rms(hid), gn2)
    grad_hidden[...] = gh
    low = gh.astype(bf16)
    gg = mt(low, wo[...])
    values = att[...].astype(f32)
    gate = act[...]
    ggl[...] = (gg * (values * inverse[...]) * gate * (1.0 - gate)).astype(bf16)
    back = rms_back(values, inverse[...], gg * gate).astype(bf16)
    size = back.shape[1] // narrow
    for i in range(narrow):
        for k in range(narrow):
            @pl.when(own[1] ^ i == k)
            def _():
                at = slice(i * size, (i + 1) * size)
                trios[k][:, :size] = back[:, at]
                trios[k][:, size : 2 * size] = ggl[:, at]
                trios[k][:, 2 * size :] = low[:, at]


def query_kernel(hn, hd, share, own, coefs, *refs):
    per = BLOCK // share
    ga = refs[: -14]
    q, k, v, ql, kent, gcol, grow, rise, dq, gk, gv, direct, first, grad = refs[-14:]
    b = pl.program_id(0)
    for i, piece in enumerate(ga):
        @pl.when(b == i // per)
        def _():
            grad[(i % per) * share : (i % per + 1) * share, :] = piece[:, : grad.shape[1]]

    causal = causal_of(BLOCK, flip_of(own, share))
    for h in range(hn):
        at = slice(h * hd, (h + 1) * hd)
        g, qh, kh, vh = grad[:, at], q[:, at], k[:, at], v[:, at]
        weights = decay_weights(causal, gcol[:, h : h + 1], grow[0, h : h + 1, :])
        scores = (mt(qh, kh) * weights).astype(bf16)
        raw = (mt(g, vh) * weights).astype(bf16)
        up = rise[:, h : h + 1]
        gq = mm(raw, kh) + up * mt(g, kent[0, h])
        dq[:, at] = (gq * slope(ql[:, at])).astype(bf16)
        gk[:, at] = tm(raw, qh)
        gv[:, at] = tm(scores, g)
        head = own[1] * hn + h
        now = coefs[KEEP, b, head] * tm((qh.astype(f32) * up).astype(bf16), g)
        direct[0, h] = now

        first[h] = jnp.where(b == 0, 0.0, first[h]) + coefs[ENTER, b, head] * now


def key_kernel(hn, hd, wide, share, own, coefs, arrived, direct, n1, dq, k, v, kl, gk, gv,
               tail, live, _kept, _sent, kept, sent, *refs):
    pieces = refs[:-5]
    dk, dv, aq, ak, av = refs[-5:]
    per = BLOCK // share
    b = pl.program_id(0)
    last = pl.num_programs(0) - 1
    for h in range(hn):
        at = slice(h * hd, (h + 1) * hd)
        head = own[1] * hn + h
        low = (coefs[ENDS, b, head] * arrived[h] + coefs[FIRST, b, head] * direct[1 - b, h]).astype(bf16)
        down = tail[:, h : h + 1]
        grad_key = gk[:, at] + down * mt(v[:, at], low)
        dk[:, at] = (grad_key * live[...] * slope(kl[:, at])).astype(bf16)
        dv[:, at] = (gv[:, at] + down * mm(k[:, at], low)).astype(bf16)
    normed = n1[...]
    tall = normed.shape[1] // wide
    for acc, part in ((aq, dq), (ak, dk), (av, dv)):
        acc[...] = jnp.where(b == 0, 0.0, acc[...]) + tm(normed, part[...])

    for item, acc in enumerate((aq, ak, av)):
        @pl.when(b == last)
        def _():
            scatter(wide, own, kept, sent, item, lambda t: acc[t * tall : (t + 1) * tall, :])

    cols = dq.shape[1]
    for i, piece in enumerate(pieces):
        @pl.when(b == i // per)
        def _():
            for item, part in enumerate((dq, dk, dv)):
                piece[:, item * cols : (item + 1) * cols] = part[(i % per) * share : (i % per + 1) * share, :]


def gate_kernel(wide, share, own, *refs):
    trios = refs[:-6]
    n1, gated, kept, sent, grads, acc = refs[-6:]
    item = pl.program_id(0)
    cols = acc.shape[1]
    tall = acc.shape[0] // wide
    for step, left in enumerate((n1, gated)):
        @pl.when(item == step)
        def _():
            at = slice((step + 1) * cols, (step + 2) * cols)
            for i, piece in enumerate(trios):
                grads[i * share : (i + 1) * share, :] = piece[:, at]
            acc[...] = tm(left[...], grads[...])

    scatter(wide, own, kept, sent, 0, lambda t: acc[t * tall : (t + 1) * tall, :])


def tokens_kernel(narrow, own, *refs):
    parts = refs[:narrow]
    ggl, wq, wk, wv, wg, tok, gh, out, *grads, total = refs[narrow:]
    step = pl.program_id(0)
    cols = parts[0].shape[1] // 3

    @pl.when(step == 0)
    def _():
        for i in range(narrow):
            for k in range(narrow):
                @pl.when(own[1] ^ i == k)
                def _():
                    for item, full in enumerate(grads):
                        full[:, i * cols : (i + 1) * cols] = parts[k][:, item * cols : (item + 1) * cols]

    grad = mt(ggl[...], wg[...])
    for full, weight in zip(grads, (wq, wk, wv)):
        grad = grad + mt(full[...], weight[...])
    total[step] = grad

    @pl.when(step == narrow - 1)
    def _():
        grad = jnp.concatenate([total[i] for i in range(narrow)], axis=1)
        values = tok[...].astype(f32)
        out[...] = gh[...] + rms_back(values, inv_rms(values), grad)


def output_kernel(narrow, *refs):
    hidden, out = refs[narrow:]
    total = hidden[...]
    for part in refs[:narrow]:
        total = total + part[...].astype(f32)
    out[...] = total.astype(bf16)


def swap_narrow(values, k):
    size = lax.axis_size("narrow")
    return lax.ppermute(values, "narrow", [(i, i ^ k) for i in range(size)])


def gather_narrow(values):
    return [values] + [swap_narrow(values, k) for k in range(1, lax.axis_size("narrow"))]


def trade_narrow(pieces):
    return [pieces[0]] + [swap_narrow(pieces[k], k) for k in range(1, len(pieces))]


def swap_core(values):
    size = lax.axis_size("wide")
    return lax.ppermute(values, "wide", [(i, i ^ 1) for i in range(size)])


def swap_step(values, step):
    size = lax.axis_size("wide")
    bits = (size - 1).bit_length()
    flip = lambda i: i ^ (1 << (1 + step if i % 2 == 0 else bits - 1 - step))
    return lax.ppermute(values, "wide", [(i, flip(i)) for i in range(size)])


def fence(*values):
    return lax.optimization_barrier(values)


def halved(low, high):
    half = low.shape[0] // 2
    return low[:half] + high[:half], low[half:] + high[half:]


def swap_all(parts, step):
    return [swap_step(part, step) for part in parts]


def swap_cores(parts):
    return [swap_core(part) for part in parts]


def target(own, place, other, wide):
    bits = (wide - 1).bit_length() - 1
    parity = (own[0] & 1) ^ other
    high = jnp.where(parity == 0, reversed_bits(place, bits), place)
    return own[0] ^ other ^ (2 * high)


def widen_square_kernel(count, narrow, places, own, *refs):
    pieces, outs = refs[:places], refs[-count:]
    for j, piece in enumerate(pieces):
        @pl.when(pl.program_id(0) == j)
        def _():
            cols = piece.shape[-1]
            for item in range(count):
                for n in range(narrow):
                    outs[item][:, n * cols : (n + 1) * cols] = piece[own[1] ^ n, item].astype(f32)


def widen_ffn_kernel(places, own, *refs):
    pieces, outs = refs[:places], refs[-3:]
    for j, piece in enumerate(pieces):
        @pl.when(pl.program_id(0) == j)
        def _():
            for item in range(3):
                outs[item][...] = piece[item].astype(f32)


def widen(kernel, own, other, first, total, pieces, block, cut, shape, outs, count, name):
    places = len(pieces)
    spec = pl.BlockSpec(block, lambda i, own: cut(target(own, first + i, other, 2 * total)))
    return pl.pallas_call(
        functools.partial(kernel, places),
        grid_spec=pltpu.PrefetchScalarGridSpec(
            num_scalar_prefetch=1,
            grid=(places,),
            in_specs=[whole(p.shape) for p in pieces] + [ANY] * len(outs),
            out_specs=[spec] * count,
        ),
        out_shape=[sds(shape, f32)] * count,
        input_output_aliases={1 + places + i: i for i in range(len(outs))},
        compiler_params=budget(16),
        cost_estimate=cost(4),
        name=f"{name}_{other}",
    )(own, *pieces, *outs)


def xor_order(values, own, axis):
    count = values.shape[axis]
    for bit in range((count - 1).bit_length()):
        step = 1 << bit
        shape = values.shape
        split = values.reshape(shape[:axis] + (count // (2 * step), 2, step) + shape[axis + 1 :])
        flipped = jnp.flip(split, axis + 1)
        values = jnp.where((own >> bit) & 1 == 1, flipped, split).reshape(shape)
    return values


def gather_factors(values):
    size, own = lax.axis_size("wide"), lax.axis_index("wide")
    full = values[None]
    for bit in range((size - 1).bit_length()):
        got = lax.ppermute(full, "wide", [(i, i ^ (1 << bit)) for i in range(size)])
        full = jnp.concatenate([full, got], axis=0)
    return xor_order(full, own, 0)


def between(factors, own, before):
    count = factors.shape[0]
    j = jnp.arange(count)[:, None]
    i = jnp.arange(count)[None, :]
    if before:
        inner, wanted = (i > j) & (i < own), j[:, 0] < own
    else:
        inner, wanted = (i < j) & (i > own), j[:, 0] > own
    terms = jnp.where(inner[:, :, None], factors[None], 1.0)
    return jnp.where(wanted[:, None], jnp.prod(terms, axis=1), 0.0)


def pass_states(message, coef):
    gathered = lax.all_gather(message, "wide", axis=0)
    return jnp.sum(coef[:, :, None, None] * gathered.astype(f32), axis=0)


def body(tokens, log_decay, lengths, pad_counts, w_query, w_key, w_value, w_gate, w_out,
         w_first, w_second, w_third, cotangent):
    wide, narrow = lax.axis_size("wide"), lax.axis_size("narrow")
    own_wide, own_narrow = lax.axis_index("wide"), lax.axis_index("narrow")
    heads, local = log_decay.shape
    share, width = tokens.shape
    hn, cols, hd = heads // narrow, width // narrow, width // heads
    blocks, per = local // BLOCK, BLOCK // share
    own = jnp.stack([own_wide, own_narrow]).astype(jnp.int32)

    tok = gather_narrow(tokens)

    columns = sds((narrow, local, hn), f32)
    gcol, rise, tail, grow, live, coefs, total = pl.pallas_call(
        functools.partial(layout_kernel, narrow, share),
        in_specs=[SMEM, SMEM, SMEM, pl.BlockSpec(memory_space=pltpu.VMEM)],
        out_shape=[columns, columns, columns, sds((blocks * narrow, hn, BLOCK), f32), sds((local, 1), f32),
                   sds((5, blocks, heads), f32), sds((1, heads), f32)],
        compiler_params=budget(16),
        cost_estimate=cost(3),
        name="layout",
    )(own, lengths, pad_counts, log_decay)

    def own_heads(values):
        return lax.dynamic_slice_in_dim(values, own_narrow * hn, hn, 1)

    shapes = [sds((local, width), bf16), sds((local, width), bf16), *[sds((local, width), f32)] * 2,
              *[sds((local, width), bf16)] * 3, *[sds((local, width), f32)] * 2,
              sds((blocks, heads, hd, hd), f32)]
    made = []
    for s in range(blocks):
        if s == 1:
            made, later, cotangent_now, product_now = fence(made, tok[per:], cotangent, total)
            tok = tok[:per] + list(later)
        weight = pl.BlockSpec((width, cols), lambda i, own: (0, i))
        column = pl.BlockSpec((1, BLOCK, hn), lambda i, own, s=s: (i, s, 0))
        full = pl.BlockSpec((BLOCK, width), lambda i, own, s=s: (s, 0))
        part = pl.BlockSpec((BLOCK, cols), lambda i, own, s=s: (s, i))
        made = pl.pallas_call(
            functools.partial(forward_kernel, hn, hd, share),
            grid_spec=pltpu.PrefetchScalarGridSpec(
                num_scalar_prefetch=1,
                grid=(narrow,),
                in_specs=[*[whole((share, width))] * 2, *[weight] * 4,
                          pl.BlockSpec((BLOCK, 1), lambda i, own, s=s: (s, 0)), column,
                          pl.BlockSpec((1, hn, BLOCK), lambda i, own, s=s: (s * narrow + i, 0, 0)),
                          column, *[ANY] * len(made)],
                out_specs=[full, full, *[part] * 7,
                           pl.BlockSpec((1, hn, hd, hd), lambda i, own, s=s: (s, i, 0, 0))],
            ),
            out_shape=shapes,
            input_output_aliases={11 + i: i for i in range(len(made))},
            compiler_params=budget(56),
            cost_estimate=cost(10),
            name=f"mixer_forward_{s}",
        )(own, tok[per * s], tok[per * s + 1], w_query, w_key, w_value, w_gate, live, gcol, grow, tail, *made)
    n1, tok_all, ql, kl, q, k, v, act, intra, contrib = made

    cot = gather_narrow(cotangent_now)
    factors = gather_factors(product_now[0])
    factors = lax.dynamic_slice_in_dim(factors, own_narrow * hn, hn, 1)
    coef_in, coef_out = between(factors, own_wide, True), between(factors, own_wide, False)
    message = own_heads(contrib)
    message = jnp.sum(own_heads(coefs[ENDS])[:, :, None, None] * message, axis=0).astype(bf16)
    entering, cot = fence(pass_states(message, coef_in).astype(bf16), cot)
    cot_all = jnp.concatenate(cot, axis=0)
    states = gather_narrow(entering)

    up = lambda b: b
    all_blk, part_blk = rows((BLOCK, width), up), rows((BLOCK, cols), up)
    own_blk = pl.BlockSpec((BLOCK, cols), lambda b, own: (b, own[1]))
    own_kent = pl.BlockSpec((1, hn, hd, hd), lambda b, own: (b, own[1], 0, 0))
    own_direct = rows((1, hn, hd, hd), up)
    att, inverse, gated, hidden, n2, kent = pl.pallas_call(
        functools.partial(out_kernel, heads, hn, hd, share),
        grid_spec=pltpu.PrefetchScalarGridSpec(
            num_scalar_prefetch=1,
            grid=(blocks,),
            in_specs=[SMEM, *[whole((hn, hd, hd))] * narrow, whole((blocks, heads, hd, hd)),
                      *[all_blk] * 4, pl.BlockSpec((narrow, BLOCK, hn), lambda b, own: (0, b, 0)),
                      whole((width, width))],
            out_specs=[all_blk, rows((BLOCK, 1), up), all_blk, whole((share, width)), all_blk, rows((1, heads, hd, hd), up)],
        ),
        out_shape=[sds((local, width), bf16), sds((local, 1), f32), sds((local, width), bf16), sds((share, width), f32),
                   sds((local, width), bf16), sds((blocks, heads, hd, hd), bf16)],
        compiler_params=budget(56),
        cost_estimate=cost(9.5),
        name="mixer_out",
    )(own, coefs, *states, contrib, q, intra, act, tok_all, rise, w_out)

    ff = w_first.shape[1]
    first_t, second_t = w_first.T, w_second.T
    ff_blk = rows((BLOCK, ff), up)
    piece_spec, piece_shape = whole((share, width)), sds((share, width), bf16)
    product, gf, gs, *gn2 = pl.pallas_call(
        functools.partial(ffn_kernel, share),
        out_shape=[*[sds((local, ff), bf16)] * 3, *[piece_shape] * narrow],
        compiler_params=budget(16),
        cost_estimate=cost(10),
        name="ffn",
    )(n2, cot_all, first_t, second_t, w_third)

    gn2 = trade_narrow(gn2)
    product_now, _ = fence(product, gn2[1])
    tall, across = ffn_cut(wide, ff, width)[:2]
    slot = (wide // 2, 3, tall, across)
    slot_spec = pl.BlockSpec((wide // 2, 1, tall, across), lambda i, own: (0, i, 0, 0))
    kept, sent, *ffn_part = pl.pallas_call(
        functools.partial(ffn_grad_kernel, wide, share),
        grid_spec=pltpu.PrefetchScalarGridSpec(
            num_scalar_prefetch=1,
            grid=(3,),
            in_specs=[*[whole((local, width))] * 2, *[whole((local, ff))] * 3, whole((ff, width))],
            out_specs=[slot_spec, slot_spec, *[piece_spec] * narrow],
            scratch_shapes=[pltpu.VMEM((ff, width), f32)],
        ),
        out_shape=[sds(slot, bf16), sds(slot, bf16), *[piece_shape] * narrow],
        compiler_params=budget(16),
        cost_estimate=cost(10),
        name="ffn_grads",
    )(own, n2, cot_all, product_now, gf, gs, w_third)
    gn2, kept, sent = fence(gn2, kept, sent)
    steps = (wide - 1).bit_length() - 1

    def single(shape, index=None):
        where = index or (lambda own: (0,) * len(shape))
        return pl.BlockSpec(shape, lambda b, own: where(own))

    row_spec = single((share, width))
    grad_hidden, ggl, *trios = pl.pallas_call(
        functools.partial(residual_kernel, narrow),
        grid_spec=pltpu.PrefetchScalarGridSpec(
            num_scalar_prefetch=1,
            grid=(1,),
            in_specs=[*[row_spec] * (narrow + 2), single((width, width)), row_spec, single((share, 1)), row_spec],
            out_specs=[row_spec] * 2 + [single((share, 3 * cols))] * narrow,
        ),
        out_shape=[sds((share, width), f32), sds((share, width), bf16),
                   *[sds((share, 3 * cols), bf16)] * narrow],
        compiler_params=budget(16),
        cost_estimate=cost(5),
        name="residual_back",
    )(own, *gn2, hidden, cotangent, w_out, att, inverse, act)
    trios, kept, sent = fence(trios, kept, sent)
    trios, kept, got, ffn_part = fence(trade_narrow(trios), kept, swap_core(sent), ffn_part)
    low, away = halved(kept, got)
    got = swap_step(away, 0)

    own_col = pl.BlockSpec((None, BLOCK, hn), lambda b, own: (own[1], b, 0))
    own_row = pl.BlockSpec((1, hn, BLOCK), lambda b, own: (b * narrow + own[1], 0, 0))
    dq, gk, gv, direct, message = pl.pallas_call(
        functools.partial(query_kernel, hn, hd, share),
        grid_spec=pltpu.PrefetchScalarGridSpec(
            num_scalar_prefetch=1,
            grid=(blocks,),
            in_specs=[SMEM, *[whole((share, 3 * cols))] * narrow, *[own_blk] * 4, own_kent,
                      own_col, own_row, own_col],
            out_specs=[*[part_blk] * 3, own_direct, whole((hn, hd, hd))],
            scratch_shapes=[pltpu.VMEM((BLOCK, cols), bf16)],
        ),
        out_shape=[sds((local, cols), bf16), *[sds((local, cols), f32)] * 2,
                   sds((blocks, hn, hd, hd), f32), sds((hn, hd, hd), f32)],
        compiler_params=budget(56),
        cost_estimate=cost(5.4),
        name="mixer_query_back",
    )(own, coefs, *trios, q, k, v, ql, kent, gcol, grow, rise)

    part_two = swap_narrow(ffn_part[2], 2)
    arrived, low, got, part_two = fence(pass_states(message.astype(bf16), coef_out), low, got, part_two)
    low_ff, away_ff = halved(low, got)

    five = (wide // 2, 5, width // wide, cols)
    one = pl.BlockSpec((wide // 2, 1, width // wide, cols), lambda i, own: (0, 3 + i, 0, 0))
    kept, sent = pl.pallas_call(
        functools.partial(gate_kernel, wide, share),
        grid_spec=pltpu.PrefetchScalarGridSpec(
            num_scalar_prefetch=1,
            grid=(2,),
            in_specs=[*[single((share, 3 * cols))] * narrow, *[single((local, width))] * 2],
            out_specs=[one] * 2,
            scratch_shapes=[pltpu.VMEM((local, cols), bf16), pltpu.VMEM((width, cols), f32)],
        ),
        out_shape=[sds(five, bf16)] * 2,
        compiler_params=budget(16),
        cost_estimate=cost(5),
        name="gate_back",
    )(own, *trios, n1, gated)
    three = whole((wide // 2, 3, width // wide, cols))
    trio_spec, trio_shape = whole((share, 3 * cols)), sds((share, 3 * cols), bf16)
    kept, sent, *dqkv = pl.pallas_call(
        functools.partial(key_kernel, hn, hd, wide, share),
        grid_spec=pltpu.PrefetchScalarGridSpec(
            num_scalar_prefetch=1,
            grid=(blocks,),
            in_specs=[SMEM, whole((hn, hd, hd)), whole((blocks, hn, hd, hd)), all_blk, part_blk,
                      *[own_blk] * 3, *[part_blk] * 2, own_col, rows((BLOCK, 1), up), ANY, ANY],
            out_specs=[three, three, *[trio_spec] * narrow],
            scratch_shapes=[*[pltpu.VMEM((BLOCK, cols), bf16)] * 2, *[pltpu.VMEM((width, cols), f32)] * 3],
        ),
        out_shape=[*[sds(five, bf16)] * 2, *[trio_shape] * narrow],
        input_output_aliases={13: 0, 14: 1},
        compiler_params=budget(16),
        cost_estimate=cost(9),
        name="mixer_key_back",
    )(own, coefs, arrived, direct, n1, dq, k, v, kl, gk, gv, tail, live, kept, sent)

    low, away = halved(kept, swap_core(sent))
    low, away, dqkv, away_ff = fence(low, away, dqkv, away_ff)
    low, high, dqkv, high_ff = fence(low, swap_step(away, 0), trade_narrow(dqkv), swap_step(away_ff, 1))
    for step in range(1, steps):
        low, away = halved(low, high)
        high = swap_step(away, step)
    for step in range(2, steps):
        low_ff, away_ff = halved(low_ff, high_ff)
        high_ff = swap_step(away_ff, step)
    piece = (low + high)[0]
    ff_piece = [(low_ff + high_ff)[0]]

    for step in reversed(range(1, steps)):
        ff_first = len(ff_piece)
        ff_piece = ff_piece + swap_all(ff_piece, step)
    ff_more = swap_all(ff_piece[:ff_first], 0)
    gate_piece, piece, ff_piece, ff_more = fence(
        jnp.stack(gather_narrow(piece[3:])), piece[:3], ff_piece, ff_more
    )
    chunks = width // across
    ffn_form = (tall, across), lambda t: (t // chunks, t % chunks), (ff, width)
    square_form = (width // wide, width), lambda t: (t, 0), (width, width)
    gate_kernels = functools.partial(widen_square_kernel, 2, narrow)
    square_kernels = functools.partial(widen_square_kernel, 3, narrow)

    zs = gather_narrow(piece)
    ff_piece = ff_piece + ff_more + swap_all(ff_piece[ff_first:], 0)
    gate_piece = [gate_piece]
    for step in reversed(range(1, steps)):
        gate_piece = gate_piece + swap_all(gate_piece, step)
    half = len(gate_piece) // 2
    gate_more = swap_all(gate_piece, 0)
    dqkv, _ = fence(dqkv, zs[1])
    grad_tokens = pl.pallas_call(
        functools.partial(tokens_kernel, narrow),
        grid_spec=pltpu.PrefetchScalarGridSpec(
            num_scalar_prefetch=1,
            grid=(narrow,),
            in_specs=[*[single((share, 3 * cols))] * narrow, row_spec, *[pl.BlockSpec((cols, width), lambda i, own: (i, 0))] * 4,
                      row_spec, row_spec],
            out_specs=row_spec,
            scratch_shapes=[*[pltpu.VMEM((share, width), bf16)] * 3, pltpu.VMEM((narrow, share, cols), f32)],
        ),
        out_shape=sds((share, width), f32),
        compiler_params=budget(16),
        cost_estimate=cost(8),
        name="tokens_back",
    )(own, *dqkv, ggl, w_query, w_key, w_value, w_gate, tokens, grad_hidden)
    square_piece, gate_piece, ff_piece, ffn_part, grad_tokens = fence(
        jnp.stack(zs), gate_piece + gate_more, ff_piece, ffn_part, grad_tokens
    )

    square_piece = [square_piece]
    for step in reversed(range(1, steps)):
        square_piece = square_piece + swap_all(square_piece, step)
    square_piece = square_piece + swap_all(square_piece[:half], 0)
    places = wide // 2
    ffn_out = widen(widen_ffn_kernel, own, 0, 0, places, ff_piece, *ffn_form, [], 3, "widen_ffn")
    gate_out = widen(gate_kernels, own, 0, 0, places, gate_piece, *square_form, [], 2, "widen_gate")
    ff_other = swap_cores(ff_piece)
    ffn_out = widen(widen_ffn_kernel, own, 1, 0, places, ff_other, *ffn_form, ffn_out, 3, "widen_ffn")
    square_piece, ffn_out, gate_out, gate_other, ffn_part = fence(
        square_piece, ffn_out, gate_out, swap_cores(gate_piece), ffn_part
    )

    part_three, part_one = swap_narrow(ffn_part[3], 3), swap_narrow(ffn_part[1], 1)
    square_last = swap_all(square_piece[half : places // 2], 0)
    done = len(square_piece)
    gate_out = widen(gate_kernels, own, 1, 0, places, gate_other, *square_form, gate_out, 2, "widen_gate")
    mixer = widen(square_kernels, own, 0, 0, places, square_piece, *square_form, [], 3, "widen_square")
    square_last, gate_out, mixer, square_piece, part_three, part_one = fence(
        square_last, gate_out, mixer, square_piece, part_three, part_one
    )

    output = pl.pallas_call(
        functools.partial(output_kernel, narrow),
        out_shape=sds((share, width), bf16),
        compiler_params=budget(16),
        cost_estimate=cost(2),
        name="output",
    )(ffn_part[0], part_one, part_two, part_three, hidden)
    mixer = widen(square_kernels, own, 0, done, places, square_last, *square_form, mixer, 3, "widen_last")
    square_other = swap_cores(square_piece + square_last)
    mixer = widen(square_kernels, own, 1, 0, places, square_other, *square_form, mixer, 3, "widen_square")
    grad_first, grad_second, grad_third = ffn_out
    grad_gate, grad_out = gate_out
    return (output, grad_tokens, *mixer, grad_gate, grad_out, grad_first.T, grad_second.T, grad_third)


def solution(mesh):
    both = P(("wide", "narrow"), None)
    in_specs = (both, P(None, "wide"), P(), P(), P(), P(), P(), P(), P(),
                P(None, "narrow"), P(None, "narrow"), P("narrow", None), both)
    out_specs = (both, both, P(), P(), P(), P(), P(),
                 P(None, "narrow"), P(None, "narrow"), P("narrow", None))
    return jax.shard_map(body, mesh=mesh, in_specs=in_specs, out_specs=out_specs, check_vma=False)
```

```python
import functools

import jax
import jax.numpy as jnp
from jax import lax
from jax.experimental import pallas as pl
from jax.experimental.pallas import tpu as pltpu
from jax.sharding import PartitionSpec as P

BLOCK = 256
epsilon = 1e-06
bf16 = jnp.bfloat16
f32 = jnp.float32
SMEM = pl.BlockSpec(memory_space=pltpu.SMEM)
ANY = pl.BlockSpec(memory_space=pl.ANY)
sds = jax.ShapeDtypeStruct


def budget(mebibytes):
    return pltpu.CompilerParams(vmem_limit_bytes=mebibytes << 20)


def cost(micros):
    return pl.CostEstimate(flops=0, transcendentals=0, bytes_accessed=int(micros * 3.2e6))


def mm(a, b):
    return lax.dot_general(a, b, (((1,), (0,)), ((), ())), preferred_element_type=f32)


def mt(a, b):
    return lax.dot_general(a, b, (((1,), (1,)), ((), ())), preferred_element_type=f32)


def tm(a, b):
    return lax.dot_general(a, b, (((0,), (0,)), ((), ())), preferred_element_type=f32)


def inv_rms(values):
    return lax.rsqrt(jnp.mean(values * values, axis=-1, keepdims=True) + epsilon)


def sigmoid(values):
    return 0.5 * jnp.tanh(0.5 * values) + 0.5


def slope(values):
    squashed = sigmoid(values)
    return squashed * (1.0 + values * (1.0 - squashed))


def rms_back(values, inverse, gradient):
    normed = values * inverse
    return inverse * (gradient - normed * jnp.mean(gradient * normed, axis=-1, keepdims=True))


def whole(shape):
    zeros = (0,) * len(shape)
    return pl.BlockSpec(shape, lambda *_: zeros)


def rows(shape, index):
    rest = (0,) * (len(shape) - 1)
    return pl.BlockSpec(shape, lambda b, *_: (index(b), *rest))


def causal_of(size, flip):
    return (lax.broadcasted_iota(jnp.int32, (size, size), 0) ^ flip) >= (
        lax.broadcasted_iota(jnp.int32, (size, size), 1) ^ flip
    )


def decay_weights(causal, g_col, g_row):
    return jnp.exp(jnp.where(causal, g_col - g_row, -1e30))


def flip_of(own, share):
    return share * (own[1] & (BLOCK // share - 1))


def exact(a, b, dims):
    return lax.dot_general(a, b, (dims, ((), ())), precision=lax.Precision.HIGHEST, preferred_element_type=f32)


KEEP, ENTER, ENDS, FIRST, SECOND = range(5)


def layout_kernel(narrow, share, own, lengths, pads, log_decay, gcol, rise, tail, grow, live, coefs, total):
    heads, local = log_decay.shape
    hn = heads // narrow
    per, blocks = BLOCK // share, local // BLOCK
    base = own[0] * local
    place = lax.broadcasted_iota(jnp.int32, (local, 1), 0)
    spot = base + ((place // share) ^ own[1]) * share + place % share
    alive = jnp.zeros((local, 1), f32)
    keeps = [jnp.float32(1.0)] * blocks
    end = jnp.int32(0)
    for s in range(lengths.shape[0]):
        start, end = end, end + lengths[s]
        alive = jnp.where((spot >= start) & (spot < end - pads[s]), 1.0, alive)
        keeps = [jnp.where(start == base + b * BLOCK, 0.0, keep) for b, keep in enumerate(keeps)]
    live[...] = alive

    size = (BLOCK, BLOCK)
    upper = (lax.broadcasted_iota(jnp.int32, size, 0) <= lax.broadcasted_iota(jnp.int32, size, 1)).astype(f32)
    eye = (lax.broadcasted_iota(jnp.int32, (heads, heads), 0)
           == lax.broadcasted_iota(jnp.int32, (heads, heads), 1)).astype(f32)
    turned = own[1] // per > 0
    rows_of, ends_of, decay_of, keep_of = [], [], [], []
    for b in range(blocks):
        part = log_decay[:, b * BLOCK : (b + 1) * BLOCK]
        g = exact(part, upper, ((1,), (0,)))
        for bit in range((per - 1).bit_length()):
            step = share << bit
            flipped = [g[:, (i ^ 1) * step : ((i ^ 1) + 1) * step] for i in range(BLOCK // step)]
            g = jnp.where((own[1] >> bit) & 1 == 1, jnp.concatenate(flipped, axis=1), g)
        end_row = exact(jnp.ones_like(part), part, ((1,), (1,)))[0:1]
        rows_of.append(g)
        ends_of.append(end_row)
        decay_of.append(jnp.exp(end_row) * keeps[b])
        keep_of.append(jnp.full((1, heads), 1.0, f32) * keeps[b])
    total[...] = decay_of[0] * decay_of[1]
    one = jnp.ones((1, heads), f32)
    kinds = (keep_of, (one, decay_of[0]), (decay_of[1], one), (one, 0.0 * one), (0.0 * one, one))
    for s in range(blocks):
        def mine(pair):
            return jnp.where(turned, pair[1 - s], pair[s])

        for kind, pair in enumerate(kinds):
            coefs[kind, s : s + 1, :] = mine(pair)
        g = mine(rows_of)
        column = exact(g, eye, ((0,), (0,)))
        up, down = jnp.exp(column), jnp.exp(mine(ends_of) - column)
        at = slice(s * BLOCK, (s + 1) * BLOCK)
        for n in range(narrow):
            group = slice(n * hn, (n + 1) * hn)
            gcol[n, at, :] = column[:, group]
            rise[n, at, :] = up[:, group]
            tail[n, at, :] = down[:, group]
            grow[s * narrow + n] = g[group, :]


def forward_kernel(hn, hd, share, own, tok_a, tok_b, wq, wk, wv, wg, live, gcol, grow, tail, *refs):
    n1, tok, ql, kl, q, k, v, act, intra, contrib = refs[-10:]
    i = pl.program_id(0)

    @pl.when(i == 0)
    def _():
        for part, source in enumerate((tok_a, tok_b)):
            at = slice(part * share, (part + 1) * share)
            tok[at, :] = source[...]
            values = source[...].astype(f32)
            n1[at, :] = (values * inv_rms(values)).astype(bf16)

    normed = n1[...]
    q_lin = mm(normed, wq[...])
    k_lin = mm(normed, wk[...])

    ql[...] = q_lin
    kl[...] = k_lin
    q[...] = (q_lin * sigmoid(q_lin)).astype(bf16)
    k[...] = (k_lin * sigmoid(k_lin) * live[...]).astype(bf16)
    v[...] = mm(normed, wv[...]).astype(bf16)
    act[...] = sigmoid(mm(normed, wg[...]))
    causal = causal_of(BLOCK, flip_of(own, share))
    for h in range(hn):
        at = slice(h * hd, (h + 1) * hd)
        qh, kh, vh = q[:, at], k[:, at], v[:, at]
        weights = decay_weights(causal, gcol[0, :, h : h + 1], grow[0, h : h + 1, :])
        scores = (mt(qh, kh) * weights).astype(bf16)
        intra[:, at] = mm(scores, vh)
        key_tail = (kh.astype(f32) * tail[0, :, h : h + 1]).astype(bf16)
        contrib[0, h] = tm(key_tail, vh)


def out_kernel(heads, hn, hd, share, own, coefs, *refs):
    narrow = heads // hn
    states = refs[:narrow]
    contrib, q, intra, act, tok, rise, wo, att, inverse, gated, hidden, n2, kent = refs[narrow:]
    b = pl.program_id(0)
    for h in range(heads):
        at = slice(h * hd, (h + 1) * hd)
        part = own[1] ^ (h // hn)
        base = states[0][h % hn].astype(f32)
        for j in range(1, narrow):
            base = jnp.where(part == j, states[j][h % hn].astype(f32), base)
        entering = coefs[ENTER, b, h] * base + coefs[SECOND, b, h] * contrib[1 - b, h]
        kept = (coefs[KEEP, b, h] * entering).astype(bf16)
        kent[0, h] = kept
        att[:, at] = (intra[:, at] + rise[h // hn, :, h % hn : h % hn + 1] * mm(q[:, at], kept)).astype(bf16)
    values = att[...].astype(f32)
    scale = inv_rms(values)
    inverse[...] = scale
    gated[...] = (values * scale * act[...]).astype(bf16)
    hid = tok[...].astype(f32) + mm(gated[...], wo[...])

    @pl.when(b == 0)
    def _():
        hidden[...] = hid[:share]

    n2[...] = (hid * inv_rms(hid)).astype(bf16)


def ffn_kernel(share, n2, cot, w1, w2, w3, product, gf, gs, *pieces):
    normed = n2[...]
    first = mt(normed, w1[...])
    second = mt(normed, w2[...])
    product[...] = (first * second).astype(bf16)
    grad = mt(cot[...], w3[...])
    gf[...] = (grad * second).astype(bf16)
    gs[...] = (grad * first).astype(bf16)
    back = (mm(gf[...], w1[...]) + mm(gs[...], w2[...])).astype(bf16)
    for i, piece in enumerate(pieces):
        piece[...] = back[i * share : (i + 1) * share]


def reversed_bits(value, count):
    out = 0
    for i in range(count):
        out = out | (((value >> i) & 1) << (count - 1 - i))
    return out


def position(offset, parity, wide):
    bits = (wide - 1).bit_length() - 1
    high = offset >> 1
    return jnp.where(parity == 0, reversed_bits(high, bits), high)


def scatter(wide, own, kept, sent, item, piece_of):
    for t in range(wide):
        offset = own[0] ^ t
        parity = own[0] & 1

        @pl.when(offset & 1 == 0)
        def _():
            kept[position(offset, parity, wide), item] = piece_of(t).astype(bf16)

        @pl.when(offset & 1 == 1)
        def _():
            sent[position(offset, 1 - parity, wide), item] = piece_of(t).astype(bf16)


def ffn_cut(wide, ff, width):
    across = min(wide, width // 128)
    return ff // (wide // across), width // across, across


def ffn_grad_kernel(wide, share, own, n2, cot, product, gf, gs, w3, kept, sent, *refs):
    pieces, acc = refs[:-1], refs[-1]
    item = pl.program_id(0)
    for i, (left, right) in enumerate(((gf, n2), (gs, n2), (product, cot))):
        @pl.when(item == i)
        def _():
            acc[...] = tm(left[...], right[...])

    tall, cols, across = ffn_cut(wide, *acc.shape)

    def piece_of(t):
        row, col = t // across * tall, t % across * cols
        return acc[row : row + tall, col : col + cols]

    scatter(wide, own, kept, sent, 0, piece_of)

    @pl.when(item == 2)
    def _():
        for i, piece in enumerate(pieces):
            piece[...] = mm(product[i * share : (i + 1) * share, :], w3[...]).astype(bf16)


def residual_kernel(narrow, own, *refs):
    parts = refs[:narrow]
    hidden, cot, wo, att, inverse, act, grad_hidden, ggl = refs[narrow : narrow + 8]
    trios = refs[narrow + 8 :]
    gn2 = parts[0][...].astype(f32)
    for part in parts[1:]:
        gn2 = gn2 + part[...].astype(f32)
    hid = hidden[...]
    gh = cot[...].astype(f32) + rms_back(hid, inv_rms(hid), gn2)
    grad_hidden[...] = gh
    low = gh.astype(bf16)
    gg = mt(low, wo[...])
    values = att[...].astype(f32)
    gate = act[...]
    ggl[...] = (gg * (values * inverse[...]) * gate * (1.0 - gate)).astype(bf16)
    back = rms_back(values, inverse[...], gg * gate).astype(bf16)
    size = back.shape[1] // narrow
    for i in range(narrow):
        for k in range(narrow):
            @pl.when(own[1] ^ i == k)
            def _():
                at = slice(i * size, (i + 1) * size)
                trios[k][:, :size] = back[:, at]
                trios[k][:, size : 2 * size] = ggl[:, at]
                trios[k][:, 2 * size :] = low[:, at]


def query_kernel(hn, hd, share, own, coefs, *refs):
    per = BLOCK // share
    ga = refs[:-15]
    q, k, v, ql, kent, gcol, grow, rise, dq, gk, gv, direct, message, grad, first = refs[-15:]
    b = pl.program_id(0)
    for i, piece in enumerate(ga):
        @pl.when(b == i // per)
        def _():
            grad[(i % per) * share : (i % per + 1) * share, :] = piece[:, : grad.shape[1]]

    causal = causal_of(BLOCK, flip_of(own, share))
    for h in range(hn):
        at = slice(h * hd, (h + 1) * hd)
        g, qh, kh, vh = grad[:, at], q[:, at], k[:, at], v[:, at]
        weights = decay_weights(causal, gcol[:, h : h + 1], grow[0, h : h + 1, :])
        scores = (mt(qh, kh) * weights).astype(bf16)
        raw = (mt(g, vh) * weights).astype(bf16)
        up = rise[:, h : h + 1]
        gq = mm(raw, kh) + up * mt(g, kent[0, h])
        dq[:, at] = (gq * slope(ql[:, at])).astype(bf16)
        gk[:, at] = tm(raw, qh)
        gv[:, at] = tm(scores, g)
        head = own[1] * hn + h
        now = coefs[KEEP, b, head] * tm((qh.astype(f32) * up).astype(bf16), g)
        direct[0, h] = now

        first[h] = jnp.where(b == 0, 0.0, first[h]) + coefs[ENTER, b, head] * now
        message[h] = first[h].astype(bf16)


def key_kernel(hn, hd, wide, share, own, coefs, arrived, direct, n1, dq, k, v, kl, gk, gv,
               tail, live, _kept, _sent, kept, sent, *refs):
    pieces = refs[:-5]
    dk, dv, aq, ak, av = refs[-5:]
    per = BLOCK // share
    b = pl.program_id(0)
    last = pl.num_programs(0) - 1
    for h in range(hn):
        at = slice(h * hd, (h + 1) * hd)
        head = own[1] * hn + h
        low = (coefs[ENDS, b, head] * arrived[h] + coefs[FIRST, b, head] * direct[1 - b, h]).astype(bf16)
        down = tail[:, h : h + 1]
        grad_key = gk[:, at] + down * mt(v[:, at], low)
        dk[:, at] = (grad_key * live[...] * slope(kl[:, at])).astype(bf16)
        dv[:, at] = (gv[:, at] + down * mm(k[:, at], low)).astype(bf16)
    normed = n1[...]
    tall = normed.shape[1] // wide
    for acc, part in ((aq, dq), (ak, dk), (av, dv)):
        acc[...] = jnp.where(b == 0, 0.0, acc[...]) + tm(normed, part[...])

    for item, acc in enumerate((aq, ak, av)):
        @pl.when(b == last)
        def _():
            scatter(wide, own, kept, sent, item, lambda t: acc[t * tall : (t + 1) * tall, :])

    cols = dq.shape[1]
    for i, piece in enumerate(pieces):
        @pl.when(b == i // per)
        def _():
            for item, part in enumerate((dq, dk, dv)):
                piece[:, item * cols : (item + 1) * cols] = part[(i % per) * share : (i % per + 1) * share, :]


def gate_kernel(wide, share, own, *refs):
    trios = refs[:-6]
    n1, gated, kept, sent, grads, acc = refs[-6:]
    item = pl.program_id(0)
    cols = acc.shape[1]
    tall = acc.shape[0] // wide
    for step, left in enumerate((n1, gated)):
        @pl.when(item == step)
        def _():
            at = slice((step + 1) * cols, (step + 2) * cols)
            for i, piece in enumerate(trios):
                grads[i * share : (i + 1) * share, :] = piece[:, at]
            acc[...] = tm(left[...], grads[...])

    scatter(wide, own, kept, sent, 0, lambda t: acc[t * tall : (t + 1) * tall, :])


def tokens_kernel(narrow, own, *refs):
    parts = refs[:narrow]
    ggl, wq, wk, wv, wg, tok, gh, out, *grads, total = refs[narrow:]
    step = pl.program_id(0)
    cols = parts[0].shape[1] // 3

    @pl.when(step == 0)
    def _():
        for i in range(narrow):
            for k in range(narrow):
                @pl.when(own[1] ^ i == k)
                def _():
                    for item, full in enumerate(grads):
                        full[:, i * cols : (i + 1) * cols] = parts[k][:, item * cols : (item + 1) * cols]

    grad = mt(ggl[...], wg[...])
    for full, weight in zip(grads, (wq, wk, wv)):
        grad = grad + mt(full[...], weight[...])
    total[step] = grad

    @pl.when(step == narrow - 1)
    def _():
        grad = jnp.concatenate([total[i] for i in range(narrow)], axis=1)
        values = tok[...].astype(f32)
        out[...] = gh[...] + rms_back(values, inv_rms(values), grad)


def output_kernel(narrow, *refs):
    hidden, out = refs[narrow:]
    total = hidden[...]
    for part in refs[:narrow]:
        total = total + part[...].astype(f32)
    out[...] = total.astype(bf16)


def swap_narrow(values, k):
    size = lax.axis_size("narrow")
    return lax.ppermute(values, "narrow", [(i, i ^ k) for i in range(size)])


def gather_narrow(values):
    return [values] + [swap_narrow(values, k) for k in range(1, lax.axis_size("narrow"))]


def trade_narrow(pieces):
    return [pieces[0]] + [swap_narrow(pieces[k], k) for k in range(1, len(pieces))]


def swap_core(values):
    size = lax.axis_size("wide")
    return lax.ppermute(values, "wide", [(i, i ^ 1) for i in range(size)])


def swap_step(values, step):
    size = lax.axis_size("wide")
    bits = (size - 1).bit_length()
    flip = lambda i: i ^ (1 << (1 + step if i % 2 == 0 else bits - 1 - step))
    return lax.ppermute(values, "wide", [(i, flip(i)) for i in range(size)])


def fence(*values):
    return lax.optimization_barrier(values)


def halved(low, high):
    half = low.shape[0] // 2
    return low[:half] + high[:half], low[half:] + high[half:]


def swap_all(parts, step):
    return [swap_step(part, step) for part in parts]


def swap_cores(parts):
    return [swap_core(part) for part in parts]


def target(own, place, other, wide):
    bits = (wide - 1).bit_length() - 1
    parity = (own[0] & 1) ^ other
    high = jnp.where(parity == 0, reversed_bits(place, bits), place)
    return own[0] ^ other ^ (2 * high)


def widen_square_kernel(count, narrow, places, own, *refs):
    pieces, outs = refs[:places], refs[-count:]
    for j, piece in enumerate(pieces):
        @pl.when(pl.program_id(0) == j)
        def _():
            cols = piece.shape[-1]
            for item in range(count):
                for n in range(narrow):
                    outs[item][:, n * cols : (n + 1) * cols] = piece[own[1] ^ n, item].astype(f32)


def widen_ffn_kernel(places, own, *refs):
    pieces, outs = refs[:places], refs[-3:]
    for j, piece in enumerate(pieces):
        @pl.when(pl.program_id(0) == j)
        def _():
            for item in range(3):
                outs[item][...] = piece[item].astype(f32)


def widen(kernel, own, other, first, total, pieces, block, cut, shape, outs, count, name):
    places = len(pieces)
    spec = pl.BlockSpec(block, lambda i, own: cut(target(own, first + i, other, 2 * total)))
    return pl.pallas_call(
        functools.partial(kernel, places),
        grid_spec=pltpu.PrefetchScalarGridSpec(
            num_scalar_prefetch=1,
            grid=(places,),
            in_specs=[whole(p.shape) for p in pieces] + [ANY] * len(outs),
            out_specs=[spec] * count,
        ),
        out_shape=[sds(shape, f32)] * count,
        input_output_aliases={1 + places + i: i for i in range(len(outs))},
        compiler_params=budget(16),
        cost_estimate=cost(4),
        name=f"{name}_{other}",
    )(own, *pieces, *outs)


def xor_order(values, own, axis):
    count = values.shape[axis]
    for bit in range((count - 1).bit_length()):
        step = 1 << bit
        shape = values.shape
        split = values.reshape(shape[:axis] + (count // (2 * step), 2, step) + shape[axis + 1 :])
        flipped = jnp.flip(split, axis + 1)
        values = jnp.where((own >> bit) & 1 == 1, flipped, split).reshape(shape)
    return values


def gather_factors(values):
    size, own = lax.axis_size("wide"), lax.axis_index("wide")
    full = values[None]
    for bit in range((size - 1).bit_length()):
        got = lax.ppermute(full, "wide", [(i, i ^ (1 << bit)) for i in range(size)])
        full = jnp.concatenate([full, got], axis=0)
    return xor_order(full, own, 0)


def between(factors, own, before):
    count = factors.shape[0]
    j = jnp.arange(count)[:, None]
    i = jnp.arange(count)[None, :]
    if before:
        inner, wanted = (i > j) & (i < own), j[:, 0] < own
    else:
        inner, wanted = (i < j) & (i > own), j[:, 0] > own
    terms = jnp.where(inner[:, :, None], factors[None], 1.0)
    return jnp.where(wanted[:, None], jnp.prod(terms, axis=1), 0.0)


def pass_states(message, coef):
    gathered = lax.all_gather(message, "wide", axis=0)
    return jnp.sum(coef[:, :, None, None] * gathered.astype(f32), axis=0)


def body(tokens, log_decay, lengths, pad_counts, w_query, w_key, w_value, w_gate, w_out,
         w_first, w_second, w_third, cotangent):
    wide, narrow = lax.axis_size("wide"), lax.axis_size("narrow")
    own_wide, own_narrow = lax.axis_index("wide"), lax.axis_index("narrow")
    heads, local = log_decay.shape
    share, width = tokens.shape
    hn, cols, hd = heads // narrow, width // narrow, width // heads
    blocks, per = local // BLOCK, BLOCK // share
    own = jnp.stack([own_wide, own_narrow]).astype(jnp.int32)

    tok = gather_narrow(tokens)

    columns = sds((narrow, local, hn), f32)
    gcol, rise, tail, grow, live, coefs, total = pl.pallas_call(
        functools.partial(layout_kernel, narrow, share),
        in_specs=[SMEM, SMEM, SMEM, pl.BlockSpec(memory_space=pltpu.VMEM)],
        out_shape=[columns, columns, columns, sds((blocks * narrow, hn, BLOCK), f32), sds((local, 1), f32),
                   sds((5, blocks, heads), f32), sds((1, heads), f32)],
        compiler_params=budget(16),
        cost_estimate=cost(3),
        name="layout",
    )(own, lengths, pad_counts, log_decay)

    def own_heads(values):
        return lax.dynamic_slice_in_dim(values, own_narrow * hn, hn, 1)

    shapes = [sds((local, width), bf16), sds((local, width), bf16), *[sds((local, width), f32)] * 2,
              *[sds((local, width), bf16)] * 3, *[sds((local, width), f32)] * 2,
              sds((blocks, heads, hd, hd), f32)]
    made = []
    for s in range(blocks):
        if s == 1:
            made, later, cotangent_now, product_now = fence(made, tok[per:], cotangent, total)
            tok = tok[:per] + list(later)
        weight = pl.BlockSpec((width, cols), lambda i, own: (0, i))
        column = pl.BlockSpec((1, BLOCK, hn), lambda i, own, s=s: (i, s, 0))
        full = pl.BlockSpec((BLOCK, width), lambda i, own, s=s: (s, 0))
        part = pl.BlockSpec((BLOCK, cols), lambda i, own, s=s: (s, i))
        made = pl.pallas_call(
            functools.partial(forward_kernel, hn, hd, share),
            grid_spec=pltpu.PrefetchScalarGridSpec(
                num_scalar_prefetch=1,
                grid=(narrow,),
                in_specs=[*[whole((share, width))] * 2, *[weight] * 4,
                          pl.BlockSpec((BLOCK, 1), lambda i, own, s=s: (s, 0)), column,
                          pl.BlockSpec((1, hn, BLOCK), lambda i, own, s=s: (s * narrow + i, 0, 0)),
                          column, *[ANY] * len(made)],
                out_specs=[full, full, *[part] * 7,
                           pl.BlockSpec((1, hn, hd, hd), lambda i, own, s=s: (s, i, 0, 0))],
            ),
            out_shape=shapes,
            input_output_aliases={11 + i: i for i in range(len(made))},
            compiler_params=budget(56),
            cost_estimate=cost(10),
            name=f"mixer_forward_{s}",
        )(own, tok[per * s], tok[per * s + 1], w_query, w_key, w_value, w_gate, live, gcol, grow, tail, *made)
    n1, tok_all, ql, kl, q, k, v, act, intra, contrib = made

    cot = gather_narrow(cotangent_now)
    factors = gather_factors(product_now[0])
    factors = lax.dynamic_slice_in_dim(factors, own_narrow * hn, hn, 1)
    coef_in, coef_out = between(factors, own_wide, True), between(factors, own_wide, False)
    message = own_heads(contrib)
    message = jnp.sum(own_heads(coefs[ENDS])[:, :, None, None] * message, axis=0).astype(bf16)
    entering, cot = fence(pass_states(message, coef_in).astype(bf16), cot)
    cot_all = jnp.concatenate(cot, axis=0)
    states = gather_narrow(entering)

    up = lambda b: b
    all_blk, part_blk = rows((BLOCK, width), up), rows((BLOCK, cols), up)
    own_blk = pl.BlockSpec((BLOCK, cols), lambda b, own: (b, own[1]))
    own_kent = pl.BlockSpec((1, hn, hd, hd), lambda b, own: (b, own[1], 0, 0))
    own_direct = rows((1, hn, hd, hd), up)
    att, inverse, gated, hidden, n2, kent = pl.pallas_call(
        functools.partial(out_kernel, heads, hn, hd, share),
        grid_spec=pltpu.PrefetchScalarGridSpec(
            num_scalar_prefetch=1,
            grid=(blocks,),
            in_specs=[SMEM, *[whole((hn, hd, hd))] * narrow, whole((blocks, heads, hd, hd)),
                      *[all_blk] * 4, pl.BlockSpec((narrow, BLOCK, hn), lambda b, own: (0, b, 0)),
                      whole((width, width))],
            out_specs=[all_blk, rows((BLOCK, 1), up), all_blk, whole((share, width)), all_blk, rows((1, heads, hd, hd), up)],
        ),
        out_shape=[sds((local, width), bf16), sds((local, 1), f32), sds((local, width), bf16), sds((share, width), f32),
                   sds((local, width), bf16), sds((blocks, heads, hd, hd), bf16)],
        compiler_params=budget(56),
        cost_estimate=cost(9.5),
        name="mixer_out",
    )(own, coefs, *states, contrib, q, intra, act, tok_all, rise, w_out)

    ff = w_first.shape[1]
    first_t, second_t = w_first.T, w_second.T
    ff_blk = rows((BLOCK, ff), up)
    piece_spec, piece_shape = whole((share, width)), sds((share, width), bf16)
    product, gf, gs, *gn2 = pl.pallas_call(
        functools.partial(ffn_kernel, share),
        out_shape=[*[sds((local, ff), bf16)] * 3, *[piece_shape] * narrow],
        compiler_params=budget(16),
        cost_estimate=cost(10),
        name="ffn",
    )(n2, cot_all, first_t, second_t, w_third)

    gn2 = trade_narrow(gn2)
    product_now, _ = fence(product, gn2[1])
    tall, across = ffn_cut(wide, ff, width)[:2]
    slot = (wide // 2, 3, tall, across)
    slot_spec = pl.BlockSpec((wide // 2, 1, tall, across), lambda i, own: (0, i, 0, 0))
    kept, sent, *ffn_part = pl.pallas_call(
        functools.partial(ffn_grad_kernel, wide, share),
        grid_spec=pltpu.PrefetchScalarGridSpec(
            num_scalar_prefetch=1,
            grid=(3,),
            in_specs=[*[whole((local, width))] * 2, *[whole((local, ff))] * 3, whole((ff, width))],
            out_specs=[slot_spec, slot_spec, *[piece_spec] * narrow],
            scratch_shapes=[pltpu.VMEM((ff, width), f32)],
        ),
        out_shape=[sds(slot, bf16), sds(slot, bf16), *[piece_shape] * narrow],
        compiler_params=budget(16),
        cost_estimate=cost(10),
        name="ffn_grads",
    )(own, n2, cot_all, product_now, gf, gs, w_third)
    gn2, kept, sent = fence(gn2, kept, sent)
    steps = (wide - 1).bit_length() - 1

    def single(shape, index=None):
        where = index or (lambda own: (0,) * len(shape))
        return pl.BlockSpec(shape, lambda b, own: where(own))

    row_spec = single((share, width))
    grad_hidden, ggl, *trios = pl.pallas_call(
        functools.partial(residual_kernel, narrow),
        grid_spec=pltpu.PrefetchScalarGridSpec(
            num_scalar_prefetch=1,
            grid=(1,),
            in_specs=[*[row_spec] * (narrow + 2), single((width, width)), row_spec, single((share, 1)), row_spec],
            out_specs=[row_spec] * 2 + [single((share, 3 * cols))] * narrow,
        ),
        out_shape=[sds((share, width), f32), sds((share, width), bf16),
                   *[sds((share, 3 * cols), bf16)] * narrow],
        compiler_params=budget(16),
        cost_estimate=cost(5),
        name="residual_back",
    )(own, *gn2, hidden, cotangent, w_out, att, inverse, act)
    trios, kept, sent = fence(trios, kept, sent)
    trios, kept, got, ffn_part = fence(trade_narrow(trios), kept, swap_core(sent), ffn_part)
    low, away = halved(kept, got)
    got = swap_step(away, 0)

    own_col = pl.BlockSpec((None, BLOCK, hn), lambda b, own: (own[1], b, 0))
    own_row = pl.BlockSpec((1, hn, BLOCK), lambda b, own: (b * narrow + own[1], 0, 0))
    dq, gk, gv, direct, message = pl.pallas_call(
        functools.partial(query_kernel, hn, hd, share),
        grid_spec=pltpu.PrefetchScalarGridSpec(
            num_scalar_prefetch=1,
            grid=(blocks,),
            in_specs=[SMEM, *[whole((share, 3 * cols))] * narrow, *[own_blk] * 4, own_kent,
                      own_col, own_row, own_col],
            out_specs=[*[part_blk] * 3, own_direct, whole((hn, hd, hd))],
            scratch_shapes=[pltpu.VMEM((BLOCK, cols), bf16), pltpu.VMEM((hn, hd, hd), f32)],
        ),
        out_shape=[sds((local, cols), bf16), *[sds((local, cols), f32)] * 2,
                   sds((blocks, hn, hd, hd), f32), sds((hn, hd, hd), bf16)],
        compiler_params=budget(56),
        cost_estimate=cost(5.4),
        name="mixer_query_back",
    )(own, coefs, *trios, q, k, v, ql, kent, gcol, grow, rise)

    part_two = swap_narrow(ffn_part[2], 2)
    arrived, low, got, part_two = fence(pass_states(message, coef_out), low, got, part_two)
    low_ff, away_ff = halved(low, got)

    five = (wide // 2, 5, width // wide, cols)
    one = pl.BlockSpec((wide // 2, 1, width // wide, cols), lambda i, own: (0, 3 + i, 0, 0))
    kept, sent = pl.pallas_call(
        functools.partial(gate_kernel, wide, share),
        grid_spec=pltpu.PrefetchScalarGridSpec(
            num_scalar_prefetch=1,
            grid=(2,),
            in_specs=[*[single((share, 3 * cols))] * narrow, *[single((local, width))] * 2],
            out_specs=[one] * 2,
            scratch_shapes=[pltpu.VMEM((local, cols), bf16), pltpu.VMEM((width, cols), f32)],
        ),
        out_shape=[sds(five, bf16)] * 2,
        compiler_params=budget(16),
        cost_estimate=cost(5),
        name="gate_back",
    )(own, *trios, n1, gated)
    three = whole((wide // 2, 3, width // wide, cols))
    trio_spec, trio_shape = whole((share, 3 * cols)), sds((share, 3 * cols), bf16)
    kept, sent, *dqkv = pl.pallas_call(
        functools.partial(key_kernel, hn, hd, wide, share),
        grid_spec=pltpu.PrefetchScalarGridSpec(
            num_scalar_prefetch=1,
            grid=(blocks,),
            in_specs=[SMEM, whole((hn, hd, hd)), whole((blocks, hn, hd, hd)), all_blk, part_blk,
                      *[own_blk] * 3, *[part_blk] * 2, own_col, rows((BLOCK, 1), up), ANY, ANY],
            out_specs=[three, three, *[trio_spec] * narrow],
            scratch_shapes=[*[pltpu.VMEM((BLOCK, cols), bf16)] * 2, *[pltpu.VMEM((width, cols), f32)] * 3],
        ),
        out_shape=[*[sds(five, bf16)] * 2, *[trio_shape] * narrow],
        input_output_aliases={13: 0, 14: 1},
        compiler_params=budget(16),
        cost_estimate=cost(9),
        name="mixer_key_back",
    )(own, coefs, arrived, direct, n1, dq, k, v, kl, gk, gv, tail, live, kept, sent)

    low, away = halved(kept, swap_core(sent))
    low, away, dqkv, away_ff = fence(low, away, dqkv, away_ff)
    low, high, dqkv, high_ff = fence(low, swap_step(away, 0), trade_narrow(dqkv), swap_step(away_ff, 1))
    for step in range(1, steps):
        low, away = halved(low, high)
        high = swap_step(away, step)
    for step in range(2, steps):
        low_ff, away_ff = halved(low_ff, high_ff)
        high_ff = swap_step(away_ff, step)
    piece = (low + high)[0]
    ff_piece = [(low_ff + high_ff)[0]]

    for step in reversed(range(1, steps)):
        ff_first = len(ff_piece)
        ff_piece = ff_piece + swap_all(ff_piece, step)
    ff_more = swap_all(ff_piece[:ff_first], 0)
    gate_piece, piece, ff_piece, ff_more = fence(
        jnp.stack(gather_narrow(piece[3:])), piece[:3], ff_piece, ff_more
    )
    chunks = width // across
    ffn_form = (tall, across), lambda t: (t // chunks, t % chunks), (ff, width)
    square_form = (width // wide, width), lambda t: (t, 0), (width, width)
    gate_kernels = functools.partial(widen_square_kernel, 2, narrow)
    square_kernels = functools.partial(widen_square_kernel, 3, narrow)

    zs = gather_narrow(piece)
    ff_piece = ff_piece + ff_more + swap_all(ff_piece[ff_first:], 0)
    gate_piece = [gate_piece]
    for step in reversed(range(1, steps)):
        gate_piece = gate_piece + swap_all(gate_piece, step)
    half = len(gate_piece) // 2
    gate_more = swap_all(gate_piece, 0)
    dqkv, _ = fence(dqkv, zs[1])
    grad_tokens = pl.pallas_call(
        functools.partial(tokens_kernel, narrow),
        grid_spec=pltpu.PrefetchScalarGridSpec(
            num_scalar_prefetch=1,
            grid=(narrow,),
            in_specs=[*[single((share, 3 * cols))] * narrow, row_spec, *[pl.BlockSpec((cols, width), lambda i, own: (i, 0))] * 4,
                      row_spec, row_spec],
            out_specs=row_spec,
            scratch_shapes=[*[pltpu.VMEM((share, width), bf16)] * 3, pltpu.VMEM((narrow, share, cols), f32)],
        ),
        out_shape=sds((share, width), f32),
        compiler_params=budget(16),
        cost_estimate=cost(8),
        name="tokens_back",
    )(own, *dqkv, ggl, w_query, w_key, w_value, w_gate, tokens, grad_hidden)
    square_piece, gate_piece, ff_piece, ffn_part, grad_tokens = fence(
        jnp.stack(zs), gate_piece + gate_more, ff_piece, ffn_part, grad_tokens
    )

    square_piece = [square_piece]
    for step in reversed(range(1, steps)):
        square_piece = square_piece + swap_all(square_piece, step)
    square_piece = square_piece + swap_all(square_piece[:half], 0)
    places = wide // 2
    ffn_out = widen(widen_ffn_kernel, own, 0, 0, places, ff_piece, *ffn_form, [], 3, "widen_ffn")
    gate_out = widen(gate_kernels, own, 0, 0, places, gate_piece, *square_form, [], 2, "widen_gate")
    ff_other = swap_cores(ff_piece)
    ffn_out = widen(widen_ffn_kernel, own, 1, 0, places, ff_other, *ffn_form, ffn_out, 3, "widen_ffn")
    square_piece, ffn_out, gate_out, gate_other, ffn_part = fence(
        square_piece, ffn_out, gate_out, swap_cores(gate_piece), ffn_part
    )

    part_three, part_one = swap_narrow(ffn_part[3], 3), swap_narrow(ffn_part[1], 1)
    square_last = swap_all(square_piece[half : places // 2], 0)
    done = len(square_piece)
    gate_out = widen(gate_kernels, own, 1, 0, places, gate_other, *square_form, gate_out, 2, "widen_gate")
    mixer = widen(square_kernels, own, 0, 0, places, square_piece, *square_form, [], 3, "widen_square")
    square_last, gate_out, mixer, square_piece, part_three, part_one = fence(
        square_last, gate_out, mixer, square_piece, part_three, part_one
    )

    output = pl.pallas_call(
        functools.partial(output_kernel, narrow),
        out_shape=sds((share, width), bf16),
        compiler_params=budget(16),
        cost_estimate=cost(2),
        name="output",
    )(ffn_part[0], part_one, part_two, part_three, hidden)
    mixer = widen(square_kernels, own, 0, done, places, square_last, *square_form, mixer, 3, "widen_last")
    square_other = swap_cores(square_piece + square_last)
    mixer = widen(square_kernels, own, 1, 0, places, square_other, *square_form, mixer, 3, "widen_square")
    grad_first, grad_second, grad_third = ffn_out
    grad_gate, grad_out = gate_out
    return (output, grad_tokens, *mixer, grad_gate, grad_out, grad_first.T, grad_second.T, grad_third)


def solution(mesh):
    both = P(("wide", "narrow"), None)
    in_specs = (both, P(None, "wide"), P(), P(), P(), P(), P(), P(), P(),
                P(None, "narrow"), P(None, "narrow"), P("narrow", None), both)
    out_specs = (both, both, P(), P(), P(), P(), P(),
                 P(None, "narrow"), P(None, "narrow"), P("narrow", None))
    return jax.shard_map(body, mesh=mesh, in_specs=in_specs, out_specs=out_specs, check_vma=False)
```
